256 devices in a mesh: gx: 8 (over x, core), gy: 8 (over z), gz: 4 (over y).
Axes of the slice: x: 4, y: 4, z: 8, core: 2. Of those that a mesh axis runs over, the one named last changes fastest.
Arguments:
- load_field: float32 [3, 128, 128, 512], P(None, 'gx', 'gy', 'gz'), may hold values from -6 to 6
- design: float32 [128, 128, 512], P('gx', 'gy', 'gz'), may hold values from 0 to 1
- solid_map: int32 [8, 8, 32], replicated, may hold values from 0 to 1, as said below
Outputs:
- displacement: float32 [3, 128, 128, 512], P(None, 'gx', 'gy', 'gz')
- sensitivity: float32 [128, 128, 512], P('gx', 'gy', 'gz')
- density: float32 [128, 128, 512], P('gx', 'gy', 'gz')
The draws below stay inside these ranges and needn't reach their ends.
Inputs may be any that keep to these rules, and one draw needn't show every extreme that they name: Brick [i, j, k] holds the elements of rows i * 16 to (i + 1) * 16 - 1 of each dimension in turn. For i < 4, every j and every aligned run of 8 bricks along the third dimension, the run at first index i and the same run at i + 4 hold exactly 8 solid bricks together. The run solid_map[0, 0, 0:8] is all solid.
All inputs are finite; a program needn't handle non-finite values.
Results may differ from the reference program's by a relative error of at most 0.0001.
Values sent between devices are 32-bit elements; how exact they have to be, the bound alone decides.
No kernel may reach another device: no remote copies, remote signals or barrier semaphores. Data moves between devices by JAX's collectives and lax.ppermute only.
A program may use at most 64 MiB of HBM per device.

```python
import math
import jax
import jax.numpy as jnp
import numpy as np
from jax import lax

BRICK = 16
BRZ = 8
ITERS = 2
NX = 128
NY = 128
NZ = 512
GBX = 8
GBY = 8
GBZ = 32


def draw_solid_map(key, part):
    key_count, key_order = jax.random.split(key)
    pair_count = GBX // 2
    columns = GBZ // BRZ
    counts = jax.random.randint(key_count, (pair_count, GBY, columns), 0, BRZ + 1)
    counts = counts.at[0, 0, 0].set(BRZ)
    scores = jax.random.randint(key_order, (2, pair_count, GBY, columns, BRZ), 0, 1 << 20) * BRZ + jnp.arange(BRZ, dtype=jnp.int32)
    rank_order = jnp.argsort(jnp.argsort(scores, axis=-1), axis=-1)
    needed = jnp.stack([counts, BRZ - counts])[..., None]
    solid_flags = (rank_order < needed).astype(jnp.int32)
    return solid_flags.reshape(GBX, GBY, GBZ)


def block_scale(key, shape, cuts, least, largest):
    factor_of, own = 1.0, jax.random.fold_in(key, 6)
    for position, parts in cuts:
        steps = jnp.exp(jax.random.uniform(jax.random.fold_in(own, position), (parts,), jnp.float32, least / len(cuts), largest / len(cuts)))
        factor_of = factor_of * jnp.repeat(steps, shape[position] // parts).reshape([-1 if axis == position else 1 for axis in range(len(shape))])
    return factor_of


def bell_draw(own_key, dims, scale, reach, cuts=(), kind=jnp.bfloat16):
    values = jax.random.normal(own_key, dims, jnp.float32) * scale
    if len(cuts) > 0:
        values = block_scale(own_key, dims, cuts, -0.22, 0.18) * values
    return jnp.clip(values, min=-reach, max=reach).astype(kind)


def setup_inputs(seed: int = 0) -> dict:
    splits = jax.random.split(jax.random.key(seed), 4)
    return {
        "load_field": bell_draw(splits[0], (3, NX, NY, NZ), 1.0, 6.0, ((1, 8), (2, 8), (3, 4)), jnp.float32),
        "design": jnp.clip(1.0 * jax.random.uniform(splits[1], (NX, NY, NZ), jnp.float32) ** block_scale(splits[1], (NX, NY, NZ), ((0, 8), (1, 8), (2, 4)), -0.2, 0.2), 0.0, 1.0),
        "solid_map": draw_solid_map(jax.random.fold_in(splits[3], 71), 0),
    }


young_floor = 0.001
spring_rate = 0.05
sharpness = 8.0
threshold = 0.5
poisson = 0.3
precise = lax.Precision.HIGHEST

def element_matrix():
    lame_first = poisson / ((1.0 + poisson) * (1.0 - 2.0 * poisson))
    shear_mod = 1.0 / (2.0 * (1.0 + poisson))
    elastic = np.zeros((6, 6))
    elastic[:3, :3] = lame_first
    for axis_one in range(3):
        elastic[axis_one, axis_one] += 2.0 * shear_mod
        elastic[axis_one + 3, axis_one + 3] = shear_mod
    gauss_point = 1.0 / math.sqrt(3.0)
    stiffness = np.zeros((24, 24))
    for point_x in (-gauss_point, gauss_point):
        for point_y in (-gauss_point, gauss_point):
            for point_z in (-gauss_point, gauss_point):
                strain = np.zeros((6, 24))
                for corner in range(8):
                    sign_a = 2 * (corner // 4) - 1
                    sign_b = 2 * (corner // 2 % 2) - 1
                    sign_c = 2 * (corner % 2) - 1
                    along_x = 0.25 * sign_a * (1 + sign_b * point_y) * (1 + sign_c * point_z)
                    along_y = 0.25 * (1 + sign_a * point_x) * sign_b * (1 + sign_c * point_z)
                    along_z = 0.25 * (1 + sign_a * point_x) * (1 + sign_b * point_y) * sign_c
                    column = 3 * corner
                    strain[0, column] = along_x
                    strain[1, column + 1] = along_y
                    strain[2, column + 2] = along_z
                    strain[3, column + 1] = along_z
                    strain[3, column + 2] = along_y
                    strain[4, column] = along_z
                    strain[4, column + 2] = along_x
                    strain[5, column] = along_y
                    strain[5, column + 1] = along_x
                stiffness += strain.T @ elastic @ strain * 0.125
    return jnp.asarray(stiffness, dtype=jnp.float32)

def cone_offsets():
    listed = []
    for step_x in range(-2, 3):
        for step_y in range(-2, 3):
            for step_z in range(-2, 3):
                radius = step_x * step_x + step_y * step_y + step_z * step_z
                if radius < 9:
                    listed.append((step_x, step_y, step_z, 3.0 - math.sqrt(radius)))
    return listed

def corner_values(node_values, width_x, width_y, width_z):
    pieces = []
    for corner in range(8):
        shift_a, shift_b, shift_c = (corner // 4, corner // 2 % 2, corner % 2)
        pieces.append(node_values[:, shift_a:shift_a + width_x, shift_b:shift_b + width_y, shift_c:shift_c + width_z])
    return jnp.concatenate(pieces, 0).reshape(24, -1)

def spread_back(forces, width_x, width_y, width_z):
    forces = forces.reshape(24, width_x, width_y, width_z)
    summed = jnp.zeros((3, width_x + 1, width_y + 1, width_z + 1), jnp.float32)
    for corner in range(8):
        shift_a, shift_b, shift_c = (corner // 4, corner // 2 % 2, corner % 2)
        summed = summed + jnp.pad(forces[3 * corner:3 * corner + 3], ((0, 0), (shift_a, 1 - shift_a), (shift_b, 1 - shift_b), (shift_c, 1 - shift_c)))
    return summed

def corner_energy(stiffness, corner_vals):
    return lax.optimization_barrier(jnp.sum(corner_vals * jnp.dot(stiffness, corner_vals, precision=precise, preferred_element_type=jnp.float32), 0))

def reference(load_field, design, solid_map):
    stiffness = element_matrix()
    offsets = cone_offsets()

    def inside(length):
        coords = jnp.arange(length, dtype=jnp.int32)
        return {step_off: ((coords + step_off >= 0) & (coords + step_off < length)).astype(jnp.float32) for step_off in range(-2, 3)}
    inside_x, inside_y, inside_z = (inside(NX), inside(NY), inside(NZ))
    weight_sum = jnp.zeros((NX, NY, NZ), jnp.float32)
    for step_x, step_y, step_z, weight in offsets:
        weight_sum = weight_sum + weight * (inside_x[step_x][:, None, None] * inside_y[step_y][None, :, None] * inside_z[step_z][None, None, :])

    def cone_sum(values):
        extended = jnp.pad(values, 2)
        summed = jnp.zeros_like(values)
        for step_x, step_y, step_z, weight in offsets:
            summed = summed + weight * extended[2 + step_x:2 + step_x + NX, 2 + step_y:2 + step_y + NY, 2 + step_z:2 + step_z + NZ]
        return summed
    smoothed = cone_sum(design) / weight_sum
    lift_value = math.tanh(sharpness * threshold)
    scale_sum = lift_value + math.tanh(sharpness * (1.0 - threshold))
    tanh_shift = jnp.tanh(sharpness * (smoothed - threshold))
    density = (lift_value + tanh_shift) / scale_sum
    cell_flags = jnp.repeat(jnp.repeat(jnp.repeat(solid_map.astype(jnp.float32), BRICK, 0), BRICK, 1), BRICK, 2)
    moduli = (young_floor + density ** 3 * (1.0 - young_floor)) * cell_flags

    def operate(vector):
        padded = jnp.pad(vector, ((0, 0), (0, 1), (0, 1), (0, 1)))

        def slab_step(upper_prev, slab_index):
            node_values = lax.dynamic_slice_in_dim(padded, slab_index, 2, 1)
            slab_moduli = lax.dynamic_slice_in_dim(moduli, slab_index, 1, 0)
            corner_vals = corner_values(node_values, 1, NY, NZ)
            forces = jnp.dot(stiffness, corner_vals * slab_moduli.reshape(1, -1), precision=precise, preferred_element_type=jnp.float32)
            spread = spread_back(forces, 1, NY, NZ)
            plane = (upper_prev + spread[:, 0])[:, :NY, :NZ]
            return (spread[:, 1], plane)
        start_carry = jnp.zeros((3, NY + 1, NZ + 1), jnp.float32)
        _, planes = lax.scan(slab_step, start_carry, jnp.arange(NX, dtype=jnp.int32))
        return jnp.transpose(planes, (1, 0, 2, 3)) + spring_rate * vector
    displacement = jnp.zeros_like(load_field)
    residual = load_field
    direction = load_field
    norm_now = jnp.sum(residual * residual)
    for iteration in range(ITERS):
        applied = operate(direction)
        step_size = norm_now / jnp.sum(direction * applied)
        displacement = displacement + step_size * direction
        residual = residual - step_size * applied
        norm_next = jnp.sum(residual * residual)
        direction = residual + norm_next / norm_now * direction
        norm_now = norm_next
    padded_disp = jnp.pad(displacement, ((0, 0), (0, 1), (0, 1), (0, 1)))

    def slab_energy(slab_index):
        node_values = lax.dynamic_slice_in_dim(padded_disp, slab_index, 2, 1)
        corner_vals = corner_values(node_values, 1, NY, NZ)
        return corner_energy(stiffness, corner_vals).reshape(NY, NZ)
    energy = lax.map(slab_energy, jnp.arange(NX, dtype=jnp.int32))
    pushed = -3.0 * (1.0 - young_floor) * density ** 2 * cell_flags * energy * (sharpness * (1.0 - tanh_shift * tanh_shift) / scale_sum) / weight_sum
    sensitivity = cone_sum(pushed)
    return (displacement, sensitivity, density)
```

```python
import math

import jax
import jax.numpy as jnp
import numpy as np
from jax import lax
from jax.experimental import pallas as pl
from jax.experimental.pallas import tpu as pltpu
from jax.sharding import PartitionSpec as P


BRICK = 16
young_floor = 0.001
spring_rate = 0.05
sharpness = 8.0
threshold = 0.5
poisson = 0.3
ALL = ("gx", "gy", "gz")
INTERPRET = False

NXL, NYL, NZL = 16, 16, 128
WIN = 24


def element_matrix():
    lame_first = poisson / ((1.0 + poisson) * (1.0 - 2.0 * poisson))
    shear_mod = 1.0 / (2.0 * (1.0 + poisson))
    elastic = np.zeros((6, 6))
    elastic[:3, :3] = lame_first
    for axis_one in range(3):
        elastic[axis_one, axis_one] += 2.0 * shear_mod
        elastic[axis_one + 3, axis_one + 3] = shear_mod
    gauss_point = 1.0 / math.sqrt(3.0)
    stiffness = np.zeros((24, 24))
    for point_x in (-gauss_point, gauss_point):
        for point_y in (-gauss_point, gauss_point):
            for point_z in (-gauss_point, gauss_point):
                strain = np.zeros((6, 24))
                for corner in range(8):
                    sign_a = 2 * (corner // 4) - 1
                    sign_b = 2 * (corner // 2 % 2) - 1
                    sign_c = 2 * (corner % 2) - 1
                    along_x = 0.25 * sign_a * (1 + sign_b * point_y) * (1 + sign_c * point_z)
                    along_y = 0.25 * (1 + sign_a * point_x) * sign_b * (1 + sign_c * point_z)
                    along_z = 0.25 * (1 + sign_a * point_x) * (1 + sign_b * point_y) * sign_c
                    column = 3 * corner
                    strain[0, column] = along_x
                    strain[1, column + 1] = along_y
                    strain[2, column + 2] = along_z
                    strain[3, column + 1] = along_z
                    strain[3, column + 2] = along_y
                    strain[4, column] = along_z
                    strain[4, column + 2] = along_x
                    strain[5, column] = along_y
                    strain[5, column + 1] = along_x
                stiffness += strain.T @ elastic @ strain * 0.125
    return stiffness


def modal_constants():
    modes = [(px, py, pz) for px in (0, 1) for py in (0, 1) for pz in (0, 1)]
    change = np.zeros((24, 24))
    for c in range(3):
        for m, mode in enumerate(modes):
            for q in range(8):
                corner = (q // 4, q // 2 % 2, q % 2)
                sign = 1.0
                for axis in range(3):
                    if mode[axis] and not corner[axis]:
                        sign = -sign
                change[8 * c + m, 3 * q + c] = sign
    hat = change @ element_matrix() @ change.T / 64.0

    def at(c1, m1, c2, m2):
        return hat[8 * c1 + modes.index(m1), 8 * c2 + modes.index(m2)]

    k = {
        "a": at(0, (1, 0, 0), 0, (1, 0, 0)),
        "b": at(0, (1, 0, 0), 1, (0, 1, 0)),
        "p": at(0, (0, 1, 1), 0, (0, 1, 1)),
        "r": at(0, (0, 1, 1), 1, (1, 0, 1)),
        "g": at(0, (0, 1, 0), 1, (1, 0, 0)),
        "h": at(2, (1, 1, 1), 2, (1, 1, 1)),
        "c": at(1, (1, 1, 0), 1, (1, 1, 0)),
        "d": at(1, (1, 1, 0), 2, (1, 0, 1)),
    }
    made = np.zeros((24, 24))

    def put(c1, m1, c2, m2, v):
        made[8 * c1 + modes.index(m1), 8 * c2 + modes.index(m2)] += v

    for c in range(3):
        unit = tuple(int(i == c) for i in range(3))
        anti = tuple(int(i != c) for i in range(3))
        put(c, (1, 1, 1), c, (1, 1, 1), k["h"])
        for e in range(3):
            unit_e = tuple(int(i == e) for i in range(3))
            anti_e = tuple(int(i != e) for i in range(3))
            put(c, unit, e, unit_e, k["a"] if c == e else k["b"])
            put(c, anti, e, anti_e, k["p"] if c == e else k["r"])
            if c != e:
                put(c, unit_e, c, unit_e, k["g"])
                put(c, unit_e, e, unit, k["g"])
                both = tuple(int(i in (c, e)) for i in range(3))
                o = 3 - c - e
                both_o = tuple(int(i in (o, e)) for i in range(3))
                put(c, both, c, both, k["c"])
                put(c, both, o, both_o, k["d"])
    assert np.abs(made - hat).max() < 1e-12
    return k


K = modal_constants()
W = {n: 3.0 - math.sqrt(n) for n in range(9)}
KS = (0, 1, 2, 4, 5, 8)


def mode(*axes):
    return tuple(int(i in axes) for i in range(3))


def f32(x):
    return float(np.float32(x))


def roll(x, shift):
    shift = shift % 128
    return x if shift == 0 else pltpu.roll(x, shift, 1)


def lane_of(shape):
    return lax.broadcasted_iota(jnp.int32, shape, 1)


def z_next(a0, a1, lane, by=1):
    r0, r1 = roll(a0, -by), roll(a1, -by)
    edge = lane >= 128 - by
    return jnp.where(edge, r1, r0), jnp.where(edge, r0, r1)


def z_prev(a0, a1, lane, by=1):
    r0, r1 = roll(a0, by), roll(a1, by)
    edge = lane < by
    return jnp.where(edge, r1, r0), jnp.where(edge, r0, r1)


def modal_of(lo, hi):
    m = {}
    for (c, py, pz), low in lo.items():
        high = hi[c, py, pz]
        if py or pz:
            m[c, (0, py, pz)] = low + high
        m[c, (1, py, pz)] = high - low
    return m


def forces_of(m, e):
    ea, eb = e * f32(K["a"] - K["b"]), e * f32(K["b"])
    ep, er = e * f32(K["p"] - K["r"]), e * f32(K["r"])
    eg, eh = e * f32(K["g"]), e * f32(K["h"])
    ec, ed = e * f32(K["c"]), e * f32(K["d"])
    f = {}
    for first, second, pick in ((ea, eb, lambda c: mode(c)), (ep, er, lambda c: mode(*{0, 1, 2} - {c}))):
        vals = [m[c, pick(c)] for c in range(3)]
        shared = (vals[0] + vals[1] + vals[2]) * second
        for c in range(3):
            f[c, pick(c)] = vals[c] * first + shared
    for c, e2 in ((0, 1), (0, 2), (1, 2)):
        shared = (m[c, mode(e2)] + m[e2, mode(c)]) * eg
        f[c, mode(e2)] = shared
        f[e2, mode(c)] = shared
    for c in range(3):
        f[c, (1, 1, 1)] = m[c, (1, 1, 1)] * eh
    for e2 in range(3):
        c, o = [i for i in range(3) if i != e2]
        v1, v2 = m[c, mode(c, e2)], m[o, mode(o, e2)]
        f[c, mode(c, e2)] = v1 * ec + v2 * ed
        f[o, mode(o, e2)] = v2 * ec + v1 * ed
    return f


def energy_of(m):
    total = None
    for first, second, pick in (
        (K["a"] - K["b"], K["b"], lambda c: mode(c)),
        (K["p"] - K["r"], K["r"], lambda c: mode(*{0, 1, 2} - {c})),
    ):
        vals = [m[c, pick(c)] for c in range(3)]
        s = vals[0] + vals[1] + vals[2]
        part = (vals[0] * vals[0] + vals[1] * vals[1] + vals[2] * vals[2]) * f32(first) + s * s * f32(second)
        total = part if total is None else total + part
    shear = None
    for c, e2 in ((0, 1), (0, 2), (1, 2)):
        s = m[c, mode(e2)] + m[e2, mode(c)]
        shear = s * s if shear is None else shear + s * s
    total = total + shear * f32(K["g"])
    triple = None
    for c in range(3):
        v = m[c, (1, 1, 1)]
        triple = v * v if triple is None else triple + v * v
    total = total + triple * f32(K["h"])
    squares = cross = None
    for e2 in range(3):
        c, o = [i for i in range(3) if i != e2]
        v1, v2 = m[c, mode(c, e2)], m[o, mode(o, e2)]
        sq, cr = v1 * v1 + v2 * v2, v1 * v2
        squares = sq if squares is None else squares + sq
        cross = cr if cross is None else cross + cr
    return total + squares * f32(K["c"]) + cross * f32(2.0 * K["d"])


def x_parts(f0, f1, f2):
    out = {}
    for k in KS:
        v = f0 * f32(W[k])
        if k + 1 in W:
            v = v + f1 * f32(W[k + 1])
        if k + 4 in W:
            v = v + f2 * f32(W[k + 4])
        out[k] = v
    return out


def pack_z_kernel(load_ref, design_ref, out_ref):
    lane = lane_of((NYL, 128))

    def step(pair, _):
        acc = jnp.zeros((NYL, 128), jnp.float32)
        for par in range(2):
            for fld in range(4):
                off = 64 * par + 16 * fld
                src = load_ref[fld, 2 * pair + par] if fld < 3 else design_ref[2 * pair + par]
                acc = jnp.where(((lane - off + 8) & 127) < 16, roll(src, off), acc)
        out_ref[pair] = acc
        return 0

    lax.fori_loop(0, 8, step, 0)


def halo_merge(high, low):
    lane = lane_of(high.shape)
    return jnp.where((lane & 15) < 8, high, low)


def pack_y_kernel(load_ref, design_ref, zhi_ref, zlo_ref, lo_ref, hi_ref):
    def step(x, _):
        for c in range(3):
            lo_ref[c * 16 + x] = load_ref[c, x, 0:8]
            hi_ref[c * 16 + x] = load_ref[c, x, 8:16]
        lo_ref[48 + x] = design_ref[x, 0:8]
        hi_ref[48 + x] = design_ref[x, 8:16]
        return 0

    lax.fori_loop(0, 16, step, 0)

    def step2(k, _):
        lo_ref[64 + k] = halo_merge(zhi_ref[k, 0:8], zlo_ref[k, 0:8])
        hi_ref[64 + k] = halo_merge(zhi_ref[k, 8:16], zlo_ref[k, 8:16])
        return 0

    lax.fori_loop(0, 8, step2, 0)


def pack_x_kernel(load_ref, design_ref, zhi_ref, zlo_ref, ylo_ref, yhi_ref, lo_ref, hi_ref):
    def plane(dst_ref, at, own, ext):
        dst_ref[at, 0:8] = ylo_ref[ext]
        dst_ref[at, 8:24] = own
        dst_ref[at, 24:32] = yhi_ref[ext]

    for c in range(3):
        for i in range(4):
            plane(lo_ref, c * 4 + i, load_ref[c, i], c * 16 + i)
        for i in range(3):
            plane(hi_ref, c * 3 + i, load_ref[c, 13 + i], c * 16 + 13 + i)
    for i in range(5):
        plane(lo_ref, 12 + i, design_ref[i], 48 + i)
        plane(hi_ref, 9 + i, design_ref[11 + i], 48 + 11 + i)
    for i in range(3):
        plane(lo_ref, 17 + i, halo_merge(zhi_ref[i], zlo_ref[i]), 64 + i)
        plane(hi_ref, 14 + i, halo_merge(zhi_ref[5 + i], zlo_ref[5 + i]), 64 + 5 + i)


def assemble(load_ref, design_ref, zhi_ref, zlo_ref, ylo_ref, yhi_ref, xlo_ref, xhi_ref, dx, rx, hx):
    def own(x, _):
        for c in range(3):
            rx[c, x + 3, 0, 0:4] = ylo_ref[c * 16 + x, 4:8]
            rx[c, x + 3, 0, 4:20] = load_ref[c, x]
            rx[c, x + 3, 0, 20:24] = yhi_ref[c * 16 + x, 0:4]
        dx[x + 5, 0, 0:8] = ylo_ref[48 + x]
        dx[x + 5, 0, 8:24] = design_ref[x]
        dx[x + 5, 0, 24:32] = yhi_ref[48 + x]
        return 0

    lax.fori_loop(0, 16, own, 0)

    def pairs(k, _):
        hx[k + 3, 0:8] = ylo_ref[64 + k]
        hx[k + 3, 8:24] = halo_merge(zhi_ref[k], zlo_ref[k])
        hx[k + 3, 24:32] = yhi_ref[64 + k]
        return 0

    lax.fori_loop(0, 8, pairs, 0)
    for i in range(3):
        hx[i] = xlo_ref[14 + i]
        hx[11 + i] = xhi_ref[17 + i]
    for i in range(5):
        dx[i, 0] = xlo_ref[9 + i]
        dx[21 + i, 0] = xhi_ref[12 + i]
    for c in range(3):
        for i in range(3):
            rx[c, i, 0, 0:24] = xlo_ref[c * 3 + i, 4:28]
        for i in range(4):
            rx[c, 19 + i, 0, 0:24] = xhi_ref[c * 4 + i, 4:28]

    def spread(n, _):
        tile = hx[n]
        dx[2 * n, 1] = roll(tile, -(64 + 48))

        return 0

    lax.fori_loop(0, 13, spread, 0)

    def spread_even(n, _):
        dx[2 * n - 1, 1] = roll(hx[n], -48)
        return 0

    lax.fori_loop(1, 14, spread_even, 0)

    def spread_load(n, _):
        tile = hx[n, 4:28]
        for c in range(3):
            rx[c, 2 * n - 2, 1, 0:24] = roll(tile, -(64 + 16 * c))
            rx[c, 2 * n - 3, 1, 0:24] = roll(tile, -16 * c)
        return 0

    lax.fori_loop(2, 12, spread_load, 0)
    for c in range(3):
        rx[c, 0, 1, 0:24] = roll(hx[1, 4:28], -(64 + 16 * c))
        rx[c, 21, 1, 0:24] = roll(hx[12, 4:28], -16 * c)
        rx[c, 22, 1, 0:24] = roll(hx[12, 4:28], -(64 + 16 * c))


def zy_plane(tile, zt, t_ref, slot, lane, tiles=2, base=0, blocks=3):
    for c in range(3):
        a0, a1 = tile(c, 0), tile(c, 1)
        n0, n1 = z_next(a0, a1, lane)
        zt[2 * c, 0, 0:24] = a0 + n0
        zt[2 * c + 1, 0, 0:24] = n0 - a0
        if tiles == 2:
            zt[2 * c, 1, 0:24] = a1 + n1
            zt[2 * c + 1, 1, 0:24] = n1 - a1
    for f in range(6):
        for t in range(tiles):
            for b in range(blocks):
                r = base + 8 * b
                lo, hi = zt[f, t, r : r + 8], zt[f, t, r + 1 : r + 9]
                t_ref[slot, 2 * f, t, 8 * b : 8 * b + 8] = lo + hi
                t_ref[slot, 2 * f + 1, t, 8 * b : 8 * b + 8] = hi - lo


def read_t(t_ref, slot, t, b):
    out = {}
    for c in range(3):
        for pz in range(2):
            for py in range(2):
                out[c, py, pz] = t_ref[slot, 4 * c + 2 * pz + py, t, 8 * b : 8 * b + 8]
    return out


def main_kernel(
    idx_ref, flag_ref, load_ref, design_ref, zhi_ref, zlo_ref, ylo_ref, yhi_ref, xlo_ref, xhi_ref,
    dens_ref, rx, qx, gx_ref, sum_ref,
    dx, hx, av, qk, fl, mo, zt, tt, gp, yp, yg,
    *, sizes,
):
    nx, ny, nz = sizes
    i_x, i_y, i_z = idx_ref[0], idx_ref[1], idx_ref[2]
    lane = lane_of((WIN, 128))
    row = lax.broadcasted_iota(jnp.int32, (WIN, 128), 0)
    assemble(load_ref, design_ref, zhi_ref, zlo_ref, ylo_ref, yhi_ref, xlo_ref, xhi_ref, dx, rx, hx)
    zt[:, :, 24:32] = jnp.zeros((6, 2, 8, 128), jnp.float32)
    yg[:, :, 0:8] = jnp.zeros((6, 2, 8, 128), jnp.float32)
    gp[...] = jnp.zeros((12, 2, 24, 128), jnp.float32)

    y_at = i_y * NYL + row - 4
    z_at = [i_z * NZL + lane, i_z * NZL + jnp.where(lane < 64, lane + 128, lane - 128)]

    def inside(at, step, length):
        return jnp.where((at + step >= 0) & (at + step < length), 1.0, 0.0)

    y_in = [inside(y_at, 0, ny), inside(y_at, 1, ny) + inside(y_at, -1, ny), inside(y_at, 2, ny) + inside(y_at, -2, ny)]
    for t in range(2):
        z_in = [inside(z_at[t], 0, nz)] + [inside(z_at[t], s, nz) + inside(z_at[t], -s, nz) for s in (1, 2)]
        qk[0, t] = y_in[0] * z_in[0]
        qk[1, t] = y_in[1] * z_in[0] + y_in[0] * z_in[1]
        qk[2, t] = y_in[1] * z_in[1]
        qk[3, t] = y_in[2] * z_in[0] + y_in[0] * z_in[2]
        qk[4, t] = y_in[1] * z_in[2] + y_in[2] * z_in[1]
        qk[5, t] = y_in[2] * z_in[2]
    for xc in range(3):
        lines = []
        for yc in range(3):
            main = jnp.zeros((WIN, 128), jnp.float32)
            for n in range(8):
                main = jnp.where((lane >> 4) == n, flag_ref[xc, yc, n + 1].astype(jnp.float32), main)
            side = jnp.where(
                lane < 64, flag_ref[xc, yc, 9].astype(jnp.float32), flag_ref[xc, yc, 0].astype(jnp.float32)
            )
            lines.append((main, side))
        for t in range(2):
            fl[xc, t] = jnp.where(row < 4, lines[0][t], jnp.where(row < 20, lines[1][t], lines[2][t]))

    lift = math.tanh(sharpness * threshold)
    scale = lift + math.tanh(sharpness * (1.0 - threshold))

    def scalar_inside(at, step):
        return jnp.where((at + step >= 0) & (at + step < nx), 1.0, 0.0)

    def density_step(e, _):
        for t in range(2):
            f0 = dx[e + 2, t]
            f1 = dx[e + 1, t] + dx[e + 3, t]
            f2 = dx[e, t] + dx[e + 4, t]
            for n, v in enumerate(x_parts(f0, f1, f2).values()):
                av[n, t] = v
        x_at = i_x * NXL + e - 3
        x0 = scalar_inside(x_at, 0)
        x1 = scalar_inside(x_at, 1) + scalar_inside(x_at, -1)
        x2 = scalar_inside(x_at, 2) + scalar_inside(x_at, -2)
        cls = jnp.where(e < 3, 0, jnp.where(e < 19, 1, 2))
        b = []
        for t in range(2):
            b.append(
                [
                    av[0, t, 4:28] + (av[1, t, 3:27] + av[1, t, 5:29]) + (av[3, t, 2:26] + av[3, t, 6:30]),
                    av[1, t, 4:28] + (av[2, t, 3:27] + av[2, t, 5:29]) + (av[4, t, 2:26] + av[4, t, 6:30]),
                    av[3, t, 4:28] + (av[4, t, 3:27] + av[4, t, 5:29]) + (av[5, t, 2:26] + av[5, t, 6:30]),
                ]
            )
        n1, p1 = z_next(b[0][1], b[1][1], lane), z_prev(b[0][1], b[1][1], lane)
        n2, p2 = z_next(b[0][2], b[1][2], lane, 2), z_prev(b[0][2], b[1][2], lane, 2)
        weights = x_parts(x0, x1, x2)
        for t in range(2):
            cone = b[t][0] + (n1[t] + p1[t]) + (n2[t] + p2[t])
            ws = None
            for n, wk in enumerate(weights.values()):
                ws = qk[n, t] * wk if ws is None else ws + qk[n, t] * wk
            inv = 1.0 / jnp.maximum(ws, 1.0)
            th = jnp.tanh(sharpness * (cone * inv - threshold))
            dens = (lift + th) * f32(1.0 / scale)
            flag = fl[cls, t]
            sq = dens * dens
            mo[e, t] = (young_floor + sq * dens * (1.0 - young_floor)) * flag
            gx_ref[e, t] = sq * flag * (1.0 - th * th) * inv * f32(-3.0 * (1.0 - young_floor) * sharpness / scale)
            if t == 0:
                av[0, 0, 0:24] = dens

        @pl.when((e >= 3) & (e < 19))
        def _():
            dens_ref[e - 3] = av[0, 0, 4:20]

        return 0

    lax.fori_loop(0, 22, density_step, 0)

    clamp = [jnp.where((y_at < ny) & (z_at[t] < nz), 1.0, 0.0) for t in range(2)]
    zy_plane(lambda c, t: rx[c, 0, t, 0:24], zt, tt, 0, lane)

    def operate_step(e, _):
        new = (e + 1) & 1
        old = e & 1
        zy_plane(lambda c, t: rx[c, e + 1, t, 0:24], zt, tt, new, lane)
        for t in range(2):
            for b in range(3):
                rows = slice(8 * b, 8 * b + 8)
                force = forces_of(modal_of(read_t(tt, old, t, b), read_t(tt, new, t, b)), mo[e, t, rows])
                for c in range(3):
                    for pz in range(2):
                        n = []
                        for py in range(2):
                            fd = force[c, (1, py, pz)]
                            fs = force.get((c, (0, py, pz)))
                            at = 4 * c + 2 * pz + py
                            before = gp[at, t, rows]
                            if fs is None:
                                gp[at, t, rows] = fd
                                n.append(before - fd)
                            else:
                                gp[at, t, rows] = fs + fd
                                n.append((fs - fd) + before)
                        yp[2 * c + pz, t, rows] = n[0] - n[1]
                        yg[2 * c + pz, t, 8 + 8 * b : 16 + 8 * b] = n[0] + n[1]

        @pl.when(e > 0)
        def _():
            x_on = jnp.where(i_x * NXL + e - 3 < nx, 1.0, 0.0)
            for c in range(3):
                p, g = [], []
                for t in range(2):
                    zs = yp[2 * c, t] + yg[2 * c, t, 7:31]
                    zd = yp[2 * c + 1, t] + yg[2 * c + 1, t, 7:31]
                    p.append(zs - zd)
                    g.append(zs + zd)
                gb = z_prev(g[0], g[1], lane)
                for t in range(2):
                    value = p[t] + gb[t] + rx[c, e, t, 0:24] * spring_rate
                    qx[c, e - 1, t, 0:24] = value * (clamp[t] * x_on)

        return 0

    lax.fori_loop(0, 22, operate_step, 0)

    zy_plane(lambda c, t: qx[c, 2, t, 0:24], zt, tt, 0, lane, tiles=1, base=4, blocks=2)
    zero = jnp.zeros((8, 128), jnp.float32)

    def sum_step(x, acc):
        s0, s1, s2, s3 = acc
        new, old = (x + 1) & 1, x & 1
        zy_plane(lambda c, t: qx[c, x + 3, t, 0:24], zt, tt, new, lane, tiles=1, base=4, blocks=2)
        for b in range(2):
            rows = slice(4 + 8 * b, 12 + 8 * b)
            for c in range(3):
                r, q = rx[c, x + 3, 0, rows], qx[c, x + 2, 0, rows]
                s0, s1, s2 = s0 + r * r, s1 + r * q, s2 + q * q
            m = modal_of(read_t(tt, old, 0, b), read_t(tt, new, 0, b))
            s3 = s3 + energy_of(m) * mo[x + 3, 0, rows]
        return s0, s1, s2, s3

    sums = lax.fori_loop(0, 16, sum_step, (zero, zero, zero, zero))
    line = jnp.zeros((8, 128), jnp.float32)
    lane8 = lane_of((8, 128))
    for n, s in enumerate(sums):
        total = jnp.sum(jnp.sum(s, axis=0, keepdims=True), axis=1, keepdims=True)
        line = jnp.where(lane8 == n, total, line)
    for n in range(sum_ref.shape[0] // 8):
        sum_ref[8 * n : 8 * n + 8] = line


def final_kernel(sum_ref, rx, qx, gx_ref, disp_ref, sens_ref, ux, zt, tt, px, av):
    lane = lane_of((WIN, 128))
    line = jnp.sum(sum_ref[...], axis=0, keepdims=True)
    lane1 = lane_of((1, 128))
    m0, m1, m2, m3 = [jnp.sum(jnp.where(lane1 == n, line, 0.0), axis=1, keepdims=True) for n in range(4)]
    m3 = m3 + spring_rate * m2
    first = m0 / m1
    norm = m0 - 2.0 * first * m1 + first * first * m2
    ratio = norm / m0
    grown = 1.0 + ratio
    second = norm / (grown * grown * m1 - 2.0 * first * grown * m2 + first * first * m3)
    c0 = jnp.broadcast_to(first + second * grown, (WIN, 128))
    c1 = jnp.broadcast_to(-second * first, (WIN, 128))
    zt[:, :, 24:32] = jnp.zeros((6, 2, 8, 128), jnp.float32)

    def displace(i, slot):
        for c in range(3):
            for t in range(2):
                ux[c, t, 0:24] = c0 * rx[c, i + 1, t, 0:24] + c1 * qx[c, i, t, 0:24]
        zy_plane(lambda c, t: ux[c, t, 0:24], zt, tt, slot, lane)

    displace(0, 0)

    def energy_step(i, _):
        new, old = (i + 1) & 1, i & 1
        displace(i + 1, new)

        @pl.when((i >= 1) & (i < 17))
        def _():
            for c in range(3):
                disp_ref[c, i - 1] = ux[c, 0, 4:20]

        for t in range(2):
            for b in range(3):
                rows = slice(8 * b, 8 * b + 8)
                m = modal_of(read_t(tt, old, t, b), read_t(tt, new, t, b))
                px[i, t, rows] = energy_of(m) * gx_ref[i + 1, t, rows]
        return 0

    lax.fori_loop(0, 20, energy_step, 0)
    lane16 = lane_of((NYL, 128))

    def cone_step(x, _):
        for t in range(2):
            f0 = px[x + 2, t]
            f1 = px[x + 1, t] + px[x + 3, t]
            f2 = px[x, t] + px[x + 4, t]
            for n, v in enumerate(x_parts(f0, f1, f2).values()):
                av[n, t, 0:24] = v
        b = []
        for t in range(2):
            b.append(
                [
                    av[0, t, 4:20] + (av[1, t, 3:19] + av[1, t, 5:21]) + (av[3, t, 2:18] + av[3, t, 6:22]),
                    av[1, t, 4:20] + (av[2, t, 3:19] + av[2, t, 5:21]) + (av[4, t, 2:18] + av[4, t, 6:22]),
                    av[3, t, 4:20] + (av[4, t, 3:19] + av[4, t, 5:21]) + (av[5, t, 2:18] + av[5, t, 6:22]),
                ]
            )
        n1, p1 = z_next(b[0][1], b[1][1], lane16)[0], z_prev(b[0][1], b[1][1], lane16)[0]
        n2, p2 = z_next(b[0][2], b[1][2], lane16, 2)[0], z_prev(b[0][2], b[1][2], lane16, 2)[0]
        sens_ref[x] = b[0][0] + (n1 + p1) + (n2 + p2)
        return 0

    lax.fori_loop(0, 16, cone_step, 0)


def s(*shape):
    return jax.ShapeDtypeStruct(shape, jnp.float32)


def v(*shape):
    return pltpu.VMEM(shape, jnp.float32)


def call(kernel, outs, scratch, *args, smem=0, **kw):
    spec_s, spec_v = pl.BlockSpec(memory_space=pltpu.SMEM), pl.BlockSpec(memory_space=pltpu.VMEM)
    single = not isinstance(outs, (tuple, list))
    return pl.pallas_call(
        kernel,
        out_shape=outs,
        in_specs=[spec_s] * smem + [spec_v] * (len(args) - smem),
        out_specs=spec_v if single else [spec_v] * len(outs),
        scratch_shapes=scratch,
        interpret=INTERPRET,
        **kw,
    )(*args)


def moved(block, axis, step):
    count = lax.axis_size(axis)
    return lax.ppermute(block, axis, [(i, i - step) for i in range(count) if 0 <= i - step < count])


def body(load, design, solid_map):
    ix, iy, iz = (lax.axis_index(a) for a in ALL)
    nx, ny, nz = (lax.axis_size(a) * n for a, n in zip(ALL, (NXL, NYL, NZL)))
    count = lax.axis_size("gx") * lax.axis_size("gy") * lax.axis_size("gz")
    idx = jnp.stack([ix, iy, iz]).astype(jnp.int32)
    flags = lax.dynamic_slice(jnp.pad(solid_map, 1), (ix, iy, iz * (NZL // BRICK)), (3, 3, 10))

    zc = call(pack_z_kernel, s(8, 16, 128), [], load, design)
    zhi, zlo = moved(zc, "gz", 1), moved(zc, "gz", -1)
    ylo_s, yhi_s = call(pack_y_kernel, (s(72, 8, 128), s(72, 8, 128)), [], load, design, zhi, zlo)
    yhi, ylo = moved(ylo_s, "gy", 1), moved(yhi_s, "gy", -1)
    xlo_s, xhi_s = call(
        pack_x_kernel, (s(20, 32, 128), s(17, 32, 128)), [], load, design, zhi, zlo, ylo, yhi
    )
    xhi, xlo = moved(xlo_s, "gx", 1), moved(xhi_s, "gx", -1)

    def main(*refs):
        main_kernel(*refs, sizes=(nx, ny, nz))

    dens, rx, qx, gfac, part = call(
        main,
        (s(16, 16, 128), s(3, 23, 2, 32, 128), s(3, 21, 2, 32, 128), s(22, 2, 24, 128), s(count, 128)),
        [
            v(26, 2, 32, 128), v(14, 32, 128), v(6, 2, 32, 128), v(6, 2, 24, 128), v(3, 2, 24, 128), v(22, 2, 24, 128),
            v(6, 2, 32, 128), v(2, 12, 2, 24, 128), v(12, 2, 24, 128), v(6, 2, 24, 128), v(6, 2, 32, 128),
        ],
        idx, flags, load, design, zhi, zlo, ylo, yhi, xlo, xhi, smem=2,
    )
    sums = lax.all_to_all(part, ALL, 0, 0, tiled=True)
    disp, sens = call(
        final_kernel,
        (s(3, 16, 16, 128), s(16, 16, 128)),
        [v(3, 2, 24, 128), v(6, 2, 32, 128), v(2, 12, 2, 24, 128), v(20, 2, 24, 128), v(6, 2, 32, 128)],
        sums, rx, qx, gfac,
    )
    return disp, sens, dens


def solution(mesh):
    nodal, cell = P(None, "gx", "gy", "gz"), P("gx", "gy", "gz")
    return jax.shard_map(
        body, mesh=mesh, in_specs=(nodal, cell, P()), out_specs=(nodal, cell, cell), check_vma=False
    )
```

```python
import math

import jax
import jax.numpy as jnp
import numpy as np
from jax import lax
from jax.experimental import pallas as pl
from jax.experimental.pallas import tpu as pltpu
from jax.sharding import PartitionSpec as P


BRICK = 16
young_floor = 0.001
spring_rate = 0.05
sharpness = 8.0
threshold = 0.5
poisson = 0.3
ALL = ("gx", "gy", "gz")
INTERPRET = False

NXL, NYL, NZL = 16, 16, 128
WIN = 24


def element_matrix():
    lame_first = poisson / ((1.0 + poisson) * (1.0 - 2.0 * poisson))
    shear_mod = 1.0 / (2.0 * (1.0 + poisson))
    elastic = np.zeros((6, 6))
    elastic[:3, :3] = lame_first
    for axis_one in range(3):
        elastic[axis_one, axis_one] += 2.0 * shear_mod
        elastic[axis_one + 3, axis_one + 3] = shear_mod
    gauss_point = 1.0 / math.sqrt(3.0)
    stiffness = np.zeros((24, 24))
    for point_x in (-gauss_point, gauss_point):
        for point_y in (-gauss_point, gauss_point):
            for point_z in (-gauss_point, gauss_point):
                strain = np.zeros((6, 24))
                for corner in range(8):
                    sign_a = 2 * (corner // 4) - 1
                    sign_b = 2 * (corner // 2 % 2) - 1
                    sign_c = 2 * (corner % 2) - 1
                    along_x = 0.25 * sign_a * (1 + sign_b * point_y) * (1 + sign_c * point_z)
                    along_y = 0.25 * (1 + sign_a * point_x) * sign_b * (1 + sign_c * point_z)
                    along_z = 0.25 * (1 + sign_a * point_x) * (1 + sign_b * point_y) * sign_c
                    column = 3 * corner
                    strain[0, column] = along_x
                    strain[1, column + 1] = along_y
                    strain[2, column + 2] = along_z
                    strain[3, column + 1] = along_z
                    strain[3, column + 2] = along_y
                    strain[4, column] = along_z
                    strain[4, column + 2] = along_x
                    strain[5, column] = along_y
                    strain[5, column + 1] = along_x
                stiffness += strain.T @ elastic @ strain * 0.125
    return stiffness


def modal_constants():
    modes = [(px, py, pz) for px in (0, 1) for py in (0, 1) for pz in (0, 1)]
    change = np.zeros((24, 24))
    for c in range(3):
        for m, mode in enumerate(modes):
            for q in range(8):
                corner = (q // 4, q // 2 % 2, q % 2)
                sign = 1.0
                for axis in range(3):
                    if mode[axis] and not corner[axis]:
                        sign = -sign
                change[8 * c + m, 3 * q + c] = sign
    hat = change @ element_matrix() @ change.T / 64.0

    def at(c1, m1, c2, m2):
        return hat[8 * c1 + modes.index(m1), 8 * c2 + modes.index(m2)]

    k = {
        "a": at(0, (1, 0, 0), 0, (1, 0, 0)),
        "b": at(0, (1, 0, 0), 1, (0, 1, 0)),
        "p": at(0, (0, 1, 1), 0, (0, 1, 1)),
        "r": at(0, (0, 1, 1), 1, (1, 0, 1)),
        "g": at(0, (0, 1, 0), 1, (1, 0, 0)),
        "h": at(2, (1, 1, 1), 2, (1, 1, 1)),
        "c": at(1, (1, 1, 0), 1, (1, 1, 0)),
        "d": at(1, (1, 1, 0), 2, (1, 0, 1)),
    }
    made = np.zeros((24, 24))

    def put(c1, m1, c2, m2, v):
        made[8 * c1 + modes.index(m1), 8 * c2 + modes.index(m2)] += v

    for c in range(3):
        unit = tuple(int(i == c) for i in range(3))
        anti = tuple(int(i != c) for i in range(3))
        put(c, (1, 1, 1), c, (1, 1, 1), k["h"])
        for e in range(3):
            unit_e = tuple(int(i == e) for i in range(3))
            anti_e = tuple(int(i != e) for i in range(3))
            put(c, unit, e, unit_e, k["a"] if c == e else k["b"])
            put(c, anti, e, anti_e, k["p"] if c == e else k["r"])
            if c != e:
                put(c, unit_e, c, unit_e, k["g"])
                put(c, unit_e, e, unit, k["g"])
                both = tuple(int(i in (c, e)) for i in range(3))
                o = 3 - c - e
                both_o = tuple(int(i in (o, e)) for i in range(3))
                put(c, both, c, both, k["c"])
                put(c, both, o, both_o, k["d"])
    assert np.abs(made - hat).max() < 1e-12
    return k


K = modal_constants()
W = {n: 3.0 - math.sqrt(n) for n in range(9)}
KS = (0, 1, 2, 4, 5, 8)


def mode(*axes):
    return tuple(int(i in axes) for i in range(3))


def f32(x):
    return float(np.float32(x))


def roll(x, shift):
    shift = shift % 128
    return x if shift == 0 else pltpu.roll(x, shift, 1)


def lane_of(shape):
    return lax.broadcasted_iota(jnp.int32, shape, 1)


def z_next(a0, a1, lane, by=1):
    r0, r1 = roll(a0, -by), roll(a1, -by)
    edge = lane >= 128 - by
    return jnp.where(edge, r1, r0), jnp.where(edge, r0, r1)


def z_prev(a0, a1, lane, by=1):
    r0, r1 = roll(a0, by), roll(a1, by)
    edge = lane < by
    return jnp.where(edge, r1, r0), jnp.where(edge, r0, r1)


def modal_of(lo, hi):
    m = {}
    for (c, py, pz), low in lo.items():
        high = hi[c, py, pz]
        if py or pz:
            m[c, (0, py, pz)] = low + high
        m[c, (1, py, pz)] = high - low
    return m


def forces_of(m, e):
    ea, eb = e * f32(K["a"] - K["b"]), e * f32(K["b"])
    ep, er = e * f32(K["p"] - K["r"]), e * f32(K["r"])
    eg, eh = e * f32(K["g"]), e * f32(K["h"])
    ec, ed = e * f32(K["c"]), e * f32(K["d"])
    f = {}
    for first, second, pick in ((ea, eb, lambda c: mode(c)), (ep, er, lambda c: mode(*{0, 1, 2} - {c}))):
        vals = [m[c, pick(c)] for c in range(3)]
        shared = (vals[0] + vals[1] + vals[2]) * second
        for c in range(3):
            f[c, pick(c)] = vals[c] * first + shared
    for c, e2 in ((0, 1), (0, 2), (1, 2)):
        shared = (m[c, mode(e2)] + m[e2, mode(c)]) * eg
        f[c, mode(e2)] = shared
        f[e2, mode(c)] = shared
    for c in range(3):
        f[c, (1, 1, 1)] = m[c, (1, 1, 1)] * eh
    for e2 in range(3):
        c, o = [i for i in range(3) if i != e2]
        v1, v2 = m[c, mode(c, e2)], m[o, mode(o, e2)]
        f[c, mode(c, e2)] = v1 * ec + v2 * ed
        f[o, mode(o, e2)] = v2 * ec + v1 * ed
    return f


def energy_of(m):
    total = None
    for first, second, pick in (
        (K["a"] - K["b"], K["b"], lambda c: mode(c)),
        (K["p"] - K["r"], K["r"], lambda c: mode(*{0, 1, 2} - {c})),
    ):
        vals = [m[c, pick(c)] for c in range(3)]
        s = vals[0] + vals[1] + vals[2]
        part = (vals[0] * vals[0] + vals[1] * vals[1] + vals[2] * vals[2]) * f32(first) + s * s * f32(second)
        total = part if total is None else total + part
    shear = None
    for c, e2 in ((0, 1), (0, 2), (1, 2)):
        s = m[c, mode(e2)] + m[e2, mode(c)]
        shear = s * s if shear is None else shear + s * s
    total = total + shear * f32(K["g"])
    triple = None
    for c in range(3):
        v = m[c, (1, 1, 1)]
        triple = v * v if triple is None else triple + v * v
    total = total + triple * f32(K["h"])
    squares = cross = None
    for e2 in range(3):
        c, o = [i for i in range(3) if i != e2]
        v1, v2 = m[c, mode(c, e2)], m[o, mode(o, e2)]
        sq, cr = v1 * v1 + v2 * v2, v1 * v2
        squares = sq if squares is None else squares + sq
        cross = cr if cross is None else cross + cr
    return total + squares * f32(K["c"]) + cross * f32(2.0 * K["d"])


def x_parts(f0, f1, f2):
    out = {}
    for k in KS:
        v = f0 * f32(W[k])
        if k + 1 in W:
            v = v + f1 * f32(W[k + 1])
        if k + 4 in W:
            v = v + f2 * f32(W[k + 4])
        out[k] = v
    return out


def pack_z_kernel(load_ref, design_ref, out_ref):
    lane = lane_of((NYL, 128))

    def step(pair, _):
        acc = jnp.zeros((NYL, 128), jnp.float32)
        for par in range(2):
            for fld in range(4):
                off = 64 * par + 16 * fld
                src = load_ref[fld, 2 * pair + par] if fld < 3 else design_ref[2 * pair + par]
                acc = jnp.where(((lane - off + 8) & 127) < 16, roll(src, off), acc)
        out_ref[pair] = acc
        return 0

    lax.fori_loop(0, 8, step, 0)


def halo_merge(high, low):
    lane = lane_of(high.shape)
    return jnp.where((lane & 15) < 8, high, low)


def pack_y_kernel(load_ref, design_ref, zhi_ref, zlo_ref, lo_ref, hi_ref):
    for dst, quad, one in ((lo_ref, 0, 4), (hi_ref, 12, 11)):
        rows = slice(quad, quad + 4)
        for x in range(16):
            dst[x, 0:4] = load_ref[0, x, rows]
            dst[x, 4:8] = load_ref[1, x, rows]
            dst[16 + x, 0:4] = load_ref[2, x, rows]
            dst[16 + x, 4:8] = design_ref[x, rows]
            dst[32 + x // 8, x % 8 : x % 8 + 1] = design_ref[x, one : one + 1]
        for k in range(8):
            dst[35 + k // 2, 4 * (k % 2) : 4 * (k % 2) + 4] = halo_merge(zhi_ref[k, rows], zlo_ref[k, rows])
            dst[34, k : k + 1] = halo_merge(zhi_ref[k, one : one + 1], zlo_ref[k, one : one + 1])


def pack_x_kernel(load_ref, design_ref, zhi_ref, zlo_ref, ylo_ref, yhi_ref, rx, dx, lo_ref, hi_ref, hx):
    none = jnp.zeros((8, 128), jnp.float32)
    for k in range(8):
        half = slice(4 * (k % 2), 4 * (k % 2) + 4)
        hx[k, 0:8] = none
        hx[k, 24:32] = none
        hx[k, 3:4] = ylo_ref[34, k : k + 1]
        hx[k, 4:8] = ylo_ref[35 + k // 2, half]
        hx[k, 8:24] = halo_merge(zhi_ref[k], zlo_ref[k])
        hx[k, 24:28] = yhi_ref[35 + k // 2, half]
        hx[k, 28:29] = yhi_ref[34, k : k + 1]
    for x in range(16):
        for c in range(3):
            tile, half = (x, slice(4 * c, 4 * c + 4)) if c < 2 else (16 + x, slice(0, 4))
            rx[c, x + 3, 0, 0:4] = ylo_ref[tile, half]
            rx[c, x + 3, 0, 4:20] = load_ref[c, x]
            rx[c, x + 3, 0, 20:24] = yhi_ref[tile, half]
        one = slice(x % 8, x % 8 + 1)
        dx[x + 5, 0, 0:8] = none
        dx[x + 5, 0, 24:32] = none
        dx[x + 5, 0, 3:4] = ylo_ref[32 + x // 8, one]
        dx[x + 5, 0, 4:8] = ylo_ref[16 + x, 4:8]
        dx[x + 5, 0, 8:24] = design_ref[x]
        dx[x + 5, 0, 24:28] = yhi_ref[16 + x, 4:8]
        dx[x + 5, 0, 28:29] = yhi_ref[32 + x // 8, one]
    for i in range(5):
        lo_ref[288 + 32 * i : 320 + 32 * i] = dx[5 + i, 0]
        hi_ref[216 + 32 * i : 248 + 32 * i] = dx[16 + i, 0]
    for i in range(3):
        lo_ref[448 + 32 * i : 480 + 32 * i] = hx[i]
        hi_ref[376 + 32 * i : 408 + 32 * i] = hx[5 + i]
    for c in range(3):
        for i in range(4):
            lo_ref[24 * (4 * c + i) : 24 * (4 * c + i) + 24] = rx[c, 3 + i, 0]
        for i in range(3):
            hi_ref[24 * (3 * c + i) : 24 * (3 * c + i) + 24] = rx[c, 16 + i, 0]
    for k in range(8):
        spread_pair(hx[k], 2 * k, (2 * k, 2 * k + 1), rx, dx, True)


def spread_pair(tile, x, wanted, rx, dx, both):
    for par in range(2):
        if x + par in wanted:
            dx[x + par + 5, 1] = roll(tile, -(64 * par + 48))
            if both or -3 <= x + par <= 19:
                for c in range(3):
                    rx[c, x + par + 3, 1] = roll(tile, -(64 * par + 16 * c))[4:28]


def x_halos(xlo_ref, xhi_ref, rx, dx):
    for c in range(3):
        for i in range(4):
            rx[c, 19 + i, 0] = xhi_ref[24 * (4 * c + i) : 24 * (4 * c + i) + 24]
        for i in range(3):
            rx[c, i, 0] = xlo_ref[24 * (3 * c + i) : 24 * (3 * c + i) + 24]
    for i in range(5):
        dx[21 + i, 0] = xhi_ref[288 + 32 * i : 320 + 32 * i]
        dx[i, 0] = xlo_ref[216 + 32 * i : 248 + 32 * i]
    for i in range(3):
        spread_pair(xhi_ref[448 + 32 * i : 480 + 32 * i], 16 + 2 * i, range(16, 21), rx, dx, False)
        spread_pair(xlo_ref[376 + 32 * i : 408 + 32 * i], -6 + 2 * i, range(-5, 0), rx, dx, False)


def place_kernel(map_ref, qk, fl, cl, *, sizes):
    nx, ny, nz = sizes
    i_x, i_y, i_z = (lax.axis_index(a) for a in ALL)
    lane = lane_of((WIN, 128))
    row = lax.broadcasted_iota(jnp.int32, (WIN, 128), 0)
    y_at = i_y * NYL + row - 4
    z_at = [i_z * NZL + lane, i_z * NZL + jnp.where(lane < 64, lane + 128, lane - 128)]

    def inside(at, step, length):
        return jnp.where((at + step >= 0) & (at + step < length), 1.0, 0.0)

    y_in = [inside(y_at, 0, ny)] + [inside(y_at, s, ny) + inside(y_at, -s, ny) for s in (1, 2)]
    for t in range(2):
        z_in = [inside(z_at[t], 0, nz)] + [inside(z_at[t], s, nz) + inside(z_at[t], -s, nz) for s in (1, 2)]
        qk[0, t] = y_in[0] * z_in[0]
        qk[1, t] = y_in[1] * z_in[0] + y_in[0] * z_in[1]
        qk[2, t] = y_in[1] * z_in[1]
        qk[3, t] = y_in[2] * z_in[0] + y_in[0] * z_in[2]
        qk[4, t] = y_in[1] * z_in[2] + y_in[2] * z_in[1]
        qk[5, t] = y_in[2] * z_in[2]
        cl[t] = y_in[0] * z_in[0]
    gbx, gby, gbz = nx // BRICK, ny // BRICK, nz // BRICK
    bricks = NZL // BRICK

    def flag_at(bx, by, bz):
        ok = (bx >= 0) & (bx < gbx) & (by >= 0) & (by < gby) & (bz >= 0) & (bz < gbz)
        value = map_ref[jnp.clip(bx, 0, gbx - 1), jnp.clip(by, 0, gby - 1), jnp.clip(bz, 0, gbz - 1)]
        return jnp.where(ok, value, 0).astype(jnp.float32)

    for xc in range(3):
        lines = []
        for yc in range(3):
            flag = [flag_at(i_x + xc - 1, i_y + yc - 1, i_z * bricks + n - 1) for n in range(bricks + 2)]
            main = jnp.zeros((WIN, 128), jnp.float32)
            for n in range(bricks):
                main = jnp.where((lane >> 4) == n, flag[n + 1], main)
            lines.append((main, jnp.where(lane < 64, flag[bricks + 1], flag[0])))
        for t in range(2):
            fl[xc, t] = jnp.where(row < 4, lines[0][t], jnp.where(row < 20, lines[1][t], lines[2][t]))


def zy_plane(tile, zt, t_ref, slot, lane, tiles=2, base=0, blocks=3):
    for c in range(3):
        a0, a1 = tile(c, 0), tile(c, 1)
        n0, n1 = z_next(a0, a1, lane)
        zt[2 * c, 0, 0:24] = a0 + n0
        zt[2 * c + 1, 0, 0:24] = n0 - a0
        if tiles == 2:
            zt[2 * c, 1, 0:24] = a1 + n1
            zt[2 * c + 1, 1, 0:24] = n1 - a1
    for f in range(6):
        for t in range(tiles):
            for b in range(blocks):
                r = base + 8 * b
                lo, hi = zt[f, t, r : r + 8], zt[f, t, r + 1 : r + 9]
                t_ref[slot, 2 * f, t, 8 * b : 8 * b + 8] = lo + hi
                t_ref[slot, 2 * f + 1, t, 8 * b : 8 * b + 8] = hi - lo


def read_t(t_ref, slot, t, b):
    out = {}
    for c in range(3):
        for pz in range(2):
            for py in range(2):
                out[c, py, pz] = t_ref[slot, 4 * c + 2 * pz + py, t, 8 * b : 8 * b + 8]
    return out


LIFT = math.tanh(sharpness * threshold)
SCALE = LIFT + math.tanh(sharpness * (1.0 - threshold))


def cone_yz(av, t, rows):
    lo, hi = rows

    def at(n, step):
        return av[n, t, lo + step : hi + step]

    def both(n, step):
        return at(n, -step) + at(n, step)

    return [
        at(0, 0) + both(1, 1) + both(3, 2),
        at(1, 0) + both(2, 1) + both(4, 2),
        at(3, 0) + both(4, 1) + both(5, 2),
    ]


def density_planes(first, last, nx, dx, qk, fl, av, mo, gf, dens_ref):
    lane = lane_of((WIN, 128))
    i_x = lax.axis_index("gx")

    def scalar_inside(at, step):
        return jnp.where((at + step >= 0) & (at + step < nx), 1.0, 0.0)

    def step(e, _):
        for t in range(2):
            f0 = dx[e + 2, t]
            f1 = dx[e + 1, t] + dx[e + 3, t]
            f2 = dx[e, t] + dx[e + 4, t]
            for n, part in enumerate(x_parts(f0, f1, f2).values()):
                av[n, t] = part
        x_at = i_x * NXL + e - 3
        x0 = scalar_inside(x_at, 0)
        x1 = scalar_inside(x_at, 1) + scalar_inside(x_at, -1)
        x2 = scalar_inside(x_at, 2) + scalar_inside(x_at, -2)
        cls = jnp.where(e < 3, 0, jnp.where(e < 19, 1, 2))
        b = [cone_yz(av, t, (4, 28)) for t in range(2)]
        n1, p1 = z_next(b[0][1], b[1][1], lane), z_prev(b[0][1], b[1][1], lane)
        n2, p2 = z_next(b[0][2], b[1][2], lane, 2), z_prev(b[0][2], b[1][2], lane, 2)
        weights = x_parts(x0, x1, x2)
        for t in range(2):
            cone = b[t][0] + (n1[t] + p1[t]) + (n2[t] + p2[t])
            ws = None
            for n, wk in enumerate(weights.values()):
                ws = qk[n, t] * wk if ws is None else ws + qk[n, t] * wk
            inv = 1.0 / jnp.maximum(ws, 1.0)
            th = jnp.tanh(sharpness * (cone * inv - threshold))
            dens = (LIFT + th) * f32(1.0 / SCALE)
            flag = fl[cls, t]
            sq = dens * dens
            mo[e, t] = (young_floor + sq * dens * (1.0 - young_floor)) * flag
            gf[e, t] = sq * flag * (1.0 - th * th) * inv * f32(-3.0 * (1.0 - young_floor) * sharpness / SCALE)
            if t == 0:
                av[0, 0, 0:24] = dens

        @pl.when((e >= 3) & (e < 19))
        def _():
            dens_ref[e - 3] = av[0, 0, 4:20]

        return 0

    lax.fori_loop(first, last, step, 0)


def operate_planes(first, last, nx, rx, mo, cl, qx, zt, tt, gp, yp, yg):
    lane = lane_of((WIN, 128))
    i_x = lax.axis_index("gx")
    gp[...] = jnp.zeros((12, 2, 24, 128), jnp.float32)
    zy_plane(lambda c, t: rx[c, first, t], zt, tt, first & 1, lane)

    def step(e, _):
        new, old = (e + 1) & 1, e & 1
        zy_plane(lambda c, t: rx[c, e + 1, t], zt, tt, new, lane)
        for t in range(2):
            for b in range(3):
                rows = slice(8 * b, 8 * b + 8)
                force = forces_of(modal_of(read_t(tt, old, t, b), read_t(tt, new, t, b)), mo[e, t, rows])
                for c in range(3):
                    for pz in range(2):
                        n = []
                        for py in range(2):
                            fd = force[c, (1, py, pz)]
                            fs = force.get((c, (0, py, pz)))
                            at = 4 * c + 2 * pz + py
                            before = gp[at, t, rows]
                            if fs is None:
                                gp[at, t, rows] = fd
                                n.append(before - fd)
                            else:
                                gp[at, t, rows] = fs + fd
                                n.append((fs - fd) + before)
                        yp[2 * c + pz, t, rows] = n[0] - n[1]
                        yg[2 * c + pz, t, 8 + 8 * b : 16 + 8 * b] = n[0] + n[1]

        @pl.when(e > first)
        def _():
            x_on = jnp.where(i_x * NXL + e - 3 < nx, 1.0, 0.0)
            for c in range(3):
                p, g = [], []
                for t in range(2):
                    zs = yp[2 * c, t] + yg[2 * c, t, 7:31]
                    zd = yp[2 * c + 1, t] + yg[2 * c + 1, t, 7:31]
                    p.append(zs - zd)
                    g.append(zs + zd)
                gb = z_prev(g[0], g[1], lane)
                for t in range(2):
                    value = p[t] + gb[t] + rx[c, e, t] * spring_rate
                    qx[c, e - 1, t] = value * (cl[t] * x_on)

        return 0

    lax.fori_loop(first, last, step, 0)


def sum_planes(first, last, acc, rx, qx, mo, zt, tt):
    lane = lane_of((WIN, 128))
    zy_plane(lambda c, t: qx[c, first + 2, t], zt, tt, first & 1, lane, tiles=1, base=4, blocks=2)

    def step(x, acc):
        s0, s1, s2, s3 = acc
        new, old = (x + 1) & 1, x & 1
        zy_plane(lambda c, t: qx[c, x + 3, t], zt, tt, new, lane, tiles=1, base=4, blocks=2)
        for b in range(2):
            rows = slice(4 + 8 * b, 12 + 8 * b)
            for c in range(3):
                r, q = rx[c, x + 3, 0, rows], qx[c, x + 2, 0, rows]
                s0, s1, s2 = s0 + r * r, s1 + r * q, s2 + q * q
            m = modal_of(read_t(tt, old, 0, b), read_t(tt, new, 0, b))
            s3 = s3 + energy_of(m) * mo[x + 3, 0, rows]
        return s0, s1, s2, s3

    return lax.fori_loop(first, last, step, acc)


def clear_edges(zt, yg):
    zt[:, :, 24:32] = jnp.zeros((6, 2, 8, 128), jnp.float32)
    yg[:, :, 0:8] = jnp.zeros((6, 2, 8, 128), jnp.float32)


def inner_kernel(
    rx, dx, qk, fl, cl, mo, gf, dens_ref, qx, acc_ref, av, zt, tt, gp, yp, yg, *, sizes
):
    nx = sizes[0]
    clear_edges(zt, yg)
    density_planes(5, 17, nx, dx, qk, fl, av, mo, gf, dens_ref)
    operate_planes(5, 17, nx, rx, mo, cl, qx, zt, tt, gp, yp, yg)
    zero = jnp.zeros((8, 128), jnp.float32)
    for n, part in enumerate(sum_planes(3, 13, (zero, zero, zero, zero), rx, qx, mo, zt, tt)):
        acc_ref[n] = part


def outer_kernel(
    rx_in, dx_in, mo_in, gf_in, dens_in, qx_in, acc_ref, xlo_ref, xhi_ref, qk, fl, cl,
    rx, dx, mo, gf, dens_ref, qx, sum_ref, av, zt, tt, gp, yp, yg, *, sizes
):
    del rx_in, dx_in, mo_in, gf_in, dens_in, qx_in
    nx = sizes[0]
    clear_edges(zt, yg)
    x_halos(xlo_ref, xhi_ref, rx, dx)
    density_planes(0, 5, nx, dx, qk, fl, av, mo, gf, dens_ref)
    density_planes(17, 22, nx, dx, qk, fl, av, mo, gf, dens_ref)
    operate_planes(0, 6, nx, rx, mo, cl, qx, zt, tt, gp, yp, yg)
    operate_planes(16, 22, nx, rx, mo, cl, qx, zt, tt, gp, yp, yg)
    acc = tuple(acc_ref[n] for n in range(4))
    acc = sum_planes(0, 3, acc, rx, qx, mo, zt, tt)
    acc = sum_planes(13, 16, acc, rx, qx, mo, zt, tt)
    line = jnp.zeros((8, 128), jnp.float32)
    lane = lane_of((8, 128))
    for n, part in enumerate(acc):
        total = jnp.sum(jnp.sum(part, axis=0, keepdims=True), axis=1, keepdims=True)
        line = jnp.where(lane == n, total, line)
    for n in range(sum_ref.shape[0] // 8):
        sum_ref[8 * n : 8 * n + 8] = line


def cross_energy(m, o):
    total = None
    for first, second, pick in (
        (K["a"] - K["b"], K["b"], lambda c: mode(c)),
        (K["p"] - K["r"], K["r"], lambda c: mode(*{0, 1, 2} - {c})),
    ):
        vm, vo = [m[c, pick(c)] for c in range(3)], [o[c, pick(c)] for c in range(3)]
        sm, so = vm[0] + vm[1] + vm[2], vo[0] + vo[1] + vo[2]
        part = (vm[0] * vo[0] + vm[1] * vo[1] + vm[2] * vo[2]) * f32(first) + sm * so * f32(second)
        total = part if total is None else total + part
    shear = None
    for c, e2 in ((0, 1), (0, 2), (1, 2)):
        v = (m[c, mode(e2)] + m[e2, mode(c)]) * (o[c, mode(e2)] + o[e2, mode(c)])
        shear = v if shear is None else shear + v
    triple = None
    for c in range(3):
        v = m[c, (1, 1, 1)] * o[c, (1, 1, 1)]
        triple = v if triple is None else triple + v
    same = cross = None
    for e2 in range(3):
        c, d = [i for i in range(3) if i != e2]
        m1, m2 = m[c, mode(c, e2)], m[d, mode(d, e2)]
        o1, o2 = o[c, mode(c, e2)], o[d, mode(d, e2)]
        sq, cr = m1 * o1 + m2 * o2, m1 * o2 + m2 * o1
        same = sq if same is None else same + sq
        cross = cr if cross is None else cross + cr
    total = total + shear * f32(K["g"]) + triple * f32(K["h"])
    return total + same * f32(K["c"]) + cross * f32(K["d"])


def cones_kernel(rx, qx, gf, dens_in, out_ref, dens_ref, zt, tr, tq, px, av):
    lane = lane_of((WIN, 128))
    dens_ref[...] = dens_in[...]
    zt[:, :, 24:32] = jnp.zeros((6, 2, 8, 128), jnp.float32)

    def planes(i, slot):
        zy_plane(lambda c, t: rx[c, i + 1, t], zt, tr, slot, lane)
        zy_plane(lambda c, t: qx[c, i, t], zt, tq, slot, lane)

    planes(0, 0)

    def energy_step(i, _):
        new, old = (i + 1) & 1, i & 1
        planes(i + 1, new)
        for t in range(2):
            for b in range(3):
                rows = slice(8 * b, 8 * b + 8)
                m = modal_of(read_t(tr, old, t, b), read_t(tr, new, t, b))
                o = modal_of(read_t(tq, old, t, b), read_t(tq, new, t, b))
                g = gf[i + 1, t, rows]
                px[0, i, t, rows] = energy_of(m) * g
                px[1, i, t, rows] = cross_energy(m, o) * (2.0 * g)
                px[2, i, t, rows] = energy_of(o) * g
        return 0

    lax.fori_loop(0, 20, energy_step, 0)
    lane16 = lane_of((NYL, 128))

    def cone_step(x, _):
        for k in range(3):
            for t in range(2):
                f0 = px[k, x + 2, t]
                f1 = px[k, x + 1, t] + px[k, x + 3, t]
                f2 = px[k, x, t] + px[k, x + 4, t]
                for n, part in enumerate(x_parts(f0, f1, f2).values()):
                    av[n, t, 0:24] = part
            b = [cone_yz(av, t, (4, 20)) for t in range(2)]
            n1, p1 = z_next(b[0][1], b[1][1], lane16)[0], z_prev(b[0][1], b[1][1], lane16)[0]
            n2, p2 = z_next(b[0][2], b[1][2], lane16, 2)[0], z_prev(b[0][2], b[1][2], lane16, 2)[0]
            out_ref[k, x] = b[0][0] + (n1 + p1) + (n2 + p2)
        return 0

    lax.fori_loop(0, 16, cone_step, 0)


def final_kernel(sum_ref, rx, qx, cones, disp_ref, sens_ref):
    line = jnp.sum(sum_ref[...], axis=0, keepdims=True)
    lane1 = lane_of((1, 128))
    m0, m1, m2, m3 = [jnp.sum(jnp.where(lane1 == n, line, 0.0), axis=1, keepdims=True) for n in range(4)]
    m3 = m3 + spring_rate * m2
    first = m0 / m1
    norm = m0 - 2.0 * first * m1 + first * first * m2
    grown = 1.0 + norm / m0
    second = norm / (grown * grown * m1 - 2.0 * first * grown * m2 + first * first * m3)
    c0 = jnp.broadcast_to(first + second * grown, (NYL, 128))
    c1 = jnp.broadcast_to(-second * first, (NYL, 128))

    def step(x, _):
        for c in range(3):
            disp_ref[c, x] = c0 * rx[c, x + 3, 0, 4:20] + c1 * qx[c, x + 2, 0, 4:20]
        sens_ref[x] = c0 * (c0 * cones[0, x] + c1 * cones[1, x]) + c1 * c1 * cones[2, x]
        return 0

    lax.fori_loop(0, 16, step, 0)


def s(*shape):
    return jax.ShapeDtypeStruct(shape, jnp.float32)


def v(*shape):
    return pltpu.VMEM(shape, jnp.float32)


def call(kernel, outs, scratch, *args, smem=0, fetch=(), flush=(), **kw):
    spec_s, spec_v = pl.BlockSpec(memory_space=pltpu.SMEM), pl.BlockSpec(memory_space=pltpu.VMEM)
    single = not isinstance(outs, (tuple, list))
    outs = [outs] if single else list(outs)
    if not INTERPRET:
        outs = [o if i in flush else pltpu.VMEM(o.shape, o.dtype) for i, o in enumerate(outs)]
        args = [
            a if i < smem or i in fetch else pltpu.with_memory_space_constraint(a, pltpu.VMEM)
            for i, a in enumerate(args)
        ]
    return pl.pallas_call(
        kernel,
        out_shape=outs[0] if single else outs,
        in_specs=[spec_s] * smem + [spec_v] * (len(args) - smem),
        out_specs=spec_v if single else [spec_v] * len(outs),
        scratch_shapes=scratch,
        interpret=INTERPRET,
        compiler_params=pltpu.CompilerParams(vmem_limit_bytes=24 << 20),
        **kw,
    )(*args)


def moved(block, axis, step):
    count = lax.axis_size(axis)
    return lax.ppermute(block, axis, [(i, i - step) for i in range(count) if 0 <= i - step < count])


def body(load, design, solid_map):
    sizes = tuple(lax.axis_size(a) * n for a, n in zip(ALL, (NXL, NYL, NZL)))
    count = lax.axis_size("gx") * lax.axis_size("gy") * lax.axis_size("gz")

    def sized(kernel):
        return lambda *refs: kernel(*refs, sizes=sizes)

    zc = call(pack_z_kernel, s(8, 16, 128), [], load, design)
    zhi, zlo = moved(zc, "gz", 1), moved(zc, "gz", -1)
    qk, fl, cl = call(
        sized(place_kernel), (s(6, 2, 24, 128), s(3, 2, 24, 128), s(2, 24, 128)), [], solid_map, smem=1
    )
    ylo_s, yhi_s = call(pack_y_kernel, (s(39, 8, 128), s(39, 8, 128)), [], load, design, zhi, zlo)
    yhi, ylo = moved(ylo_s, "gy", 1), moved(yhi_s, "gy", -1)
    rx_t, dx_t = s(3, 23, 2, 24, 128), s(26, 2, 32, 128)
    mo_t, dens_t, qx_t = s(22, 2, 24, 128), s(16, 16, 128), s(3, 21, 2, 24, 128)
    rx, dx, xlo_s, xhi_s = call(
        pack_x_kernel, (rx_t, dx_t, s(544, 128), s(472, 128)), [v(8, 32, 128)],
        load, design, zhi, zlo, ylo, yhi,
    )
    xhi, xlo = moved(xlo_s, "gx", 1), moved(xhi_s, "gx", -1)
    scratch = [
        v(6, 2, 32, 128), v(6, 2, 32, 128), v(2, 12, 2, 24, 128), v(12, 2, 24, 128), v(6, 2, 24, 128), v(6, 2, 32, 128),
    ]
    mo, gf, dens, qx, acc = call(
        sized(inner_kernel), (mo_t, mo_t, dens_t, qx_t, s(4, 8, 128)), scratch, rx, dx, qk, fl, cl
    )
    rx, dx, mo, gf, dens, qx, part = call(
        sized(outer_kernel), (rx_t, dx_t, mo_t, mo_t, dens_t, qx_t, s(count, 128)), scratch,
        rx, dx, mo, gf, dens, qx, acc, xlo, xhi, qk, fl, cl,
        flush=(6,), input_output_aliases={n: n for n in range(6)},
    )
    sums = lax.all_to_all(part, ALL, 0, 0, tiled=True)
    cones, dens = call(
        cones_kernel, (s(3, 16, 16, 128), dens_t),
        [v(6, 2, 32, 128), v(2, 12, 2, 24, 128), v(2, 12, 2, 24, 128), v(3, 20, 2, 24, 128), v(6, 2, 32, 128)],
        rx, qx, gf, dens, flush=(1,),
    )
    disp, sens = call(
        final_kernel, (s(3, 16, 16, 128), s(16, 16, 128)), [], sums, rx, qx, cones, flush=(0, 1)
    )
    return disp, sens, dens


def solution(mesh):
    nodal, cell = P(None, "gx", "gy", "gz"), P("gx", "gy", "gz")
    return jax.shard_map(
        body, mesh=mesh, in_specs=(nodal, cell, P()), out_specs=(nodal, cell, cell), check_vma=False
    )
```

```python
import math

import jax
import jax.numpy as jnp
import numpy as np
from jax import lax
from jax.experimental import pallas as pl
from jax.experimental.pallas import tpu as pltpu
from jax.sharding import PartitionSpec as P


BRICK = 16
young_floor = 0.001
spring_rate = 0.05
sharpness = 8.0
threshold = 0.5
poisson = 0.3
ALL = ("gx", "gy", "gz")
INTERPRET = False

NXL, NYL, NZL = 16, 16, 128
WIN = 24


def element_matrix():
    lame_first = poisson / ((1.0 + poisson) * (1.0 - 2.0 * poisson))
    shear_mod = 1.0 / (2.0 * (1.0 + poisson))
    elastic = np.zeros((6, 6))
    elastic[:3, :3] = lame_first
    for axis_one in range(3):
        elastic[axis_one, axis_one] += 2.0 * shear_mod
        elastic[axis_one + 3, axis_one + 3] = shear_mod
    gauss_point = 1.0 / math.sqrt(3.0)
    stiffness = np.zeros((24, 24))
    for point_x in (-gauss_point, gauss_point):
        for point_y in (-gauss_point, gauss_point):
            for point_z in (-gauss_point, gauss_point):
                strain = np.zeros((6, 24))
                for corner in range(8):
                    sign_a = 2 * (corner // 4) - 1
                    sign_b = 2 * (corner // 2 % 2) - 1
                    sign_c = 2 * (corner % 2) - 1
                    along_x = 0.25 * sign_a * (1 + sign_b * point_y) * (1 + sign_c * point_z)
                    along_y = 0.25 * (1 + sign_a * point_x) * sign_b * (1 + sign_c * point_z)
                    along_z = 0.25 * (1 + sign_a * point_x) * (1 + sign_b * point_y) * sign_c
                    column = 3 * corner
                    strain[0, column] = along_x
                    strain[1, column + 1] = along_y
                    strain[2, column + 2] = along_z
                    strain[3, column + 1] = along_z
                    strain[3, column + 2] = along_y
                    strain[4, column] = along_z
                    strain[4, column + 2] = along_x
                    strain[5, column] = along_y
                    strain[5, column + 1] = along_x
                stiffness += strain.T @ elastic @ strain * 0.125
    return stiffness


def modal_constants():
    modes = [(px, py, pz) for px in (0, 1) for py in (0, 1) for pz in (0, 1)]
    change = np.zeros((24, 24))
    for c in range(3):
        for m, mode in enumerate(modes):
            for q in range(8):
                corner = (q // 4, q // 2 % 2, q % 2)
                sign = 1.0
                for axis in range(3):
                    if mode[axis] and not corner[axis]:
                        sign = -sign
                change[8 * c + m, 3 * q + c] = sign
    hat = change @ element_matrix() @ change.T / 64.0

    def at(c1, m1, c2, m2):
        return hat[8 * c1 + modes.index(m1), 8 * c2 + modes.index(m2)]

    k = {
        "a": at(0, (1, 0, 0), 0, (1, 0, 0)),
        "b": at(0, (1, 0, 0), 1, (0, 1, 0)),
        "p": at(0, (0, 1, 1), 0, (0, 1, 1)),
        "r": at(0, (0, 1, 1), 1, (1, 0, 1)),
        "g": at(0, (0, 1, 0), 1, (1, 0, 0)),
        "h": at(2, (1, 1, 1), 2, (1, 1, 1)),
        "c": at(1, (1, 1, 0), 1, (1, 1, 0)),
        "d": at(1, (1, 1, 0), 2, (1, 0, 1)),
    }
    made = np.zeros((24, 24))

    def put(c1, m1, c2, m2, v):
        made[8 * c1 + modes.index(m1), 8 * c2 + modes.index(m2)] += v

    for c in range(3):
        unit = tuple(int(i == c) for i in range(3))
        anti = tuple(int(i != c) for i in range(3))
        put(c, (1, 1, 1), c, (1, 1, 1), k["h"])
        for e in range(3):
            unit_e = tuple(int(i == e) for i in range(3))
            anti_e = tuple(int(i != e) for i in range(3))
            put(c, unit, e, unit_e, k["a"] if c == e else k["b"])
            put(c, anti, e, anti_e, k["p"] if c == e else k["r"])
            if c != e:
                put(c, unit_e, c, unit_e, k["g"])
                put(c, unit_e, e, unit, k["g"])
                both = tuple(int(i in (c, e)) for i in range(3))
                o = 3 - c - e
                both_o = tuple(int(i in (o, e)) for i in range(3))
                put(c, both, c, both, k["c"])
                put(c, both, o, both_o, k["d"])
    assert np.abs(made - hat).max() < 1e-12
    return k


K = modal_constants()
W = {n: 3.0 - math.sqrt(n) for n in range(9)}
KS = (0, 1, 2, 4, 5, 8)


def mode(*axes):
    return tuple(int(i in axes) for i in range(3))


def f32(x):
    return float(np.float32(x))


def roll(x, shift):
    shift = shift % 128
    return x if shift == 0 else pltpu.roll(x, shift, 1)


def lane_of(shape):
    return lax.broadcasted_iota(jnp.int32, shape, 1)


def z_next(a0, a1, lane, by=1):
    r0, r1 = roll(a0, -by), roll(a1, -by)
    edge = lane >= 128 - by
    return jnp.where(edge, r1, r0), jnp.where(edge, r0, r1)


def z_prev(a0, a1, lane, by=1):
    r0, r1 = roll(a0, by), roll(a1, by)
    edge = lane < by
    return jnp.where(edge, r1, r0), jnp.where(edge, r0, r1)


def modal_of(lo, hi):
    m = {}
    for (c, py, pz), low in lo.items():
        high = hi[c, py, pz]
        if py or pz:
            m[c, (0, py, pz)] = low + high
        m[c, (1, py, pz)] = high - low
    return m


def forces_of(m, e):
    ea, eb = e * f32(K["a"] - K["b"]), e * f32(K["b"])
    ep, er = e * f32(K["p"] - K["r"]), e * f32(K["r"])
    eg, eh = e * f32(K["g"]), e * f32(K["h"])
    ec, ed = e * f32(K["c"]), e * f32(K["d"])
    f = {}
    for first, second, pick in ((ea, eb, lambda c: mode(c)), (ep, er, lambda c: mode(*{0, 1, 2} - {c}))):
        vals = [m[c, pick(c)] for c in range(3)]
        shared = (vals[0] + vals[1] + vals[2]) * second
        for c in range(3):
            f[c, pick(c)] = vals[c] * first + shared
    for c, e2 in ((0, 1), (0, 2), (1, 2)):
        shared = (m[c, mode(e2)] + m[e2, mode(c)]) * eg
        f[c, mode(e2)] = shared
        f[e2, mode(c)] = shared
    for c in range(3):
        f[c, (1, 1, 1)] = m[c, (1, 1, 1)] * eh
    for e2 in range(3):
        c, o = [i for i in range(3) if i != e2]
        v1, v2 = m[c, mode(c, e2)], m[o, mode(o, e2)]
        f[c, mode(c, e2)] = v1 * ec + v2 * ed
        f[o, mode(o, e2)] = v2 * ec + v1 * ed
    return f


def energy_of(m):
    total = None
    for first, second, pick in (
        (K["a"] - K["b"], K["b"], lambda c: mode(c)),
        (K["p"] - K["r"], K["r"], lambda c: mode(*{0, 1, 2} - {c})),
    ):
        vals = [m[c, pick(c)] for c in range(3)]
        s = vals[0] + vals[1] + vals[2]
        part = (vals[0] * vals[0] + vals[1] * vals[1] + vals[2] * vals[2]) * f32(first) + s * s * f32(second)
        total = part if total is None else total + part
    shear = None
    for c, e2 in ((0, 1), (0, 2), (1, 2)):
        s = m[c, mode(e2)] + m[e2, mode(c)]
        shear = s * s if shear is None else shear + s * s
    total = total + shear * f32(K["g"])
    triple = None
    for c in range(3):
        v = m[c, (1, 1, 1)]
        triple = v * v if triple is None else triple + v * v
    total = total + triple * f32(K["h"])
    squares = cross = None
    for e2 in range(3):
        c, o = [i for i in range(3) if i != e2]
        v1, v2 = m[c, mode(c, e2)], m[o, mode(o, e2)]
        sq, cr = v1 * v1 + v2 * v2, v1 * v2
        squares = sq if squares is None else squares + sq
        cross = cr if cross is None else cross + cr
    return total + squares * f32(K["c"]) + cross * f32(2.0 * K["d"])


def x_parts(f0, f1, f2):
    out = {}
    for k in KS:
        v = f0 * f32(W[k])
        if k + 1 in W:
            v = v + f1 * f32(W[k + 1])
        if k + 4 in W:
            v = v + f2 * f32(W[k + 4])
        out[k] = v
    return out


def pack_z_kernel(load_hbm, design_hbm, load_ref, design_ref, out_ref, sems):
    copies = [pltpu.make_async_copy(load_hbm.at[c], load_ref.at[c], sems.at[c]) for c in range(3)]
    copies.append(pltpu.make_async_copy(design_hbm, design_ref, sems.at[3]))
    for one in copies:
        one.start()
    for one in copies:
        one.wait()
    lane = lane_of((NYL, 128))

    def step(pair, _):
        acc = jnp.zeros((NYL, 128), jnp.float32)
        for par in range(2):
            for fld in range(4):
                off = 64 * par + 16 * fld
                src = load_ref[fld, 2 * pair + par] if fld < 3 else design_ref[2 * pair + par]
                acc = jnp.where(((lane - off + 8) & 127) < 16, roll(src, off), acc)
        out_ref[pair] = acc
        return 0

    lax.fori_loop(0, 8, step, 0)


def halo_merge(high, low):
    lane = lane_of(high.shape)
    return jnp.where((lane & 15) < 8, high, low)


def pack_y_kernel(load_ref, design_ref, zhi_ref, zlo_ref, place_ref, lo_ref, hi_ref):
    del place_ref
    for dst, quad, one in ((lo_ref, 0, 4), (hi_ref, 12, 11)):
        rows = slice(quad, quad + 4)
        for x in range(16):
            dst[x, 0:4] = load_ref[0, x, rows]
            dst[x, 4:8] = load_ref[1, x, rows]
            dst[16 + x, 0:4] = load_ref[2, x, rows]
            dst[16 + x, 4:8] = design_ref[x, rows]
            dst[32 + x // 8, x % 8 : x % 8 + 1] = design_ref[x, one : one + 1]
        for k in range(8):
            dst[35 + k // 2, 4 * (k % 2) : 4 * (k % 2) + 4] = halo_merge(zhi_ref[k, rows], zlo_ref[k, rows])
            dst[34, k : k + 1] = halo_merge(zhi_ref[k, one : one + 1], zlo_ref[k, one : one + 1])


def pack_x_kernel(load_ref, design_ref, zhi_ref, zlo_ref, ylo_ref, yhi_ref, rx, dx, lo_ref, hi_ref, hx):
    none = jnp.zeros((8, 128), jnp.float32)
    for k in range(8):
        half = slice(4 * (k % 2), 4 * (k % 2) + 4)
        hx[k, 0:8] = none
        hx[k, 24:32] = none
        hx[k, 3:4] = ylo_ref[34, k : k + 1]
        hx[k, 4:8] = ylo_ref[35 + k // 2, half]
        hx[k, 8:24] = halo_merge(zhi_ref[k], zlo_ref[k])
        hx[k, 24:28] = yhi_ref[35 + k // 2, half]
        hx[k, 28:29] = yhi_ref[34, k : k + 1]
    for x in range(16):
        for c in range(3):
            tile, half = (x, slice(4 * c, 4 * c + 4)) if c < 2 else (16 + x, slice(0, 4))
            rx[c, x + 3, 0, 0:4] = ylo_ref[tile, half]
            rx[c, x + 3, 0, 4:20] = load_ref[c, x]
            rx[c, x + 3, 0, 20:24] = yhi_ref[tile, half]
        one = slice(x % 8, x % 8 + 1)
        dx[x + 5, 0, 0:8] = none
        dx[x + 5, 0, 24:32] = none
        dx[x + 5, 0, 3:4] = ylo_ref[32 + x // 8, one]
        dx[x + 5, 0, 4:8] = ylo_ref[16 + x, 4:8]
        dx[x + 5, 0, 8:24] = design_ref[x]
        dx[x + 5, 0, 24:28] = yhi_ref[16 + x, 4:8]
        dx[x + 5, 0, 28:29] = yhi_ref[32 + x // 8, one]
    for i in range(5):
        lo_ref[288 + 32 * i : 320 + 32 * i] = dx[5 + i, 0]
        hi_ref[216 + 32 * i : 248 + 32 * i] = dx[16 + i, 0]
    for i in range(3):
        lo_ref[448 + 32 * i : 480 + 32 * i] = hx[i]
        hi_ref[376 + 32 * i : 408 + 32 * i] = hx[5 + i]
    for c in range(3):
        for i in range(4):
            lo_ref[24 * (4 * c + i) : 24 * (4 * c + i) + 24] = rx[c, 3 + i, 0]
        for i in range(3):
            hi_ref[24 * (3 * c + i) : 24 * (3 * c + i) + 24] = rx[c, 16 + i, 0]
    for k in range(8):
        spread_pair(hx[k], 2 * k, (2 * k, 2 * k + 1), rx, dx, True)


def spread_pair(tile, x, wanted, rx, dx, both):
    for par in range(2):
        if x + par in wanted:
            dx[x + par + 5, 1] = roll(tile, -(64 * par + 48))
            if both or -3 <= x + par <= 19:
                for c in range(3):
                    rx[c, x + par + 3, 1] = roll(tile, -(64 * par + 16 * c))[4:28]


def x_halos(xlo_ref, xhi_ref, rx, dx):
    for c in range(3):
        for i in range(4):
            rx[c, 19 + i, 0] = xhi_ref[24 * (4 * c + i) : 24 * (4 * c + i) + 24]
        for i in range(3):
            rx[c, i, 0] = xlo_ref[24 * (3 * c + i) : 24 * (3 * c + i) + 24]
    for i in range(5):
        dx[21 + i, 0] = xhi_ref[288 + 32 * i : 320 + 32 * i]
        dx[i, 0] = xlo_ref[216 + 32 * i : 248 + 32 * i]
    for i in range(3):
        spread_pair(xhi_ref[448 + 32 * i : 480 + 32 * i], 16 + 2 * i, range(16, 21), rx, dx, False)
        spread_pair(xlo_ref[376 + 32 * i : 408 + 32 * i], -6 + 2 * i, range(-5, 0), rx, dx, False)


def place_kernel(map_ref, order_ref, qk, fl, cl, *, sizes):
    del order_ref
    nx, ny, nz = sizes
    i_x, i_y, i_z = (lax.axis_index(a) for a in ALL)
    lane = lane_of((WIN, 128))
    row = lax.broadcasted_iota(jnp.int32, (WIN, 128), 0)
    y_at = i_y * NYL + row - 4
    z_at = [i_z * NZL + lane, i_z * NZL + jnp.where(lane < 64, lane + 128, lane - 128)]

    def inside(at, step, length):
        return jnp.where((at + step >= 0) & (at + step < length), 1.0, 0.0)

    y_in = [inside(y_at, 0, ny)] + [inside(y_at, s, ny) + inside(y_at, -s, ny) for s in (1, 2)]
    for t in range(2):
        z_in = [inside(z_at[t], 0, nz)] + [inside(z_at[t], s, nz) + inside(z_at[t], -s, nz) for s in (1, 2)]
        qk[0, t] = y_in[0] * z_in[0]
        qk[1, t] = y_in[1] * z_in[0] + y_in[0] * z_in[1]
        qk[2, t] = y_in[1] * z_in[1]
        qk[3, t] = y_in[2] * z_in[0] + y_in[0] * z_in[2]
        qk[4, t] = y_in[1] * z_in[2] + y_in[2] * z_in[1]
        qk[5, t] = y_in[2] * z_in[2]
        cl[t] = y_in[0] * z_in[0]
    gbx, gby, gbz = nx // BRICK, ny // BRICK, nz // BRICK
    bricks = NZL // BRICK

    def flag_at(bx, by, bz):
        ok = (bx >= 0) & (bx < gbx) & (by >= 0) & (by < gby) & (bz >= 0) & (bz < gbz)
        value = map_ref[jnp.clip(bx, 0, gbx - 1), jnp.clip(by, 0, gby - 1), jnp.clip(bz, 0, gbz - 1)]
        return jnp.where(ok, value, 0).astype(jnp.float32)

    for xc in range(3):
        lines = []
        for yc in range(3):
            flag = [flag_at(i_x + xc - 1, i_y + yc - 1, i_z * bricks + n - 1) for n in range(bricks + 2)]
            main = jnp.zeros((WIN, 128), jnp.float32)
            for n in range(bricks):
                main = jnp.where((lane >> 4) == n, flag[n + 1], main)
            lines.append((main, jnp.where(lane < 64, flag[bricks + 1], flag[0])))
        for t in range(2):
            fl[xc, t] = jnp.where(row < 4, lines[0][t], jnp.where(row < 20, lines[1][t], lines[2][t]))


def zy_plane(tile, zt, t_ref, slot, lane, tiles=2, base=0, blocks=3):
    for c in range(3):
        a0, a1 = tile(c, 0), tile(c, 1)
        n0, n1 = z_next(a0, a1, lane)
        zt[2 * c, 0, 0:24] = a0 + n0
        zt[2 * c + 1, 0, 0:24] = n0 - a0
        if tiles == 2:
            zt[2 * c, 1, 0:24] = a1 + n1
            zt[2 * c + 1, 1, 0:24] = n1 - a1
    for f in range(6):
        for t in range(tiles):
            for b in range(blocks):
                r = base + 8 * b
                lo, hi = zt[f, t, r : r + 8], zt[f, t, r + 1 : r + 9]
                t_ref[slot, 2 * f, t, 8 * b : 8 * b + 8] = lo + hi
                t_ref[slot, 2 * f + 1, t, 8 * b : 8 * b + 8] = hi - lo


def read_t(t_ref, slot, t, b):
    out = {}
    for c in range(3):
        for pz in range(2):
            for py in range(2):
                out[c, py, pz] = t_ref[slot, 4 * c + 2 * pz + py, t, 8 * b : 8 * b + 8]
    return out


LIFT = math.tanh(sharpness * threshold)
SCALE = LIFT + math.tanh(sharpness * (1.0 - threshold))


def cone_yz(av, t, rows):
    lo, hi = rows

    def at(n, step):
        return av[n, t, lo + step : hi + step]

    def both(n, step):
        return at(n, -step) + at(n, step)

    return [
        at(0, 0) + both(1, 1) + both(3, 2),
        at(1, 0) + both(2, 1) + both(4, 2),
        at(3, 0) + both(4, 1) + both(5, 2),
    ]


def density_planes(first, last, nx, dx, qk, fl, av, mo, gf, dens_ref):
    lane = lane_of((WIN, 128))
    i_x = lax.axis_index("gx")

    def scalar_inside(at, step):
        return jnp.where((at + step >= 0) & (at + step < nx), 1.0, 0.0)

    def step(e, _):
        for t in range(2):
            f0 = dx[e + 2, t]
            f1 = dx[e + 1, t] + dx[e + 3, t]
            f2 = dx[e, t] + dx[e + 4, t]
            for n, part in enumerate(x_parts(f0, f1, f2).values()):
                av[n, t] = part
        x_at = i_x * NXL + e - 3
        x0 = scalar_inside(x_at, 0)
        x1 = scalar_inside(x_at, 1) + scalar_inside(x_at, -1)
        x2 = scalar_inside(x_at, 2) + scalar_inside(x_at, -2)
        cls = jnp.where(e < 3, 0, jnp.where(e < 19, 1, 2))
        b = [cone_yz(av, t, (4, 28)) for t in range(2)]
        n1, p1 = z_next(b[0][1], b[1][1], lane), z_prev(b[0][1], b[1][1], lane)
        n2, p2 = z_next(b[0][2], b[1][2], lane, 2), z_prev(b[0][2], b[1][2], lane, 2)
        weights = x_parts(x0, x1, x2)
        for t in range(2):
            cone = b[t][0] + (n1[t] + p1[t]) + (n2[t] + p2[t])
            ws = None
            for n, wk in enumerate(weights.values()):
                ws = qk[n, t] * wk if ws is None else ws + qk[n, t] * wk
            inv = 1.0 / jnp.maximum(ws, 1.0)
            th = jnp.tanh(sharpness * (cone * inv - threshold))
            dens = (LIFT + th) * f32(1.0 / SCALE)
            flag = fl[cls, t]
            sq = dens * dens
            mo[e, t] = (young_floor + sq * dens * (1.0 - young_floor)) * flag
            gf[e, t] = sq * flag * (1.0 - th * th) * inv * f32(-3.0 * (1.0 - young_floor) * sharpness / SCALE)
            if t == 0:
                av[0, 0, 0:24] = dens

        @pl.when((e >= 3) & (e < 19))
        def _():
            dens_ref[e - 3] = av[0, 0, 4:20]

        return 0

    lax.fori_loop(first, last, step, 0)


def operate_planes(first, last, nx, rx, mo, cl, qx, zt, tt, gp, yp, yg):
    lane = lane_of((WIN, 128))
    i_x = lax.axis_index("gx")
    gp[...] = jnp.zeros((12, 2, 24, 128), jnp.float32)
    zy_plane(lambda c, t: rx[c, first, t], zt, tt, first & 1, lane)

    def step(e, _):
        new, old = (e + 1) & 1, e & 1
        zy_plane(lambda c, t: rx[c, e + 1, t], zt, tt, new, lane)
        for t in range(2):
            for b in range(3):
                rows = slice(8 * b, 8 * b + 8)
                force = forces_of(modal_of(read_t(tt, old, t, b), read_t(tt, new, t, b)), mo[e, t, rows])
                for c in range(3):
                    for pz in range(2):
                        n = []
                        for py in range(2):
                            fd = force[c, (1, py, pz)]
                            fs = force.get((c, (0, py, pz)))
                            at = 4 * c + 2 * pz + py
                            before = gp[at, t, rows]
                            if fs is None:
                                gp[at, t, rows] = fd
                                n.append(before - fd)
                            else:
                                gp[at, t, rows] = fs + fd
                                n.append((fs - fd) + before)
                        yp[2 * c + pz, t, rows] = n[0] - n[1]
                        yg[2 * c + pz, t, 8 + 8 * b : 16 + 8 * b] = n[0] + n[1]

        @pl.when(e > first)
        def _():
            x_on = jnp.where(i_x * NXL + e - 3 < nx, 1.0, 0.0)
            for c in range(3):
                p, g = [], []
                for t in range(2):
                    zs = yp[2 * c, t] + yg[2 * c, t, 7:31]
                    zd = yp[2 * c + 1, t] + yg[2 * c + 1, t, 7:31]
                    p.append(zs - zd)
                    g.append(zs + zd)
                gb = z_prev(g[0], g[1], lane)
                for t in range(2):
                    value = p[t] + gb[t] + rx[c, e, t] * spring_rate
                    qx[c, e - 1, t] = value * (cl[t] * x_on)

        return 0

    lax.fori_loop(first, last, step, 0)


def clear_edges(zt, yg):
    zt[:, :, 24:32] = jnp.zeros((6, 2, 8, 128), jnp.float32)
    yg[:, :, 0:8] = jnp.zeros((6, 2, 8, 128), jnp.float32)


def inner_kernel(rx, dx, qk, fl, cl, mo, gf, dens_ref, qx, av, zt, tt, gp, yp, yg, *, sizes):
    nx = sizes[0]
    clear_edges(zt, yg)
    density_planes(5, 17, nx, dx, qk, fl, av, mo, gf, dens_ref)
    operate_planes(5, 17, nx, rx, mo, cl, qx, zt, tt, gp, yp, yg)


def outer_kernel(
    rx_in, dx_in, mo_in, gf_in, dens_in, qx_in, xlo_ref, xhi_ref, qk, fl, cl,
    rx, dx, mo, gf, dens_ref, qx, px, own_ref, sum_ref, av, zt, tt, tq, gp, yp, yg, *, sizes
):
    del rx_in, dx_in, mo_in, gf_in, dens_in, qx_in
    nx = sizes[0]
    clear_edges(zt, yg)
    x_halos(xlo_ref, xhi_ref, rx, dx)
    density_planes(0, 5, nx, dx, qk, fl, av, mo, gf, dens_ref)
    density_planes(17, 22, nx, dx, qk, fl, av, mo, gf, dens_ref)
    operate_planes(0, 6, nx, rx, mo, cl, qx, zt, tt, gp, yp, yg)
    operate_planes(16, 22, nx, rx, mo, cl, qx, zt, tt, gp, yp, yg)
    line = jnp.zeros((8, 128), jnp.float32)
    lane = lane_of((8, 128))
    for n, part in enumerate(energy_planes(rx, qx, mo, gf, px, zt, tt, tq)):
        total = jnp.sum(jnp.sum(part, axis=0, keepdims=True), axis=1, keepdims=True)
        line = jnp.where(lane == n, total, line)
    for n in range(sum_ref.shape[0] // 8):
        sum_ref[8 * n : 8 * n + 8] = line
    for c in range(3):
        for x in range(16):
            own_ref[c, x] = qx[c, x + 2, 0, 4:20]


def cross_energy(m, o):
    total = None
    for first, second, pick in (
        (K["a"] - K["b"], K["b"], lambda c: mode(c)),
        (K["p"] - K["r"], K["r"], lambda c: mode(*{0, 1, 2} - {c})),
    ):
        vm, vo = [m[c, pick(c)] for c in range(3)], [o[c, pick(c)] for c in range(3)]
        sm, so = vm[0] + vm[1] + vm[2], vo[0] + vo[1] + vo[2]
        part = (vm[0] * vo[0] + vm[1] * vo[1] + vm[2] * vo[2]) * f32(first) + sm * so * f32(second)
        total = part if total is None else total + part
    shear = None
    for c, e2 in ((0, 1), (0, 2), (1, 2)):
        v = (m[c, mode(e2)] + m[e2, mode(c)]) * (o[c, mode(e2)] + o[e2, mode(c)])
        shear = v if shear is None else shear + v
    triple = None
    for c in range(3):
        v = m[c, (1, 1, 1)] * o[c, (1, 1, 1)]
        triple = v if triple is None else triple + v
    same = cross = None
    for e2 in range(3):
        c, d = [i for i in range(3) if i != e2]
        m1, m2 = m[c, mode(c, e2)], m[d, mode(d, e2)]
        o1, o2 = o[c, mode(c, e2)], o[d, mode(d, e2)]
        sq, cr = m1 * o1 + m2 * o2, m1 * o2 + m2 * o1
        same = sq if same is None else same + sq
        cross = cr if cross is None else cross + cr
    total = total + shear * f32(K["g"]) + triple * f32(K["h"])
    return total + same * f32(K["c"]) + cross * f32(K["d"])


def energy_planes(rx, qx, mo, gf, px, zt, tr, tq):
    lane = lane_of((WIN, 128))
    row = lax.broadcasted_iota(jnp.int32, (8, 128), 0)

    def planes(i, slot):
        zy_plane(lambda c, t: rx[c, i + 1, t], zt, tr, slot, lane)
        zy_plane(lambda c, t: qx[c, i, t], zt, tq, slot, lane)

    planes(0, 0)
    zero = jnp.zeros((8, 128), jnp.float32)

    def energy_step(i, acc):
        s0, s1, s2, s3 = acc
        new, old = (i + 1) & 1, i & 1
        planes(i + 1, new)
        mine = jnp.where((i >= 2) & (i < 18), 1.0, 0.0)
        for b in range(2):
            rows = slice(4 + 8 * b, 12 + 8 * b)
            for c in range(3):
                r, q = rx[c, i + 1, 0, rows], qx[c, i, 0, rows]
                rm, qm = r * mine, q * mine
                s0, s1, s2 = s0 + rm * r, s1 + rm * q, s2 + qm * q
        for t in range(2):
            for b in range(3):
                rows = slice(8 * b, 8 * b + 8)
                m = modal_of(read_t(tr, old, t, b), read_t(tr, new, t, b))
                o = modal_of(read_t(tq, old, t, b), read_t(tq, new, t, b))
                g = gf[i + 1, t, rows]
                px[0, i, t, rows] = energy_of(m) * g
                px[1, i, t, rows] = cross_energy(m, o) * (2.0 * g)
                e11 = energy_of(o)
                px[2, i, t, rows] = e11 * g
                if t == 0:
                    part = e11 * (mo[i + 1, 0, rows] * mine)
                    if b == 0:
                        part = jnp.where(row >= 4, part, 0.0)
                    if b == 2:
                        part = jnp.where(row < 4, part, 0.0)
                    s3 = s3 + part
        return s0, s1, s2, s3

    return lax.fori_loop(0, 20, energy_step, (zero, zero, zero, zero))


def cones_kernel(px, dens_in, out_ref, dens_ref, av):
    dens_ref[...] = dens_in[...]
    lane16 = lane_of((NYL, 128))

    def cone_step(x, _):
        for k in range(3):
            for t in range(2):
                f0 = px[k, x + 2, t]
                f1 = px[k, x + 1, t] + px[k, x + 3, t]
                f2 = px[k, x, t] + px[k, x + 4, t]
                for n, part in enumerate(x_parts(f0, f1, f2).values()):
                    av[k, n, t, 0:24] = part
            b = [cone_yz(av.at[k], t, (4, 20)) for t in range(2)]
            n1, p1 = z_next(b[0][1], b[1][1], lane16)[0], z_prev(b[0][1], b[1][1], lane16)[0]
            n2, p2 = z_next(b[0][2], b[1][2], lane16, 2)[0], z_prev(b[0][2], b[1][2], lane16, 2)[0]
            out_ref[k, x] = b[0][0] + (n1 + p1) + (n2 + p2)
        return 0

    lax.fori_loop(0, 16, cone_step, 0)


def final_kernel(sum_ref, load_ref, own_ref, cones, disp_ref, sens_ref):
    line = jnp.sum(sum_ref[...], axis=0, keepdims=True)
    lane1 = lane_of((1, 128))
    m0, m1, m2, m3 = [jnp.sum(jnp.where(lane1 == n, line, 0.0), axis=1, keepdims=True) for n in range(4)]
    m3 = m3 + spring_rate * m2
    first = m0 / m1
    norm = m0 - 2.0 * first * m1 + first * first * m2
    grown = 1.0 + norm / m0
    second = norm / (grown * grown * m1 - 2.0 * first * grown * m2 + first * first * m3)
    c0 = jnp.broadcast_to(first + second * grown, (NYL, 128))
    c1 = jnp.broadcast_to(-second * first, (NYL, 128))

    def step(x, _):
        for c in range(3):
            disp_ref[c, x] = c0 * load_ref[c, x] + c1 * own_ref[c, x]
        sens_ref[x] = c0 * (c0 * cones[0, x] + c1 * cones[1, x]) + c1 * c1 * cones[2, x]
        return 0

    lax.fori_loop(0, 16, step, 0)


def s(*shape):
    return jax.ShapeDtypeStruct(shape, jnp.float32)


def v(*shape):
    return pltpu.VMEM(shape, jnp.float32)


def call(kernel, outs, scratch, *args, smem=0, hbm=0, flush=(), **kw):
    spec_s, spec_v = pl.BlockSpec(memory_space=pltpu.SMEM), pl.BlockSpec(memory_space=pltpu.VMEM)
    single = not isinstance(outs, (tuple, list))
    outs = [outs] if single else list(outs)
    if not INTERPRET:
        outs = [o if i in flush else pltpu.VMEM(o.shape, o.dtype) for i, o in enumerate(outs)]
        args = [
            a if i < smem else pltpu.with_memory_space_constraint(a, pltpu.HBM if i < smem + hbm else pltpu.VMEM)
            for i, a in enumerate(args)
        ]
    return pl.pallas_call(
        kernel,
        out_shape=outs[0] if single else outs,
        in_specs=[spec_s] * smem
        + [pl.BlockSpec(memory_space=pltpu.HBM)] * hbm
        + [spec_v] * (len(args) - smem - hbm),
        out_specs=spec_v if single else [spec_v] * len(outs),
        scratch_shapes=scratch,
        interpret=INTERPRET,
        compiler_params=pltpu.CompilerParams(vmem_limit_bytes=24 << 20),
        **kw,
    )(*args)


def moved(block, axis, step):
    count = lax.axis_size(axis)
    return lax.ppermute(block, axis, [(i, i - step) for i in range(count) if 0 <= i - step < count])


def body(load, design, solid_map):
    sizes = tuple(lax.axis_size(a) * n for a, n in zip(ALL, (NXL, NYL, NZL)))
    count = lax.axis_size("gx") * lax.axis_size("gy") * lax.axis_size("gz")

    def sized(kernel):
        return lambda *refs: kernel(*refs, sizes=sizes)

    load, design, zc = call(
        pack_z_kernel, (s(3, 16, 16, 128), s(16, 16, 128), s(8, 16, 128)), [pltpu.SemaphoreType.DMA((4,))],
        load, design, hbm=2,
    )
    zhi, zlo = moved(zc, "gz", 1), moved(zc, "gz", -1)
    qk, fl, cl = call(
        sized(place_kernel), (s(6, 2, 24, 128), s(3, 2, 24, 128), s(2, 24, 128)), [], solid_map, zc, smem=1
    )
    ylo_s, yhi_s = call(pack_y_kernel, (s(39, 8, 128), s(39, 8, 128)), [], load, design, zhi, zlo, cl)
    yhi, ylo = moved(ylo_s, "gy", 1), moved(yhi_s, "gy", -1)
    rx_t, dx_t = s(3, 23, 2, 24, 128), s(26, 2, 32, 128)
    mo_t, dens_t, qx_t = s(22, 2, 24, 128), s(16, 16, 128), s(3, 21, 2, 24, 128)
    rx, dx, xlo_s, xhi_s = call(
        pack_x_kernel, (rx_t, dx_t, s(544, 128), s(472, 128)), [v(8, 32, 128)],
        load, design, zhi, zlo, ylo, yhi,
    )
    xhi, xlo = moved(xlo_s, "gx", 1), moved(xhi_s, "gx", -1)
    scratch = [
        v(6, 2, 32, 128), v(6, 2, 32, 128), v(2, 12, 2, 24, 128), v(12, 2, 24, 128), v(6, 2, 24, 128), v(6, 2, 32, 128),
    ]
    mo, gf, dens, qx = call(sized(inner_kernel), (mo_t, mo_t, dens_t, qx_t), scratch, rx, dx, qk, fl, cl)
    scratch.insert(2, scratch[2])
    rx, dx, mo, gf, dens, qx, px, own, part = call(
        sized(outer_kernel),
        (rx_t, dx_t, mo_t, mo_t, dens_t, qx_t, s(3, 20, 2, 24, 128), s(3, 16, 16, 128), s(count, 128)), scratch,
        rx, dx, mo, gf, dens, qx, xlo, xhi, qk, fl, cl,
        flush=(8,), input_output_aliases={n: n for n in range(6)},
    )
    sums = lax.all_to_all(part, ALL, 0, 0, tiled=True)
    cones, dens = call(
        cones_kernel, (s(3, 16, 16, 128), dens_t), [v(3, 6, 2, 32, 128)], px, dens, flush=(1,)
    )
    disp, sens = call(
        final_kernel, (s(3, 16, 16, 128), s(16, 16, 128)), [], sums, load, own, cones, flush=(0, 1)
    )
    return disp, sens, dens


def solution(mesh):
    nodal, cell = P(None, "gx", "gy", "gz"), P("gx", "gy", "gz")
    return jax.shard_map(
        body, mesh=mesh, in_specs=(nodal, cell, P()), out_specs=(nodal, cell, cell), check_vma=False
    )
```

```python
import math

import jax
import jax.numpy as jnp
import numpy as np
from jax import lax
from jax.experimental import pallas as pl
from jax.experimental.pallas import tpu as pltpu
from jax.sharding import PartitionSpec as P


BRICK = 16
young_floor = 0.001
spring_rate = 0.05
sharpness = 8.0
threshold = 0.5
poisson = 0.3
ALL = ("gx", "gy", "gz")
INTERPRET = False

NXL, NYL, NZL = 16, 16, 128
WIN = 24


def element_matrix():
    lame_first = poisson / ((1.0 + poisson) * (1.0 - 2.0 * poisson))
    shear_mod = 1.0 / (2.0 * (1.0 + poisson))
    elastic = np.zeros((6, 6))
    elastic[:3, :3] = lame_first
    for axis_one in range(3):
        elastic[axis_one, axis_one] += 2.0 * shear_mod
        elastic[axis_one + 3, axis_one + 3] = shear_mod
    gauss_point = 1.0 / math.sqrt(3.0)
    stiffness = np.zeros((24, 24))
    for point_x in (-gauss_point, gauss_point):
        for point_y in (-gauss_point, gauss_point):
            for point_z in (-gauss_point, gauss_point):
                strain = np.zeros((6, 24))
                for corner in range(8):
                    sign_a = 2 * (corner // 4) - 1
                    sign_b = 2 * (corner // 2 % 2) - 1
                    sign_c = 2 * (corner % 2) - 1
                    along_x = 0.25 * sign_a * (1 + sign_b * point_y) * (1 + sign_c * point_z)
                    along_y = 0.25 * (1 + sign_a * point_x) * sign_b * (1 + sign_c * point_z)
                    along_z = 0.25 * (1 + sign_a * point_x) * (1 + sign_b * point_y) * sign_c
                    column = 3 * corner
                    strain[0, column] = along_x
                    strain[1, column + 1] = along_y
                    strain[2, column + 2] = along_z
                    strain[3, column + 1] = along_z
                    strain[3, column + 2] = along_y
                    strain[4, column] = along_z
                    strain[4, column + 2] = along_x
                    strain[5, column] = along_y
                    strain[5, column + 1] = along_x
                stiffness += strain.T @ elastic @ strain * 0.125
    return stiffness


def modal_constants():
    modes = [(px, py, pz) for px in (0, 1) for py in (0, 1) for pz in (0, 1)]
    change = np.zeros((24, 24))
    for c in range(3):
        for m, mode in enumerate(modes):
            for q in range(8):
                corner = (q // 4, q // 2 % 2, q % 2)
                sign = 1.0
                for axis in range(3):
                    if mode[axis] and not corner[axis]:
                        sign = -sign
                change[8 * c + m, 3 * q + c] = sign
    hat = change @ element_matrix() @ change.T / 64.0

    def at(c1, m1, c2, m2):
        return hat[8 * c1 + modes.index(m1), 8 * c2 + modes.index(m2)]

    k = {
        "a": at(0, (1, 0, 0), 0, (1, 0, 0)),
        "b": at(0, (1, 0, 0), 1, (0, 1, 0)),
        "p": at(0, (0, 1, 1), 0, (0, 1, 1)),
        "r": at(0, (0, 1, 1), 1, (1, 0, 1)),
        "g": at(0, (0, 1, 0), 1, (1, 0, 0)),
        "h": at(2, (1, 1, 1), 2, (1, 1, 1)),
        "c": at(1, (1, 1, 0), 1, (1, 1, 0)),
        "d": at(1, (1, 1, 0), 2, (1, 0, 1)),
    }
    made = np.zeros((24, 24))

    def put(c1, m1, c2, m2, v):
        made[8 * c1 + modes.index(m1), 8 * c2 + modes.index(m2)] += v

    for c in range(3):
        unit = tuple(int(i == c) for i in range(3))
        anti = tuple(int(i != c) for i in range(3))
        put(c, (1, 1, 1), c, (1, 1, 1), k["h"])
        for e in range(3):
            unit_e = tuple(int(i == e) for i in range(3))
            anti_e = tuple(int(i != e) for i in range(3))
            put(c, unit, e, unit_e, k["a"] if c == e else k["b"])
            put(c, anti, e, anti_e, k["p"] if c == e else k["r"])
            if c != e:
                put(c, unit_e, c, unit_e, k["g"])
                put(c, unit_e, e, unit, k["g"])
                both = tuple(int(i in (c, e)) for i in range(3))
                o = 3 - c - e
                both_o = tuple(int(i in (o, e)) for i in range(3))
                put(c, both, c, both, k["c"])
                put(c, both, o, both_o, k["d"])
    assert np.abs(made - hat).max() < 1e-12
    return k


K = modal_constants()
W = {n: 3.0 - math.sqrt(n) for n in range(9)}
KS = (0, 1, 2, 4, 5, 8)


def mode(*axes):
    return tuple(int(i in axes) for i in range(3))


def f32(x):
    return float(np.float32(x))


def roll(x, shift):
    shift = shift % 128
    return x if shift == 0 else pltpu.roll(x, shift, 1)


def lane_of(shape):
    return lax.broadcasted_iota(jnp.int32, shape, 1)


def z_next(a0, a1, lane, by=1):
    r0, r1 = roll(a0, -by), roll(a1, -by)
    edge = lane >= 128 - by
    return jnp.where(edge, r1, r0), jnp.where(edge, r0, r1)


def z_prev(a0, a1, lane, by=1):
    r0, r1 = roll(a0, by), roll(a1, by)
    edge = lane < by
    return jnp.where(edge, r1, r0), jnp.where(edge, r0, r1)


def modal_of(lo, hi):
    m = {}
    for (c, py, pz), low in lo.items():
        high = hi[c, py, pz]
        if py or pz:
            m[c, (0, py, pz)] = low + high
        m[c, (1, py, pz)] = high - low
    return m


def forces_of(m, e):
    ea, eb = e * f32(K["a"] - K["b"]), e * f32(K["b"])
    ep, er = e * f32(K["p"] - K["r"]), e * f32(K["r"])
    eg, eh = e * f32(K["g"]), e * f32(K["h"])
    ec, ed = e * f32(K["c"]), e * f32(K["d"])
    f = {}
    for first, second, pick in ((ea, eb, lambda c: mode(c)), (ep, er, lambda c: mode(*{0, 1, 2} - {c}))):
        vals = [m[c, pick(c)] for c in range(3)]
        shared = (vals[0] + vals[1] + vals[2]) * second
        for c in range(3):
            f[c, pick(c)] = vals[c] * first + shared
    for c, e2 in ((0, 1), (0, 2), (1, 2)):
        shared = (m[c, mode(e2)] + m[e2, mode(c)]) * eg
        f[c, mode(e2)] = shared
        f[e2, mode(c)] = shared
    for c in range(3):
        f[c, (1, 1, 1)] = m[c, (1, 1, 1)] * eh
    for e2 in range(3):
        c, o = [i for i in range(3) if i != e2]
        v1, v2 = m[c, mode(c, e2)], m[o, mode(o, e2)]
        f[c, mode(c, e2)] = v1 * ec + v2 * ed
        f[o, mode(o, e2)] = v2 * ec + v1 * ed
    return f


def energy_of(m):
    total = None
    for first, second, pick in (
        (K["a"] - K["b"], K["b"], lambda c: mode(c)),
        (K["p"] - K["r"], K["r"], lambda c: mode(*{0, 1, 2} - {c})),
    ):
        vals = [m[c, pick(c)] for c in range(3)]
        s = vals[0] + vals[1] + vals[2]
        part = (vals[0] * vals[0] + vals[1] * vals[1] + vals[2] * vals[2]) * f32(first) + s * s * f32(second)
        total = part if total is None else total + part
    shear = None
    for c, e2 in ((0, 1), (0, 2), (1, 2)):
        s = m[c, mode(e2)] + m[e2, mode(c)]
        shear = s * s if shear is None else shear + s * s
    total = total + shear * f32(K["g"])
    triple = None
    for c in range(3):
        v = m[c, (1, 1, 1)]
        triple = v * v if triple is None else triple + v * v
    total = total + triple * f32(K["h"])
    squares = cross = None
    for e2 in range(3):
        c, o = [i for i in range(3) if i != e2]
        v1, v2 = m[c, mode(c, e2)], m[o, mode(o, e2)]
        sq, cr = v1 * v1 + v2 * v2, v1 * v2
        squares = sq if squares is None else squares + sq
        cross = cr if cross is None else cross + cr
    return total + squares * f32(K["c"]) + cross * f32(2.0 * K["d"])


def x_parts(f0, f1, f2):
    out = {}
    for k in KS:
        v = f0 * f32(W[k])
        if k + 1 in W:
            v = v + f1 * f32(W[k + 1])
        if k + 4 in W:
            v = v + f2 * f32(W[k + 4])
        out[k] = v
    return out


def pack_z_kernel(load_hbm, design_hbm, load_ref, design_ref, out_ref, sems):
    copies = [pltpu.make_async_copy(load_hbm.at[c], load_ref.at[c], sems.at[c]) for c in range(3)]
    copies.append(pltpu.make_async_copy(design_hbm, design_ref, sems.at[3]))
    for one in copies:
        one.start()
    for one in copies:
        one.wait()
    lane = lane_of((NYL, 128))

    def step(pair, _):
        acc = jnp.zeros((NYL, 128), jnp.float32)
        for par in range(2):
            for fld in range(4):
                off = 64 * par + 16 * fld
                src = load_ref[fld, 2 * pair + par] if fld < 3 else design_ref[2 * pair + par]
                acc = jnp.where(((lane - off + 8) & 127) < 16, roll(src, off), acc)
        out_ref[pair] = acc
        return 0

    lax.fori_loop(0, 8, step, 0)


def halo_merge(high, low):
    lane = lane_of(high.shape)
    return jnp.where((lane & 15) < 8, high, low)


def pack_y_kernel(load_ref, design_ref, zhi_ref, zlo_ref, place_ref, lo_ref, hi_ref):
    del place_ref
    for dst, quad, one in ((lo_ref, 0, 4), (hi_ref, 12, 11)):
        rows = slice(quad, quad + 4)
        for x in range(16):
            dst[x, 0:4] = load_ref[0, x, rows]
            dst[x, 4:8] = load_ref[1, x, rows]
            dst[16 + x, 0:4] = load_ref[2, x, rows]
            dst[16 + x, 4:8] = design_ref[x, rows]
            dst[32 + x // 8, x % 8 : x % 8 + 1] = design_ref[x, one : one + 1]
        for k in range(8):
            dst[35 + k // 2, 4 * (k % 2) : 4 * (k % 2) + 4] = halo_merge(zhi_ref[k, rows], zlo_ref[k, rows])
            dst[34, k : k + 1] = halo_merge(zhi_ref[k, one : one + 1], zlo_ref[k, one : one + 1])


def pack_x_kernel(load_ref, design_ref, zhi_ref, zlo_ref, ylo_ref, yhi_ref, rx, rxt, dx, lo_ref, hi_ref, hx):
    none = jnp.zeros((8, 128), jnp.float32)
    for k in range(8):
        half = slice(4 * (k % 2), 4 * (k % 2) + 4)
        hx[k, 0:8] = none
        hx[k, 24:32] = none
        hx[k, 3:4] = ylo_ref[34, k : k + 1]
        hx[k, 4:8] = ylo_ref[35 + k // 2, half]
        hx[k, 8:24] = halo_merge(zhi_ref[k], zlo_ref[k])
        hx[k, 24:28] = yhi_ref[35 + k // 2, half]
        hx[k, 28:29] = yhi_ref[34, k : k + 1]
    for x in range(16):
        for c in range(3):
            tile, half = (x, slice(4 * c, 4 * c + 4)) if c < 2 else (16 + x, slice(0, 4))
            rx[c, x + 3, 0:4] = ylo_ref[tile, half]
            rx[c, x + 3, 4:20] = load_ref[c, x]
            rx[c, x + 3, 20:24] = yhi_ref[tile, half]
        one = slice(x % 8, x % 8 + 1)
        dx[x + 5, 0, 0:8] = none
        dx[x + 5, 0, 24:32] = none
        dx[x + 5, 0, 3:4] = ylo_ref[32 + x // 8, one]
        dx[x + 5, 0, 4:8] = ylo_ref[16 + x, 4:8]
        dx[x + 5, 0, 8:24] = design_ref[x]
        dx[x + 5, 0, 24:28] = yhi_ref[16 + x, 4:8]
        dx[x + 5, 0, 28:29] = yhi_ref[32 + x // 8, one]
    for i in range(5):
        lo_ref[288 + 32 * i : 320 + 32 * i] = dx[5 + i, 0]
        hi_ref[216 + 32 * i : 248 + 32 * i] = dx[16 + i, 0]
    for i in range(3):
        lo_ref[448 + 32 * i : 480 + 32 * i] = hx[i]
        hi_ref[376 + 32 * i : 408 + 32 * i] = hx[5 + i]
    for c in range(3):
        for i in range(4):
            lo_ref[24 * (4 * c + i) : 24 * (4 * c + i) + 24] = rx[c, 3 + i]
        for i in range(3):
            hi_ref[24 * (3 * c + i) : 24 * (3 * c + i) + 24] = rx[c, 16 + i]
    for k in range(8):
        spread_pair(hx[k], 2 * k, (2 * k, 2 * k + 1), rxt, dx, True)


def spread_pair(tile, x, wanted, rxt, dx, both):
    for par in range(2):
        if x + par in wanted:
            dx[x + par + 5, 1] = roll(tile, -(64 * par + 48))
            if both or -3 <= x + par <= 19:
                for c in range(3):
                    rxt[c, x + par + 3] = roll(tile, -(64 * par + 16 * c))[4:28]


def x_halos(xlo_ref, xhi_ref, rx, rxt, dx):
    for c in range(3):
        for i in range(4):
            rx[c, 19 + i] = xhi_ref[24 * (4 * c + i) : 24 * (4 * c + i) + 24]
        for i in range(3):
            rx[c, i] = xlo_ref[24 * (3 * c + i) : 24 * (3 * c + i) + 24]
    for i in range(5):
        dx[21 + i, 0] = xhi_ref[288 + 32 * i : 320 + 32 * i]
        dx[i, 0] = xlo_ref[216 + 32 * i : 248 + 32 * i]
    for i in range(3):
        spread_pair(xhi_ref[448 + 32 * i : 480 + 32 * i], 16 + 2 * i, range(16, 21), rxt, dx, False)
        spread_pair(xlo_ref[376 + 32 * i : 408 + 32 * i], -6 + 2 * i, range(-5, 0), rxt, dx, False)


def place_kernel(map_ref, order_ref, qk, fl, cl, *, sizes):
    del order_ref
    nx, ny, nz = sizes
    i_x, i_y, i_z = (lax.axis_index(a) for a in ALL)
    lane = lane_of((WIN, 128))
    row = lax.broadcasted_iota(jnp.int32, (WIN, 128), 0)
    y_at = i_y * NYL + row - 4
    z_at = [i_z * NZL + lane, i_z * NZL + jnp.where(lane < 64, lane + 128, lane - 128)]

    def inside(at, step, length):
        return jnp.where((at + step >= 0) & (at + step < length), 1.0, 0.0)

    y_in = [inside(y_at, 0, ny)] + [inside(y_at, s, ny) + inside(y_at, -s, ny) for s in (1, 2)]
    for t in range(2):
        z_in = [inside(z_at[t], 0, nz)] + [inside(z_at[t], s, nz) + inside(z_at[t], -s, nz) for s in (1, 2)]
        qk[0, t] = y_in[0] * z_in[0]
        qk[1, t] = y_in[1] * z_in[0] + y_in[0] * z_in[1]
        qk[2, t] = y_in[1] * z_in[1]
        qk[3, t] = y_in[2] * z_in[0] + y_in[0] * z_in[2]
        qk[4, t] = y_in[1] * z_in[2] + y_in[2] * z_in[1]
        qk[5, t] = y_in[2] * z_in[2]
        cl[t] = y_in[0] * z_in[0]
    gbx, gby, gbz = nx // BRICK, ny // BRICK, nz // BRICK
    bricks = NZL // BRICK

    def flag_at(bx, by, bz):
        ok = (bx >= 0) & (bx < gbx) & (by >= 0) & (by < gby) & (bz >= 0) & (bz < gbz)
        value = map_ref[jnp.clip(bx, 0, gbx - 1), jnp.clip(by, 0, gby - 1), jnp.clip(bz, 0, gbz - 1)]
        return jnp.where(ok, value, 0).astype(jnp.float32)

    for xc in range(3):
        lines = []
        for yc in range(3):
            flag = [flag_at(i_x + xc - 1, i_y + yc - 1, i_z * bricks + n - 1) for n in range(bricks + 2)]
            main = jnp.zeros((WIN, 128), jnp.float32)
            for n in range(bricks):
                main = jnp.where((lane >> 4) == n, flag[n + 1], main)
            lines.append((main, jnp.where(lane < 64, flag[bricks + 1], flag[0])))
        for t in range(2):
            fl[xc, t] = jnp.where(row < 4, lines[0][t], jnp.where(row < 20, lines[1][t], lines[2][t]))


def zy_plane(tile, zt, t_ref, slot, lane, tiles=2, base=0, blocks=3):
    for c in range(3):
        a0, a1 = tile(c, 0), tile(c, 1)
        n0, n1 = z_next(a0, a1, lane)
        zt[2 * c, 0, 0:24] = a0 + n0
        zt[2 * c + 1, 0, 0:24] = n0 - a0
        if tiles == 2:
            zt[2 * c, 1, 0:24] = a1 + n1
            zt[2 * c + 1, 1, 0:24] = n1 - a1
    for f in range(6):
        for t in range(tiles):
            for b in range(blocks):
                r = base + 8 * b
                lo, hi = zt[f, t, r : r + 8], zt[f, t, r + 1 : r + 9]
                t_ref[slot, 2 * f, t, 8 * b : 8 * b + 8] = lo + hi
                t_ref[slot, 2 * f + 1, t, 8 * b : 8 * b + 8] = hi - lo


def read_t(t_ref, slot, t, b):
    out = {}
    for c in range(3):
        for pz in range(2):
            for py in range(2):
                out[c, py, pz] = t_ref[slot, 4 * c + 2 * pz + py, t, 8 * b : 8 * b + 8]
    return out


LIFT = math.tanh(sharpness * threshold)
SCALE = LIFT + math.tanh(sharpness * (1.0 - threshold))


def cone_yz(av, t, rows):
    lo, hi = rows

    def at(n, step):
        return av[n, t, lo + step : hi + step]

    def both(n, step):
        return at(n, -step) + at(n, step)

    return [
        at(0, 0) + both(1, 1) + both(3, 2),
        at(1, 0) + both(2, 1) + both(4, 2),
        at(3, 0) + both(4, 1) + both(5, 2),
    ]


def density_planes(first, last, nx, dx, qk, fl, av, mo, gfs, dens_ref):
    lane = lane_of((WIN, 128))
    i_x = lax.axis_index("gx")

    def scalar_inside(at, step):
        return jnp.where((at + step >= 0) & (at + step < nx), 1.0, 0.0)

    def step(e, _):
        for t in range(2):
            f0 = dx[e + 2, t]
            f1 = dx[e + 1, t] + dx[e + 3, t]
            f2 = dx[e, t] + dx[e + 4, t]
            for n, part in enumerate(x_parts(f0, f1, f2).values()):
                av[n, t] = part
        x_at = i_x * NXL + e - 3
        x0 = scalar_inside(x_at, 0)
        x1 = scalar_inside(x_at, 1) + scalar_inside(x_at, -1)
        x2 = scalar_inside(x_at, 2) + scalar_inside(x_at, -2)
        cls = jnp.where(e < 3, 0, jnp.where(e < 19, 1, 2))
        b = [cone_yz(av, t, (4, 28)) for t in range(2)]
        n1, p1 = z_next(b[0][1], b[1][1], lane), z_prev(b[0][1], b[1][1], lane)
        n2, p2 = z_next(b[0][2], b[1][2], lane, 2), z_prev(b[0][2], b[1][2], lane, 2)
        weights = x_parts(x0, x1, x2)
        for t in range(2):
            cone = b[t][0] + (n1[t] + p1[t]) + (n2[t] + p2[t])
            ws = None
            for n, wk in enumerate(weights.values()):
                ws = qk[n, t] * wk if ws is None else ws + qk[n, t] * wk
            inv = 1.0 / jnp.maximum(ws, 1.0)
            th = jnp.tanh(sharpness * (cone * inv - threshold))
            dens = (LIFT + th) * f32(1.0 / SCALE)
            flag = fl[cls, t]
            sq = dens * dens
            mo[e, t] = (young_floor + sq * dens * (1.0 - young_floor)) * flag
            gfs[t][e] = sq * flag * (1.0 - th * th) * inv * f32(-3.0 * (1.0 - young_floor) * sharpness / SCALE)
            if t == 0:
                av[0, 0, 0:24] = dens

        @pl.when((e >= 3) & (e < 19))
        def _():
            dens_ref[e - 3] = av[0, 0, 4:20]

        return 0

    lax.fori_loop(first, last, step, 0)


def operate_planes(first, last, nx, rs, mo, cl, qs, zt, tt, gp, yp, yg):
    lane = lane_of((WIN, 128))
    i_x = lax.axis_index("gx")
    gp[...] = jnp.zeros((12, 2, 24, 128), jnp.float32)
    zy_plane(lambda c, t: rs[t][c, first], zt, tt, first & 1, lane)

    def step(e, _):
        new, old = (e + 1) & 1, e & 1
        zy_plane(lambda c, t: rs[t][c, e + 1], zt, tt, new, lane)
        for t in range(2):
            for b in range(3):
                rows = slice(8 * b, 8 * b + 8)
                force = forces_of(modal_of(read_t(tt, old, t, b), read_t(tt, new, t, b)), mo[e, t, rows])
                for c in range(3):
                    for pz in range(2):
                        n = []
                        for py in range(2):
                            fd = force[c, (1, py, pz)]
                            fs = force.get((c, (0, py, pz)))
                            at = 4 * c + 2 * pz + py
                            before = gp[at, t, rows]
                            if fs is None:
                                gp[at, t, rows] = fd
                                n.append(before - fd)
                            else:
                                gp[at, t, rows] = fs + fd
                                n.append((fs - fd) + before)
                        yp[2 * c + pz, t, rows] = n[0] - n[1]
                        yg[2 * c + pz, t, 8 + 8 * b : 16 + 8 * b] = n[0] + n[1]

        @pl.when(e > first)
        def _():
            x_on = jnp.where(i_x * NXL + e - 3 < nx, 1.0, 0.0)
            for c in range(3):
                p, g = [], []
                for t in range(2):
                    zs = yp[2 * c, t] + yg[2 * c, t, 7:31]
                    zd = yp[2 * c + 1, t] + yg[2 * c + 1, t, 7:31]
                    p.append(zs - zd)
                    g.append(zs + zd)
                gb = z_prev(g[0], g[1], lane)
                for t in range(2):
                    value = p[t] + gb[t] + rs[t][c, e] * spring_rate
                    qs[t][c, e - 1] = value * (cl[t] * x_on)

        return 0

    lax.fori_loop(first, last, step, 0)


def sum_planes(first, last, acc, rs, qs, mo, zt, tt):
    lane = lane_of((WIN, 128))
    zy_plane(lambda c, t: qs[t][c, first + 2], zt, tt, first & 1, lane, tiles=1, base=4, blocks=2)

    def step(x, acc):
        s0, s1, s2, s3 = acc
        new, old = (x + 1) & 1, x & 1
        zy_plane(lambda c, t: qs[t][c, x + 3], zt, tt, new, lane, tiles=1, base=4, blocks=2)
        for b in range(2):
            rows = slice(4 + 8 * b, 12 + 8 * b)
            for c in range(3):
                r, q = rs[0][c, x + 3, rows], qs[0][c, x + 2, rows]
                s0, s1, s2 = s0 + r * r, s1 + r * q, s2 + q * q
            m = modal_of(read_t(tt, old, 0, b), read_t(tt, new, 0, b))
            s3 = s3 + energy_of(m) * mo[x + 3, 0, rows]
        return s0, s1, s2, s3

    return lax.fori_loop(first, last, step, acc)


def clear_edges(zt, yg):
    zt[:, :, 24:32] = jnp.zeros((6, 2, 8, 128), jnp.float32)
    yg[:, :, 0:8] = jnp.zeros((6, 2, 8, 128), jnp.float32)


def inner_kernel(
    rx, rxt, dx, qk, fl, cl, mo, gf, gft, dens_ref, qx, qxt, acc_ref, av, zt, tt, gp, yp, yg, *, sizes
):
    nx = sizes[0]
    clear_edges(zt, yg)
    density_planes(5, 17, nx, dx, qk, fl, av, mo, (gf, gft), dens_ref)
    operate_planes(5, 17, nx, (rx, rxt), mo, cl, (qx, qxt), zt, tt, gp, yp, yg)
    zero = jnp.zeros((8, 128), jnp.float32)
    for n, part in enumerate(sum_planes(3, 13, (zero,) * 4, (rx, rxt), (qx, qxt), mo, zt, tt)):
        acc_ref[n] = part


def outer_kernel(
    rx_in, rxt_in, dx_in, mo_in, gf_in, gft_in, dens_in, qx_in, qxt_in, acc_ref, xlo_ref, xhi_ref, qk, fl, cl,
    rx, rxt, dx, mo, gf, gft, dens_ref, qx, qxt, rp, qp, gpk, sum_ref, av, zt, tt, gp, yp, yg, *, sizes
):
    del rx_in, rxt_in, dx_in, mo_in, gf_in, gft_in, dens_in, qx_in, qxt_in
    nx = sizes[0]
    rs, qs, gfs = (rx, rxt), (qx, qxt), (gf, gft)
    clear_edges(zt, yg)
    x_halos(xlo_ref, xhi_ref, rx, rxt, dx)
    density_planes(0, 5, nx, dx, qk, fl, av, mo, gfs, dens_ref)
    density_planes(17, 22, nx, dx, qk, fl, av, mo, gfs, dens_ref)
    operate_planes(0, 6, nx, rs, mo, cl, qs, zt, tt, gp, yp, yg)
    operate_planes(16, 22, nx, rs, mo, cl, qs, zt, tt, gp, yp, yg)
    acc = tuple(acc_ref[n] for n in range(4))
    acc = sum_planes(0, 3, acc, rs, qs, mo, zt, tt)
    acc = sum_planes(13, 16, acc, rs, qs, mo, zt, tt)
    line = jnp.zeros((8, 128), jnp.float32)
    lane = lane_of((8, 128))
    for n, part in enumerate(acc):
        total = jnp.sum(jnp.sum(part, axis=0, keepdims=True), axis=1, keepdims=True)
        line = jnp.where(lane == n, total, line)
    for n in range(sum_ref.shape[0] // 8):
        sum_ref[8 * n : 8 * n + 8] = line

    def pack_step(j, _):
        for c in range(3):
            rp[c, j] = pack_chunks([(rx[c, 4 * k + j + 1], rxt[c, 4 * k + j + 1]) for k in range(4)])
            qp[c, j] = pack_chunks([(qx[c, 4 * k + j], qxt[c, 4 * k + j]) for k in range(4)])
        return 0

    lax.fori_loop(0, 9, pack_step, 0)

    def pack_weights(j, _):
        gpk[j] = pack_chunks([(gf[4 * k + j + 1], gft[4 * k + j + 1]) for k in range(4)])
        return 0

    lax.fori_loop(0, 8, pack_weights, 0)


def pack_chunks(tiles):
    lane = lane_of((WIN, 128))
    out = None
    for k, (main, side) in enumerate(tiles):
        high = roll(jnp.where(lane >= 64, main, side), 32 * k + 4)
        low = roll(jnp.where(lane >= 64, side, main), 32 * k + 28)
        out = high if out is None else jnp.where(lane >= 32 * k, high, out)
        out = jnp.where(lane >= 32 * k + 16, low, out)
    return out


def cross_energy(m, o):
    total = None
    for first, second, pick in (
        (K["a"] - K["b"], K["b"], lambda c: mode(c)),
        (K["p"] - K["r"], K["r"], lambda c: mode(*{0, 1, 2} - {c})),
    ):
        vm, vo = [m[c, pick(c)] for c in range(3)], [o[c, pick(c)] for c in range(3)]
        sm, so = vm[0] + vm[1] + vm[2], vo[0] + vo[1] + vo[2]
        part = (vm[0] * vo[0] + vm[1] * vo[1] + vm[2] * vo[2]) * f32(first) + sm * so * f32(second)
        total = part if total is None else total + part
    shear = None
    for c, e2 in ((0, 1), (0, 2), (1, 2)):
        v = (m[c, mode(e2)] + m[e2, mode(c)]) * (o[c, mode(e2)] + o[e2, mode(c)])
        shear = v if shear is None else shear + v
    triple = None
    for c in range(3):
        v = m[c, (1, 1, 1)] * o[c, (1, 1, 1)]
        triple = v if triple is None else triple + v
    same = cross = None
    for e2 in range(3):
        c, d = [i for i in range(3) if i != e2]
        m1, m2 = m[c, mode(c, e2)], m[d, mode(d, e2)]
        o1, o2 = o[c, mode(c, e2)], o[d, mode(d, e2)]
        sq, cr = m1 * o1 + m2 * o2, m1 * o2 + m2 * o1
        same = sq if same is None else same + sq
        cross = cr if cross is None else cross + cr
    total = total + shear * f32(K["g"]) + triple * f32(K["h"])
    return total + same * f32(K["c"]) + cross * f32(K["d"])


def tail_kernel(rx, qx, gf, rp, qp, gpk, dens_in, out_ref, dens_ref, px, pp, zt, tr, tq, av, ap, bp):
    dens_ref[...] = dens_in[...]
    lane = lane_of((WIN, 128))
    edge = lane == 127
    zt[:, :, 24:32] = jnp.zeros((6, 2, 8, 128), jnp.float32)

    def half_plane(at, after, t_ref, slot):
        for c in range(3):
            a = at(c)
            n = after(c, a)
            zt[2 * c, 0, 0:24] = a + n
            zt[2 * c + 1, 0, 0:24] = n - a
        for f in range(6):
            for b in range(3):
                lo, hi = zt[f, 0, 8 * b : 8 * b + 8], zt[f, 0, 8 * b + 1 : 8 * b + 9]
                t_ref[slot, 2 * f, 0, 8 * b : 8 * b + 8] = lo + hi
                t_ref[slot, 2 * f + 1, 0, 8 * b : 8 * b + 8] = hi - lo

    def main_plane(i, slot):
        chunk = jnp.minimum(i >> 2, 3)
        j, shift = i - 4 * chunk, 123 - 32 * chunk

        def after(src):
            return lambda c, a: jnp.where(edge, pltpu.roll(src[c, j], shift, 1), roll(a, -1))

        half_plane(lambda c: rx[c, i + 1], after(rp), tr, slot)
        half_plane(lambda c: qx[c, i], after(qp), tq, slot)

    def end_plane(j, slot):
        half_plane(lambda c: rp[c, j], lambda c, a: roll(a, -1), tr, slot)
        half_plane(lambda c: qp[c, j], lambda c, a: roll(a, -1), tq, slot)

    def energies(i, g_ref, out):
        new, old = (i + 1) & 1, i & 1
        for b in range(3):
            rows = slice(8 * b, 8 * b + 8)
            m = modal_of(read_t(tr, old, 0, b), read_t(tr, new, 0, b))
            o = modal_of(read_t(tq, old, 0, b), read_t(tq, new, 0, b))
            g = g_ref[rows]
            out[0, i, rows] = energy_of(m) * g
            out[1, i, rows] = cross_energy(m, o) * (2.0 * g)
            out[2, i, rows] = energy_of(o) * g

    def main_step(i, _):
        main_plane(i + 1, (i + 1) & 1)
        energies(i, gf.at[i + 1], px)
        return 0

    def end_step(j, _):
        end_plane(j + 1, (j + 1) & 1)
        energies(j, gpk.at[j], pp)
        return 0

    main_plane(jnp.int32(0), 0)
    lax.fori_loop(0, 20, main_step, 0)
    end_plane(0, 0)
    lax.fori_loop(0, 8, end_step, 0)

    def parts_of(src, k, x, dst):
        f0 = src[k, x + 2]
        f1 = src[k, x + 1] + src[k, x + 3]
        f2 = src[k, x] + src[k, x + 4]
        for n, part in enumerate(x_parts(f0, f1, f2).values()):
            dst[k, n, 0, 0:24] = part

    def end_cone(j, _):
        for k in range(3):
            parts_of(pp, k, j, ap)
            b = cone_yz(ap.at[k], 0, (4, 20))
            bp[k, j, 0] = b[1]
            bp[k, j, 1] = b[2]
        return 0

    lax.fori_loop(0, 4, end_cone, 0)
    lane16 = lane_of((NYL, 128))
    for chunk in range(4):

        def cone_step(j, _):
            x = 4 * chunk + j
            for k in range(3):
                parts_of(px, k, x, av)
                b0, b1, b2 = cone_yz(av.at[k], 0, (4, 20))
                e1, e2 = bp[k, j, 0], bp[k, j, 1]
                n1 = jnp.where(lane16 == 127, roll(e1, 123 - 32 * chunk), roll(b1, -1))
                p1 = jnp.where(lane16 == 0, roll(e1, -(32 * chunk + 27)), roll(b1, 1))
                n2 = jnp.where(lane16 >= 126, roll(e2, 122 - 32 * chunk), roll(b2, -2))
                p2 = jnp.where(lane16 < 2, roll(e2, -(32 * chunk + 26)), roll(b2, 2))
                out_ref[k, x] = b0 + (n1 + p1) + (n2 + p2)
            return 0

        lax.fori_loop(0, 4, cone_step, 0)


def final_kernel(sum_ref, rx, qx, cones, disp_ref, sens_ref):
    line = jnp.sum(sum_ref[...], axis=0, keepdims=True)
    lane1 = lane_of((1, 128))
    m0, m1, m2, m3 = [jnp.sum(jnp.where(lane1 == n, line, 0.0), axis=1, keepdims=True) for n in range(4)]
    m3 = m3 + spring_rate * m2
    first = m0 / m1
    norm = m0 - 2.0 * first * m1 + first * first * m2
    grown = 1.0 + norm / m0
    second = norm / (grown * grown * m1 - 2.0 * first * grown * m2 + first * first * m3)
    c0 = jnp.broadcast_to(first + second * grown, (NYL, 128))
    c1 = jnp.broadcast_to(-second * first, (NYL, 128))

    def step(x, _):
        for c in range(3):
            disp_ref[c, x] = c0 * rx[c, x + 3, 4:20] + c1 * qx[c, x + 2, 4:20]
        sens_ref[x] = c0 * (c0 * cones[0, x] + c1 * cones[1, x]) + c1 * c1 * cones[2, x]
        return 0

    lax.fori_loop(0, 16, step, 0)


def s(*shape):
    return jax.ShapeDtypeStruct(shape, jnp.float32)


def v(*shape):
    return pltpu.VMEM(shape, jnp.float32)


def call(kernel, outs, scratch, *args, smem=0, hbm=0, flush=(), **kw):
    spec_s, spec_v = pl.BlockSpec(memory_space=pltpu.SMEM), pl.BlockSpec(memory_space=pltpu.VMEM)
    single = not isinstance(outs, (tuple, list))
    outs = [outs] if single else list(outs)
    if not INTERPRET:
        outs = [o if i in flush else pltpu.VMEM(o.shape, o.dtype) for i, o in enumerate(outs)]
        args = [
            a if i < smem else pltpu.with_memory_space_constraint(a, pltpu.HBM if i < smem + hbm else pltpu.VMEM)
            for i, a in enumerate(args)
        ]
    return pl.pallas_call(
        kernel,
        out_shape=outs[0] if single else outs,
        in_specs=[spec_s] * smem
        + [pl.BlockSpec(memory_space=pltpu.HBM)] * hbm
        + [spec_v] * (len(args) - smem - hbm),
        out_specs=spec_v if single else [spec_v] * len(outs),
        scratch_shapes=scratch,
        interpret=INTERPRET,
        compiler_params=pltpu.CompilerParams(vmem_limit_bytes=24 << 20),
        **kw,
    )(*args)


def moved(block, axis, step):
    count = lax.axis_size(axis)
    return lax.ppermute(block, axis, [(i, i - step) for i in range(count) if 0 <= i - step < count])


def body(load, design, solid_map):
    sizes = tuple(lax.axis_size(a) * n for a, n in zip(ALL, (NXL, NYL, NZL)))
    count = lax.axis_size("gx") * lax.axis_size("gy") * lax.axis_size("gz")

    def sized(kernel):
        return lambda *refs: kernel(*refs, sizes=sizes)

    load, design, zc = call(
        pack_z_kernel, (s(3, 16, 16, 128), s(16, 16, 128), s(8, 16, 128)), [pltpu.SemaphoreType.DMA((4,))],
        load, design, hbm=2,
    )
    zhi, zlo = moved(zc, "gz", 1), moved(zc, "gz", -1)
    qk, fl, cl = call(
        sized(place_kernel), (s(6, 2, 24, 128), s(3, 2, 24, 128), s(2, 24, 128)), [], solid_map, zc, smem=1
    )
    ylo_s, yhi_s = call(pack_y_kernel, (s(39, 8, 128), s(39, 8, 128)), [], load, design, zhi, zlo, cl)
    yhi, ylo = moved(ylo_s, "gy", 1), moved(yhi_s, "gy", -1)
    rx_t, dx_t, mo_t, gf_t = s(3, 23, 24, 128), s(26, 2, 32, 128), s(22, 2, 24, 128), s(22, 24, 128)
    dens_t, qx_t = s(16, 16, 128), s(3, 21, 24, 128)
    rx, rxt, dx, xlo_s, xhi_s = call(
        pack_x_kernel, (rx_t, rx_t, dx_t, s(544, 128), s(472, 128)), [v(8, 32, 128)],
        load, design, zhi, zlo, ylo, yhi,
    )
    xhi, xlo = moved(xlo_s, "gx", 1), moved(xhi_s, "gx", -1)
    scratch = [
        v(6, 2, 32, 128), v(6, 2, 32, 128), v(2, 12, 2, 24, 128), v(12, 2, 24, 128), v(6, 2, 24, 128), v(6, 2, 32, 128),
    ]
    mo, gf, gft, dens, qx, qxt, acc = call(
        sized(inner_kernel), (mo_t, gf_t, gf_t, dens_t, qx_t, qx_t, s(4, 8, 128)), scratch, rx, rxt, dx, qk, fl, cl
    )
    held = rx_t, rx_t, dx_t, mo_t, gf_t, gf_t, dens_t, qx_t, qx_t
    rx, _, _, _, gf, _, dens, qx, _, rp, qp, gpk, part = call(
        sized(outer_kernel),
        (*held, s(3, 9, 24, 128), s(3, 9, 24, 128), s(8, 24, 128), s(count, 128)), scratch,
        rx, rxt, dx, mo, gf, gft, dens, qx, qxt, acc, xlo, xhi, qk, fl, cl,
        flush=(12,), input_output_aliases={n: n for n in range(len(held))},
    )
    sums = lax.all_to_all(part, ALL, 0, 0, tiled=True)
    cones, dens = call(
        tail_kernel, (s(3, 16, 16, 128), dens_t),
        [
            v(3, 20, 24, 128), v(3, 8, 24, 128), v(6, 2, 32, 128), v(2, 12, 1, 24, 128), v(2, 12, 1, 24, 128),
            v(3, 6, 1, 32, 128), v(3, 6, 1, 32, 128), v(3, 4, 2, 16, 128),
        ],
        rx, qx, gf, rp, qp, gpk, dens, flush=(1,),
    )
    disp, sens = call(
        final_kernel, (s(3, 16, 16, 128), s(16, 16, 128)), [], sums, rx, qx, cones, flush=(0, 1)
    )
    return disp, sens, dens


def solution(mesh):
    nodal, cell = P(None, "gx", "gy", "gz"), P("gx", "gy", "gz")
    return jax.shard_map(
        body, mesh=mesh, in_specs=(nodal, cell, P()), out_specs=(nodal, cell, cell), check_vma=False
    )
```

```python
import math

import jax
import jax.numpy as jnp
import numpy as np
from jax import lax
from jax.experimental import pallas as pl
from jax.experimental.pallas import tpu as pltpu
from jax.sharding import Mesh
from jax.sharding import PartitionSpec as P


BRICK = 16
young_floor = 0.001
spring_rate = 0.05
sharpness = 8.0
threshold = 0.5
poisson = 0.3
GX = ("gx_0", "gx_1")
ALL = (GX, "gy", "gz")
INTERPRET = False

NXL, NYL, NZL = 16, 16, 128
WIN = 24


def element_matrix():
    lame_first = poisson / ((1.0 + poisson) * (1.0 - 2.0 * poisson))
    shear_mod = 1.0 / (2.0 * (1.0 + poisson))
    elastic = np.zeros((6, 6))
    elastic[:3, :3] = lame_first
    for axis_one in range(3):
        elastic[axis_one, axis_one] += 2.0 * shear_mod
        elastic[axis_one + 3, axis_one + 3] = shear_mod
    gauss_point = 1.0 / math.sqrt(3.0)
    stiffness = np.zeros((24, 24))
    for point_x in (-gauss_point, gauss_point):
        for point_y in (-gauss_point, gauss_point):
            for point_z in (-gauss_point, gauss_point):
                strain = np.zeros((6, 24))
                for corner in range(8):
                    sign_a = 2 * (corner // 4) - 1
                    sign_b = 2 * (corner // 2 % 2) - 1
                    sign_c = 2 * (corner % 2) - 1
                    along_x = 0.25 * sign_a * (1 + sign_b * point_y) * (1 + sign_c * point_z)
                    along_y = 0.25 * (1 + sign_a * point_x) * sign_b * (1 + sign_c * point_z)
                    along_z = 0.25 * (1 + sign_a * point_x) * (1 + sign_b * point_y) * sign_c
                    column = 3 * corner
                    strain[0, column] = along_x
                    strain[1, column + 1] = along_y
                    strain[2, column + 2] = along_z
                    strain[3, column + 1] = along_z
                    strain[3, column + 2] = along_y
                    strain[4, column] = along_z
                    strain[4, column + 2] = along_x
                    strain[5, column] = along_y
                    strain[5, column + 1] = along_x
                stiffness += strain.T @ elastic @ strain * 0.125
    return stiffness


def modal_constants():
    modes = [(px, py, pz) for px in (0, 1) for py in (0, 1) for pz in (0, 1)]
    change = np.zeros((24, 24))
    for c in range(3):
        for m, mode in enumerate(modes):
            for q in range(8):
                corner = (q // 4, q // 2 % 2, q % 2)
                sign = 1.0
                for axis in range(3):
                    if mode[axis] and not corner[axis]:
                        sign = -sign
                change[8 * c + m, 3 * q + c] = sign
    hat = change @ element_matrix() @ change.T / 64.0

    def at(c1, m1, c2, m2):
        return hat[8 * c1 + modes.index(m1), 8 * c2 + modes.index(m2)]

    k = {
        "a": at(0, (1, 0, 0), 0, (1, 0, 0)),
        "b": at(0, (1, 0, 0), 1, (0, 1, 0)),
        "p": at(0, (0, 1, 1), 0, (0, 1, 1)),
        "r": at(0, (0, 1, 1), 1, (1, 0, 1)),
        "g": at(0, (0, 1, 0), 1, (1, 0, 0)),
        "h": at(2, (1, 1, 1), 2, (1, 1, 1)),
        "c": at(1, (1, 1, 0), 1, (1, 1, 0)),
        "d": at(1, (1, 1, 0), 2, (1, 0, 1)),
    }
    made = np.zeros((24, 24))

    def put(c1, m1, c2, m2, v):
        made[8 * c1 + modes.index(m1), 8 * c2 + modes.index(m2)] += v

    for c in range(3):
        unit = tuple(int(i == c) for i in range(3))
        anti = tuple(int(i != c) for i in range(3))
        put(c, (1, 1, 1), c, (1, 1, 1), k["h"])
        for e in range(3):
            unit_e = tuple(int(i == e) for i in range(3))
            anti_e = tuple(int(i != e) for i in range(3))
            put(c, unit, e, unit_e, k["a"] if c == e else k["b"])
            put(c, anti, e, anti_e, k["p"] if c == e else k["r"])
            if c != e:
                put(c, unit_e, c, unit_e, k["g"])
                put(c, unit_e, e, unit, k["g"])
                both = tuple(int(i in (c, e)) for i in range(3))
                o = 3 - c - e
                both_o = tuple(int(i in (o, e)) for i in range(3))
                put(c, both, c, both, k["c"])
                put(c, both, o, both_o, k["d"])
    assert np.abs(made - hat).max() < 1e-12
    return k


K = modal_constants()
W = {n: 3.0 - math.sqrt(n) for n in range(9)}
KS = (0, 1, 2, 4, 5, 8)


def mode(*axes):
    return tuple(int(i in axes) for i in range(3))


def f32(x):
    return float(np.float32(x))


def roll(x, shift):
    shift = shift % 128
    return x if shift == 0 else pltpu.roll(x, shift, 1)


def lane_of(shape):
    return lax.broadcasted_iota(jnp.int32, shape, 1)


def z_next(a0, a1, lane, by=1):
    r0, r1 = roll(a0, -by), roll(a1, -by)
    edge = lane >= 128 - by
    return jnp.where(edge, r1, r0), jnp.where(edge, r0, r1)


def z_prev(a0, a1, lane, by=1):
    r0, r1 = roll(a0, by), roll(a1, by)
    edge = lane < by
    return jnp.where(edge, r1, r0), jnp.where(edge, r0, r1)


def modal_of(lo, hi):
    m = {}
    for (c, py, pz), low in lo.items():
        high = hi[c, py, pz]
        if py or pz:
            m[c, (0, py, pz)] = low + high
        m[c, (1, py, pz)] = high - low
    return m


def forces_of(m, e):
    ea, eb = e * f32(K["a"] - K["b"]), e * f32(K["b"])
    ep, er = e * f32(K["p"] - K["r"]), e * f32(K["r"])
    eg, eh = e * f32(K["g"]), e * f32(K["h"])
    ec, ed = e * f32(K["c"]), e * f32(K["d"])
    f = {}
    for first, second, pick in ((ea, eb, lambda c: mode(c)), (ep, er, lambda c: mode(*{0, 1, 2} - {c}))):
        vals = [m[c, pick(c)] for c in range(3)]
        shared = (vals[0] + vals[1] + vals[2]) * second
        for c in range(3):
            f[c, pick(c)] = vals[c] * first + shared
    for c, e2 in ((0, 1), (0, 2), (1, 2)):
        shared = (m[c, mode(e2)] + m[e2, mode(c)]) * eg
        f[c, mode(e2)] = shared
        f[e2, mode(c)] = shared
    for c in range(3):
        f[c, (1, 1, 1)] = m[c, (1, 1, 1)] * eh
    for e2 in range(3):
        c, o = [i for i in range(3) if i != e2]
        v1, v2 = m[c, mode(c, e2)], m[o, mode(o, e2)]
        f[c, mode(c, e2)] = v1 * ec + v2 * ed
        f[o, mode(o, e2)] = v2 * ec + v1 * ed
    return f


def energy_of(m):
    total = None
    for first, second, pick in (
        (K["a"] - K["b"], K["b"], lambda c: mode(c)),
        (K["p"] - K["r"], K["r"], lambda c: mode(*{0, 1, 2} - {c})),
    ):
        vals = [m[c, pick(c)] for c in range(3)]
        s = vals[0] + vals[1] + vals[2]
        part = (vals[0] * vals[0] + vals[1] * vals[1] + vals[2] * vals[2]) * f32(first) + s * s * f32(second)
        total = part if total is None else total + part
    shear = None
    for c, e2 in ((0, 1), (0, 2), (1, 2)):
        s = m[c, mode(e2)] + m[e2, mode(c)]
        shear = s * s if shear is None else shear + s * s
    total = total + shear * f32(K["g"])
    triple = None
    for c in range(3):
        v = m[c, (1, 1, 1)]
        triple = v * v if triple is None else triple + v * v
    total = total + triple * f32(K["h"])
    squares = cross = None
    for e2 in range(3):
        c, o = [i for i in range(3) if i != e2]
        v1, v2 = m[c, mode(c, e2)], m[o, mode(o, e2)]
        sq, cr = v1 * v1 + v2 * v2, v1 * v2
        squares = sq if squares is None else squares + sq
        cross = cr if cross is None else cross + cr
    return total + squares * f32(K["c"]) + cross * f32(2.0 * K["d"])


def x_parts(f0, f1, f2):
    out = {}
    for k in KS:
        v = f0 * f32(W[k])
        if k + 1 in W:
            v = v + f1 * f32(W[k + 1])
        if k + 4 in W:
            v = v + f2 * f32(W[k + 4])
        out[k] = v
    return out


def pack_z_kernel(load_hbm, design_hbm, load_ref, design_ref, out_ref, sems):
    copies = [pltpu.make_async_copy(load_hbm.at[c], load_ref.at[c], sems.at[c]) for c in range(3)]
    copies.append(pltpu.make_async_copy(design_hbm, design_ref, sems.at[3]))
    for one in copies:
        one.start()
    for one in copies:
        one.wait()
    lane = lane_of((NYL, 128))

    def step(pair, _):
        acc = jnp.zeros((NYL, 128), jnp.float32)
        for par in range(2):
            for fld in range(4):
                off = 64 * par + 16 * fld
                src = load_ref[fld, 2 * pair + par] if fld < 3 else design_ref[2 * pair + par]
                acc = jnp.where(((lane - off + 8) & 127) < 16, roll(src, off), acc)
        out_ref[pair] = acc
        return 0

    lax.fori_loop(0, 8, step, 0)


def halo_merge(high, low):
    lane = lane_of(high.shape)
    return jnp.where((lane & 15) < 8, high, low)


def pack_y_kernel(load_ref, design_ref, zhi_ref, zlo_ref, place_ref, lo_ref, hi_ref):
    del place_ref
    for dst, quad, one in ((lo_ref, 0, 4), (hi_ref, 12, 11)):
        rows = slice(quad, quad + 4)
        for x in range(16):
            dst[x, 0:4] = load_ref[0, x, rows]
            dst[x, 4:8] = load_ref[1, x, rows]
            dst[16 + x, 0:4] = load_ref[2, x, rows]
            dst[16 + x, 4:8] = design_ref[x, rows]
            dst[32 + x // 8, x % 8 : x % 8 + 1] = design_ref[x, one : one + 1]
        for k in range(8):
            dst[35 + k // 2, 4 * (k % 2) : 4 * (k % 2) + 4] = halo_merge(zhi_ref[k, rows], zlo_ref[k, rows])
            dst[34, k : k + 1] = halo_merge(zhi_ref[k, one : one + 1], zlo_ref[k, one : one + 1])


def pack_x_kernel(load_ref, design_ref, zhi_ref, zlo_ref, ylo_ref, yhi_ref, rx, rxt, dx, lo_ref, hi_ref, hx):
    none = jnp.zeros((8, 128), jnp.float32)
    for k in range(8):
        half = slice(4 * (k % 2), 4 * (k % 2) + 4)
        hx[k, 0:8] = none
        hx[k, 24:32] = none
        hx[k, 3:4] = ylo_ref[34, k : k + 1]
        hx[k, 4:8] = ylo_ref[35 + k // 2, half]
        hx[k, 8:24] = halo_merge(zhi_ref[k], zlo_ref[k])
        hx[k, 24:28] = yhi_ref[35 + k // 2, half]
        hx[k, 28:29] = yhi_ref[34, k : k + 1]
    for x in range(16):
        for c in range(3):
            tile, half = (x, slice(4 * c, 4 * c + 4)) if c < 2 else (16 + x, slice(0, 4))
            rx[c, x + 3, 0:4] = ylo_ref[tile, half]
            rx[c, x + 3, 4:20] = load_ref[c, x]
            rx[c, x + 3, 20:24] = yhi_ref[tile, half]
        one = slice(x % 8, x % 8 + 1)
        dx[x + 5, 0, 0:8] = none
        dx[x + 5, 0, 24:32] = none
        dx[x + 5, 0, 3:4] = ylo_ref[32 + x // 8, one]
        dx[x + 5, 0, 4:8] = ylo_ref[16 + x, 4:8]
        dx[x + 5, 0, 8:24] = design_ref[x]
        dx[x + 5, 0, 24:28] = yhi_ref[16 + x, 4:8]
        dx[x + 5, 0, 28:29] = yhi_ref[32 + x // 8, one]
    for i in range(5):
        lo_ref[288 + 32 * i : 320 + 32 * i] = dx[5 + i, 0]
        hi_ref[216 + 32 * i : 248 + 32 * i] = dx[16 + i, 0]
    for i in range(3):
        lo_ref[448 + 32 * i : 480 + 32 * i] = hx[i]
        hi_ref[376 + 32 * i : 408 + 32 * i] = hx[5 + i]
    for c in range(3):
        for i in range(4):
            lo_ref[24 * (4 * c + i) : 24 * (4 * c + i) + 24] = rx[c, 3 + i]
        for i in range(3):
            hi_ref[24 * (3 * c + i) : 24 * (3 * c + i) + 24] = rx[c, 16 + i]
    for k in range(8):
        spread_pair(hx[k], 2 * k, (2 * k, 2 * k + 1), rxt, dx, True)


def spread_pair(tile, x, wanted, rxt, dx, both):
    for par in range(2):
        if x + par in wanted:
            dx[x + par + 5, 1] = roll(tile, -(64 * par + 48))
            if both or -3 <= x + par <= 19:
                for c in range(3):
                    rxt[c, x + par + 3] = roll(tile, -(64 * par + 16 * c))[4:28]


def x_halos(xlo_ref, xhi_ref, rx, rxt, dx):
    for c in range(3):
        for i in range(4):
            rx[c, 19 + i] = xhi_ref[24 * (4 * c + i) : 24 * (4 * c + i) + 24]
        for i in range(3):
            rx[c, i] = xlo_ref[24 * (3 * c + i) : 24 * (3 * c + i) + 24]
    for i in range(5):
        dx[21 + i, 0] = xhi_ref[288 + 32 * i : 320 + 32 * i]
        dx[i, 0] = xlo_ref[216 + 32 * i : 248 + 32 * i]
    for i in range(3):
        spread_pair(xhi_ref[448 + 32 * i : 480 + 32 * i], 16 + 2 * i, range(16, 21), rxt, dx, False)
        spread_pair(xlo_ref[376 + 32 * i : 408 + 32 * i], -6 + 2 * i, range(-5, 0), rxt, dx, False)


def place_kernel(map_ref, order_ref, qk, fl, cl, *, sizes):
    del order_ref
    nx, ny, nz = sizes
    i_x, i_y, i_z = (lax.axis_index(a) for a in ALL)
    lane = lane_of((WIN, 128))
    row = lax.broadcasted_iota(jnp.int32, (WIN, 128), 0)
    y_at = i_y * NYL + row - 4
    z_at = [i_z * NZL + lane, i_z * NZL + jnp.where(lane < 64, lane + 128, lane - 128)]

    def inside(at, step, length):
        return jnp.where((at + step >= 0) & (at + step < length), 1.0, 0.0)

    y_in = [inside(y_at, 0, ny)] + [inside(y_at, s, ny) + inside(y_at, -s, ny) for s in (1, 2)]
    for t in range(2):
        z_in = [inside(z_at[t], 0, nz)] + [inside(z_at[t], s, nz) + inside(z_at[t], -s, nz) for s in (1, 2)]
        qk[0, t] = y_in[0] * z_in[0]
        qk[1, t] = y_in[1] * z_in[0] + y_in[0] * z_in[1]
        qk[2, t] = y_in[1] * z_in[1]
        qk[3, t] = y_in[2] * z_in[0] + y_in[0] * z_in[2]
        qk[4, t] = y_in[1] * z_in[2] + y_in[2] * z_in[1]
        qk[5, t] = y_in[2] * z_in[2]
        cl[t] = y_in[0] * z_in[0]
    gbx, gby, gbz = nx // BRICK, ny // BRICK, nz // BRICK
    bricks = NZL // BRICK

    def flag_at(bx, by, bz):
        ok = (bx >= 0) & (bx < gbx) & (by >= 0) & (by < gby) & (bz >= 0) & (bz < gbz)
        value = map_ref[jnp.clip(bx, 0, gbx - 1), jnp.clip(by, 0, gby - 1), jnp.clip(bz, 0, gbz - 1)]
        return jnp.where(ok, value, 0).astype(jnp.float32)

    for xc in range(3):
        lines = []
        for yc in range(3):
            flag = [flag_at(i_x + xc - 1, i_y + yc - 1, i_z * bricks + n - 1) for n in range(bricks + 2)]
            main = jnp.zeros((WIN, 128), jnp.float32)
            for n in range(bricks):
                main = jnp.where((lane >> 4) == n, flag[n + 1], main)
            lines.append((main, jnp.where(lane < 64, flag[bricks + 1], flag[0])))
        for t in range(2):
            fl[xc, t] = jnp.where(row < 4, lines[0][t], jnp.where(row < 20, lines[1][t], lines[2][t]))


def zy_plane(tile, zt, t_ref, slot, lane, tiles=2, base=0, blocks=3):
    for c in range(3):
        a0, a1 = tile(c, 0), tile(c, 1)
        n0, n1 = z_next(a0, a1, lane)
        zt[2 * c, 0, 0:24] = a0 + n0
        zt[2 * c + 1, 0, 0:24] = n0 - a0
        if tiles == 2:
            zt[2 * c, 1, 0:24] = a1 + n1
            zt[2 * c + 1, 1, 0:24] = n1 - a1
    for f in range(6):
        for t in range(tiles):
            for b in range(blocks):
                r = base + 8 * b
                lo, hi = zt[f, t, r : r + 8], zt[f, t, r + 1 : r + 9]
                t_ref[slot, 2 * f, t, 8 * b : 8 * b + 8] = lo + hi
                t_ref[slot, 2 * f + 1, t, 8 * b : 8 * b + 8] = hi - lo


def read_t(t_ref, slot, t, b):
    out = {}
    for c in range(3):
        for pz in range(2):
            for py in range(2):
                out[c, py, pz] = t_ref[slot, 4 * c + 2 * pz + py, t, 8 * b : 8 * b + 8]
    return out


LIFT = math.tanh(sharpness * threshold)
SCALE = LIFT + math.tanh(sharpness * (1.0 - threshold))


def cone_yz(av, t, rows):
    lo, hi = rows

    def at(n, step):
        return av[n, t, lo + step : hi + step]

    def both(n, step):
        return at(n, -step) + at(n, step)

    return [
        at(0, 0) + both(1, 1) + both(3, 2),
        at(1, 0) + both(2, 1) + both(4, 2),
        at(3, 0) + both(4, 1) + both(5, 2),
    ]


def density_planes(first, last, nx, dx, qk, fl, av, mo, gfs, dens_ref):
    lane = lane_of((WIN, 128))
    i_x = lax.axis_index(GX)

    def scalar_inside(at, step):
        return jnp.where((at + step >= 0) & (at + step < nx), 1.0, 0.0)

    def step(e, _):
        for t in range(2):
            f0 = dx[e + 2, t]
            f1 = dx[e + 1, t] + dx[e + 3, t]
            f2 = dx[e, t] + dx[e + 4, t]
            for n, part in enumerate(x_parts(f0, f1, f2).values()):
                av[n, t] = part
        x_at = i_x * NXL + e - 3
        x0 = scalar_inside(x_at, 0)
        x1 = scalar_inside(x_at, 1) + scalar_inside(x_at, -1)
        x2 = scalar_inside(x_at, 2) + scalar_inside(x_at, -2)
        cls = jnp.where(e < 3, 0, jnp.where(e < 19, 1, 2))
        b = [cone_yz(av, t, (4, 28)) for t in range(2)]
        n1, p1 = z_next(b[0][1], b[1][1], lane), z_prev(b[0][1], b[1][1], lane)
        n2, p2 = z_next(b[0][2], b[1][2], lane, 2), z_prev(b[0][2], b[1][2], lane, 2)
        weights = x_parts(x0, x1, x2)
        for t in range(2):
            cone = b[t][0] + (n1[t] + p1[t]) + (n2[t] + p2[t])
            ws = None
            for n, wk in enumerate(weights.values()):
                ws = qk[n, t] * wk if ws is None else ws + qk[n, t] * wk
            inv = 1.0 / jnp.maximum(ws, 1.0)
            th = jnp.tanh(sharpness * (cone * inv - threshold))
            dens = (LIFT + th) * f32(1.0 / SCALE)
            flag = fl[cls, t]
            sq = dens * dens
            mo[e, t] = (young_floor + sq * dens * (1.0 - young_floor)) * flag
            gfs[t][e] = sq * flag * (1.0 - th * th) * inv * f32(-3.0 * (1.0 - young_floor) * sharpness / SCALE)
            if t == 0:
                av[0, 0, 0:24] = dens

        @pl.when((e >= 3) & (e < 19))
        def _():
            dens_ref[e - 3] = av[0, 0, 4:20]

        return 0

    lax.fori_loop(first, last, step, 0)


def operate_planes(first, last, nx, rs, mo, cl, qs, zt, tt, gp, yp, yg):
    lane = lane_of((WIN, 128))
    i_x = lax.axis_index(GX)
    gp[...] = jnp.zeros((12, 2, 24, 128), jnp.float32)
    zy_plane(lambda c, t: rs[t][c, first], zt, tt, first & 1, lane)

    def step(e, _):
        new, old = (e + 1) & 1, e & 1
        zy_plane(lambda c, t: rs[t][c, e + 1], zt, tt, new, lane)
        for t in range(2):
            for b in range(3):
                rows = slice(8 * b, 8 * b + 8)
                force = forces_of(modal_of(read_t(tt, old, t, b), read_t(tt, new, t, b)), mo[e, t, rows])
                for c in range(3):
                    for pz in range(2):
                        n = []
                        for py in range(2):
                            fd = force[c, (1, py, pz)]
                            fs = force.get((c, (0, py, pz)))
                            at = 4 * c + 2 * pz + py
                            before = gp[at, t, rows]
                            if fs is None:
                                gp[at, t, rows] = fd
                                n.append(before - fd)
                            else:
                                gp[at, t, rows] = fs + fd
                                n.append((fs - fd) + before)
                        yp[2 * c + pz, t, rows] = n[0] - n[1]
                        yg[2 * c + pz, t, 8 + 8 * b : 16 + 8 * b] = n[0] + n[1]

        @pl.when(e > first)
        def _():
            x_on = jnp.where(i_x * NXL + e - 3 < nx, 1.0, 0.0)
            for c in range(3):
                p, g = [], []
                for t in range(2):
                    zs = yp[2 * c, t] + yg[2 * c, t, 7:31]
                    zd = yp[2 * c + 1, t] + yg[2 * c + 1, t, 7:31]
                    p.append(zs - zd)
                    g.append(zs + zd)
                gb = z_prev(g[0], g[1], lane)
                for t in range(2):
                    value = p[t] + gb[t] + rs[t][c, e] * spring_rate
                    qs[t][c, e - 1] = value * (cl[t] * x_on)

        return 0

    lax.fori_loop(first, last, step, 0)


def sum_planes(first, last, acc, rs, qs, mo, zt, tt):
    lane = lane_of((WIN, 128))
    zy_plane(lambda c, t: qs[t][c, first + 2], zt, tt, first & 1, lane, tiles=1, base=4, blocks=2)

    def step(x, acc):
        s0, s1, s2, s3 = acc
        new, old = (x + 1) & 1, x & 1
        zy_plane(lambda c, t: qs[t][c, x + 3], zt, tt, new, lane, tiles=1, base=4, blocks=2)
        for b in range(2):
            rows = slice(4 + 8 * b, 12 + 8 * b)
            for c in range(3):
                r, q = rs[0][c, x + 3, rows], qs[0][c, x + 2, rows]
                s0, s1, s2 = s0 + r * r, s1 + r * q, s2 + q * q
            m = modal_of(read_t(tt, old, 0, b), read_t(tt, new, 0, b))
            s3 = s3 + energy_of(m) * mo[x + 3, 0, rows]
        return s0, s1, s2, s3

    return lax.fori_loop(first, last, step, acc)


def clear_edges(zt, yg):
    zt[:, :, 24:32] = jnp.zeros((6, 2, 8, 128), jnp.float32)
    yg[:, :, 0:8] = jnp.zeros((6, 2, 8, 128), jnp.float32)


def inner_kernel(
    rx, rxt, dx, qk, fl, cl, mo, gf, gft, dens_ref, qx, qxt, acc_ref, av, zt, tt, gp, yp, yg, *, sizes
):
    nx = sizes[0]
    clear_edges(zt, yg)
    density_planes(5, 17, nx, dx, qk, fl, av, mo, (gf, gft), dens_ref)
    operate_planes(5, 17, nx, (rx, rxt), mo, cl, (qx, qxt), zt, tt, gp, yp, yg)
    zero = jnp.zeros((8, 128), jnp.float32)
    for n, part in enumerate(sum_planes(3, 13, (zero,) * 4, (rx, rxt), (qx, qxt), mo, zt, tt)):
        acc_ref[n] = part


def outer_kernel(
    rx_in, rxt_in, dx_in, mo_in, gf_in, gft_in, dens_in, qx_in, qxt_in, acc_ref, xlo_ref, xhi_ref, qk, fl, cl,
    rx, rxt, dx, mo, gf, gft, dens_ref, qx, qxt, rp, qp, gpk, sum_ref, av, zt, tt, gp, yp, yg, *, sizes
):
    del rx_in, rxt_in, dx_in, mo_in, gf_in, gft_in, dens_in, qx_in, qxt_in
    nx = sizes[0]
    rs, qs, gfs = (rx, rxt), (qx, qxt), (gf, gft)
    clear_edges(zt, yg)
    x_halos(xlo_ref, xhi_ref, rx, rxt, dx)
    density_planes(0, 5, nx, dx, qk, fl, av, mo, gfs, dens_ref)
    density_planes(17, 22, nx, dx, qk, fl, av, mo, gfs, dens_ref)
    operate_planes(0, 6, nx, rs, mo, cl, qs, zt, tt, gp, yp, yg)
    operate_planes(16, 22, nx, rs, mo, cl, qs, zt, tt, gp, yp, yg)
    acc = tuple(acc_ref[n] for n in range(4))
    acc = sum_planes(0, 3, acc, rs, qs, mo, zt, tt)
    acc = sum_planes(13, 16, acc, rs, qs, mo, zt, tt)
    line = jnp.zeros((8, 128), jnp.float32)
    lane = lane_of((8, 128))
    for n, part in enumerate(acc):
        total = jnp.sum(jnp.sum(part, axis=0, keepdims=True), axis=1, keepdims=True)
        line = jnp.where(lane == n, total, line)
    sum_ref[...] = line

    def pack_step(j, _):
        for c in range(3):
            rp[c, j] = pack_chunks([(rx[c, 4 * k + j + 1], rxt[c, 4 * k + j + 1]) for k in range(4)])
            qp[c, j] = pack_chunks([(qx[c, 4 * k + j], qxt[c, 4 * k + j]) for k in range(4)])
        return 0

    lax.fori_loop(0, 9, pack_step, 0)

    def pack_weights(j, _):
        gpk[j] = pack_chunks([(gf[4 * k + j + 1], gft[4 * k + j + 1]) for k in range(4)])
        return 0

    lax.fori_loop(0, 8, pack_weights, 0)


def pack_chunks(tiles):
    lane = lane_of((WIN, 128))
    out = None
    for k, (main, side) in enumerate(tiles):
        high = roll(jnp.where(lane >= 64, main, side), 32 * k + 4)
        low = roll(jnp.where(lane >= 64, side, main), 32 * k + 28)
        out = high if out is None else jnp.where(lane >= 32 * k, high, out)
        out = jnp.where(lane >= 32 * k + 16, low, out)
    return out


def cross_energy(m, o):
    total = None
    for first, second, pick in (
        (K["a"] - K["b"], K["b"], lambda c: mode(c)),
        (K["p"] - K["r"], K["r"], lambda c: mode(*{0, 1, 2} - {c})),
    ):
        vm, vo = [m[c, pick(c)] for c in range(3)], [o[c, pick(c)] for c in range(3)]
        sm, so = vm[0] + vm[1] + vm[2], vo[0] + vo[1] + vo[2]
        part = (vm[0] * vo[0] + vm[1] * vo[1] + vm[2] * vo[2]) * f32(first) + sm * so * f32(second)
        total = part if total is None else total + part
    shear = None
    for c, e2 in ((0, 1), (0, 2), (1, 2)):
        v = (m[c, mode(e2)] + m[e2, mode(c)]) * (o[c, mode(e2)] + o[e2, mode(c)])
        shear = v if shear is None else shear + v
    triple = None
    for c in range(3):
        v = m[c, (1, 1, 1)] * o[c, (1, 1, 1)]
        triple = v if triple is None else triple + v
    same = cross = None
    for e2 in range(3):
        c, d = [i for i in range(3) if i != e2]
        m1, m2 = m[c, mode(c, e2)], m[d, mode(d, e2)]
        o1, o2 = o[c, mode(c, e2)], o[d, mode(d, e2)]
        sq, cr = m1 * o1 + m2 * o2, m1 * o2 + m2 * o1
        same = sq if same is None else same + sq
        cross = cr if cross is None else cross + cr
    total = total + shear * f32(K["g"]) + triple * f32(K["h"])
    return total + same * f32(K["c"]) + cross * f32(K["d"])


def tail_kernel(rx, qx, gf, rp, qp, gpk, dens_in, out_ref, dens_ref, px, pp, zt, tr, tq, av, ap, bp):
    dens_ref[...] = dens_in[...]
    lane = lane_of((WIN, 128))
    edge = lane == 127
    zt[:, :, 24:32] = jnp.zeros((6, 2, 8, 128), jnp.float32)

    def half_plane(at, after, t_ref, slot):
        for c in range(3):
            a = at(c)
            n = after(c, a)
            zt[2 * c, 0, 0:24] = a + n
            zt[2 * c + 1, 0, 0:24] = n - a
        for f in range(6):
            for b in range(3):
                lo, hi = zt[f, 0, 8 * b : 8 * b + 8], zt[f, 0, 8 * b + 1 : 8 * b + 9]
                t_ref[slot, 2 * f, 0, 8 * b : 8 * b + 8] = lo + hi
                t_ref[slot, 2 * f + 1, 0, 8 * b : 8 * b + 8] = hi - lo

    def main_plane(i, slot):
        chunk = jnp.minimum(i >> 2, 3)
        j, shift = i - 4 * chunk, 123 - 32 * chunk

        def after(src):
            return lambda c, a: jnp.where(edge, pltpu.roll(src[c, j], shift, 1), roll(a, -1))

        half_plane(lambda c: rx[c, i + 1], after(rp), tr, slot)
        half_plane(lambda c: qx[c, i], after(qp), tq, slot)

    def end_plane(j, slot):
        half_plane(lambda c: rp[c, j], lambda c, a: roll(a, -1), tr, slot)
        half_plane(lambda c: qp[c, j], lambda c, a: roll(a, -1), tq, slot)

    def energies(i, g_ref, out):
        new, old = (i + 1) & 1, i & 1
        for b in range(3):
            rows = slice(8 * b, 8 * b + 8)
            m = modal_of(read_t(tr, old, 0, b), read_t(tr, new, 0, b))
            o = modal_of(read_t(tq, old, 0, b), read_t(tq, new, 0, b))
            g = g_ref[rows]
            out[0, i, rows] = energy_of(m) * g
            out[1, i, rows] = cross_energy(m, o) * (2.0 * g)
            out[2, i, rows] = energy_of(o) * g

    def main_step(i, _):
        main_plane(i + 1, (i + 1) & 1)
        energies(i, gf.at[i + 1], px)
        return 0

    def end_step(j, _):
        end_plane(j + 1, (j + 1) & 1)
        energies(j, gpk.at[j], pp)
        return 0

    main_plane(jnp.int32(0), 0)
    lax.fori_loop(0, 20, main_step, 0)
    end_plane(0, 0)
    lax.fori_loop(0, 8, end_step, 0)

    def parts_of(src, k, x, dst):
        f0 = src[k, x + 2]
        f1 = src[k, x + 1] + src[k, x + 3]
        f2 = src[k, x] + src[k, x + 4]
        for n, part in enumerate(x_parts(f0, f1, f2).values()):
            dst[k, n, 0, 0:24] = part

    def end_cone(j, _):
        for k in range(3):
            parts_of(pp, k, j, ap)
            b = cone_yz(ap.at[k], 0, (4, 20))
            bp[k, j, 0] = b[1]
            bp[k, j, 1] = b[2]
        return 0

    lax.fori_loop(0, 4, end_cone, 0)
    lane16 = lane_of((NYL, 128))
    for chunk in range(4):

        def cone_step(j, _):
            x = 4 * chunk + j
            for k in range(3):
                parts_of(px, k, x, av)
                b0, b1, b2 = cone_yz(av.at[k], 0, (4, 20))
                e1, e2 = bp[k, j, 0], bp[k, j, 1]
                n1 = jnp.where(lane16 == 127, roll(e1, 123 - 32 * chunk), roll(b1, -1))
                p1 = jnp.where(lane16 == 0, roll(e1, -(32 * chunk + 27)), roll(b1, 1))
                n2 = jnp.where(lane16 >= 126, roll(e2, 122 - 32 * chunk), roll(b2, -2))
                p2 = jnp.where(lane16 < 2, roll(e2, -(32 * chunk + 26)), roll(b2, 2))
                out_ref[k, x] = b0 + (n1 + p1) + (n2 + p2)
            return 0

        lax.fori_loop(0, 4, cone_step, 0)


def final_kernel(sum_ref, rx, qx, cones, disp_ref, sens_ref):
    line = jnp.sum(sum_ref[...], axis=0, keepdims=True)
    lane1 = lane_of((1, 128))
    m0, m1, m2, m3 = [jnp.sum(jnp.where(lane1 == n, line, 0.0), axis=1, keepdims=True) for n in range(4)]
    m3 = m3 + spring_rate * m2
    first = m0 / m1
    norm = m0 - 2.0 * first * m1 + first * first * m2
    grown = 1.0 + norm / m0
    second = norm / (grown * grown * m1 - 2.0 * first * grown * m2 + first * first * m3)
    c0 = jnp.broadcast_to(first + second * grown, (NYL, 128))
    c1 = jnp.broadcast_to(-second * first, (NYL, 128))

    def step(x, _):
        for c in range(3):
            disp_ref[c, x] = c0 * rx[c, x + 3, 4:20] + c1 * qx[c, x + 2, 4:20]
        sens_ref[x] = c0 * (c0 * cones[0, x] + c1 * cones[1, x]) + c1 * c1 * cones[2, x]
        return 0

    lax.fori_loop(0, 16, step, 0)


def s(*shape):
    return jax.ShapeDtypeStruct(shape, jnp.float32)


def v(*shape):
    return pltpu.VMEM(shape, jnp.float32)


def call(kernel, outs, scratch, *args, smem=0, hbm=0, flush=(), **kw):
    spec_s, spec_v = pl.BlockSpec(memory_space=pltpu.SMEM), pl.BlockSpec(memory_space=pltpu.VMEM)
    single = not isinstance(outs, (tuple, list))
    outs = [outs] if single else list(outs)
    if not INTERPRET:
        outs = [o if i in flush else pltpu.VMEM(o.shape, o.dtype) for i, o in enumerate(outs)]
        args = [
            a if i < smem else pltpu.with_memory_space_constraint(a, pltpu.HBM if i < smem + hbm else pltpu.VMEM)
            for i, a in enumerate(args)
        ]
    return pl.pallas_call(
        kernel,
        out_shape=outs[0] if single else outs,
        in_specs=[spec_s] * smem
        + [pl.BlockSpec(memory_space=pltpu.HBM)] * hbm
        + [spec_v] * (len(args) - smem - hbm),
        out_specs=spec_v if single else [spec_v] * len(outs),
        scratch_shapes=scratch,
        interpret=INTERPRET,
        compiler_params=pltpu.CompilerParams(vmem_limit_bytes=24 << 20),
        **kw,
    )(*args)


def moved(block, axis, step):
    count = lax.axis_size(axis)
    return lax.ppermute(block, axis, [(i, i - step) for i in range(count) if 0 <= i - step < count])


def body(load, design, solid_map):
    sizes = tuple(lax.axis_size(a) * n for a, n in zip(ALL, (NXL, NYL, NZL)))
    others = ("gx_0", "gy", "gz")

    def sized(kernel):
        return lambda *refs: kernel(*refs, sizes=sizes)

    load, design, zc = call(
        pack_z_kernel, (s(3, 16, 16, 128), s(16, 16, 128), s(8, 16, 128)), [pltpu.SemaphoreType.DMA((4,))],
        load, design, hbm=2,
    )
    zhi, zlo = moved(zc, "gz", 1), moved(zc, "gz", -1)
    qk, fl, cl = call(
        sized(place_kernel), (s(6, 2, 24, 128), s(3, 2, 24, 128), s(2, 24, 128)), [], solid_map, zc, smem=1
    )
    ylo_s, yhi_s = call(pack_y_kernel, (s(39, 8, 128), s(39, 8, 128)), [], load, design, zhi, zlo, cl)
    yhi, ylo = moved(ylo_s, "gy", 1), moved(yhi_s, "gy", -1)
    rx_t, dx_t, mo_t, gf_t = s(3, 23, 24, 128), s(26, 2, 32, 128), s(22, 2, 24, 128), s(22, 24, 128)
    dens_t, qx_t = s(16, 16, 128), s(3, 21, 24, 128)
    rx, rxt, dx, xlo_s, xhi_s = call(
        pack_x_kernel, (rx_t, rx_t, dx_t, s(544, 128), s(472, 128)), [v(8, 32, 128)],
        load, design, zhi, zlo, ylo, yhi,
    )
    xhi, xlo = moved(xlo_s, GX, 1), moved(xhi_s, GX, -1)
    scratch = [
        v(6, 2, 32, 128), v(6, 2, 32, 128), v(2, 12, 2, 24, 128), v(12, 2, 24, 128), v(6, 2, 24, 128), v(6, 2, 32, 128),
    ]
    mo, gf, gft, dens, qx, qxt, acc = call(
        sized(inner_kernel), (mo_t, gf_t, gf_t, dens_t, qx_t, qx_t, s(4, 8, 128)), scratch, rx, rxt, dx, qk, fl, cl
    )
    held = rx_t, rx_t, dx_t, mo_t, gf_t, gf_t, dens_t, qx_t, qx_t
    rx, _, _, _, gf, _, dens, qx, _, rp, qp, gpk, part = call(
        sized(outer_kernel),
        (*held, s(3, 9, 24, 128), s(3, 9, 24, 128), s(8, 24, 128), s(8, 128)), scratch,
        rx, rxt, dx, mo, gf, gft, dens, qx, qxt, acc, xlo, xhi, qk, fl, cl,
        input_output_aliases={n: n for n in range(len(held))},
    )
    pair = lax.axis_size("gx_1")
    for step in range(1, pair):
        part = part + lax.ppermute(part, "gx_1", [(i, (i + step) % pair) for i in range(pair)])
    part = jnp.broadcast_to(part[:1], (math.prod(lax.axis_size(a) for a in others), 128))
    sums = lax.all_to_all(part, others, 0, 0, tiled=True)
    cones, dens = call(
        tail_kernel, (s(3, 16, 16, 128), dens_t),
        [
            v(3, 20, 24, 128), v(3, 8, 24, 128), v(6, 2, 32, 128), v(2, 12, 1, 24, 128), v(2, 12, 1, 24, 128),
            v(3, 6, 1, 32, 128), v(3, 6, 1, 32, 128), v(3, 4, 2, 16, 128),
        ],
        rx, qx, gf, rp, qp, gpk, dens, flush=(1,),
    )
    disp, sens = call(
        final_kernel, (s(3, 16, 16, 128), s(16, 16, 128)), [], sums, rx, qx, cones, flush=(0, 1)
    )
    return disp, sens, dens


def solution(mesh):
    cores = 2
    split = Mesh(
        mesh.devices.reshape(mesh.shape["gx"] // cores, cores, mesh.shape["gy"], mesh.shape["gz"]),
        (*GX, "gy", "gz"),
    )
    nodal, cell = P(None, GX, "gy", "gz"), P(GX, "gy", "gz")
    return jax.shard_map(
        body, mesh=split, in_specs=(nodal, cell, P()), out_specs=(nodal, cell, cell), check_vma=False
    )
```

```python
import math

import jax
import jax.numpy as jnp
import numpy as np
from jax import lax
from jax.experimental import pallas as pl
from jax.experimental.pallas import tpu as pltpu
from jax.sharding import Mesh
from jax.sharding import PartitionSpec as P


BRICK = 16
young_floor = 0.001
spring_rate = 0.05
sharpness = 8.0
threshold = 0.5
poisson = 0.3
GX = ("gx_0", "gx_1")
ALL = (GX, "gy", "gz")
INTERPRET = False

NXL, NYL, NZL = 16, 16, 128
WIN = 24


def element_matrix():
    lame_first = poisson / ((1.0 + poisson) * (1.0 - 2.0 * poisson))
    shear_mod = 1.0 / (2.0 * (1.0 + poisson))
    elastic = np.zeros((6, 6))
    elastic[:3, :3] = lame_first
    for axis_one in range(3):
        elastic[axis_one, axis_one] += 2.0 * shear_mod
        elastic[axis_one + 3, axis_one + 3] = shear_mod
    gauss_point = 1.0 / math.sqrt(3.0)
    stiffness = np.zeros((24, 24))
    for point_x in (-gauss_point, gauss_point):
        for point_y in (-gauss_point, gauss_point):
            for point_z in (-gauss_point, gauss_point):
                strain = np.zeros((6, 24))
                for corner in range(8):
                    sign_a = 2 * (corner // 4) - 1
                    sign_b = 2 * (corner // 2 % 2) - 1
                    sign_c = 2 * (corner % 2) - 1
                    along_x = 0.25 * sign_a * (1 + sign_b * point_y) * (1 + sign_c * point_z)
                    along_y = 0.25 * (1 + sign_a * point_x) * sign_b * (1 + sign_c * point_z)
                    along_z = 0.25 * (1 + sign_a * point_x) * (1 + sign_b * point_y) * sign_c
                    column = 3 * corner
                    strain[0, column] = along_x
                    strain[1, column + 1] = along_y
                    strain[2, column + 2] = along_z
                    strain[3, column + 1] = along_z
                    strain[3, column + 2] = along_y
                    strain[4, column] = along_z
                    strain[4, column + 2] = along_x
                    strain[5, column] = along_y
                    strain[5, column + 1] = along_x
                stiffness += strain.T @ elastic @ strain * 0.125
    return stiffness


def modal_constants():
    modes = [(px, py, pz) for px in (0, 1) for py in (0, 1) for pz in (0, 1)]
    change = np.zeros((24, 24))
    for c in range(3):
        for m, mode in enumerate(modes):
            for q in range(8):
                corner = (q // 4, q // 2 % 2, q % 2)
                sign = 1.0
                for axis in range(3):
                    if mode[axis] and not corner[axis]:
                        sign = -sign
                change[8 * c + m, 3 * q + c] = sign
    hat = change @ element_matrix() @ change.T / 64.0

    def at(c1, m1, c2, m2):
        return hat[8 * c1 + modes.index(m1), 8 * c2 + modes.index(m2)]

    k = {
        "a": at(0, (1, 0, 0), 0, (1, 0, 0)),
        "b": at(0, (1, 0, 0), 1, (0, 1, 0)),
        "p": at(0, (0, 1, 1), 0, (0, 1, 1)),
        "r": at(0, (0, 1, 1), 1, (1, 0, 1)),
        "g": at(0, (0, 1, 0), 1, (1, 0, 0)),
        "h": at(2, (1, 1, 1), 2, (1, 1, 1)),
        "c": at(1, (1, 1, 0), 1, (1, 1, 0)),
        "d": at(1, (1, 1, 0), 2, (1, 0, 1)),
    }
    made = np.zeros((24, 24))

    def put(c1, m1, c2, m2, v):
        made[8 * c1 + modes.index(m1), 8 * c2 + modes.index(m2)] += v

    for c in range(3):
        unit = tuple(int(i == c) for i in range(3))
        anti = tuple(int(i != c) for i in range(3))
        put(c, (1, 1, 1), c, (1, 1, 1), k["h"])
        for e in range(3):
            unit_e = tuple(int(i == e) for i in range(3))
            anti_e = tuple(int(i != e) for i in range(3))
            put(c, unit, e, unit_e, k["a"] if c == e else k["b"])
            put(c, anti, e, anti_e, k["p"] if c == e else k["r"])
            if c != e:
                put(c, unit_e, c, unit_e, k["g"])
                put(c, unit_e, e, unit, k["g"])
                both = tuple(int(i in (c, e)) for i in range(3))
                o = 3 - c - e
                both_o = tuple(int(i in (o, e)) for i in range(3))
                put(c, both, c, both, k["c"])
                put(c, both, o, both_o, k["d"])
    assert np.abs(made - hat).max() < 1e-12
    return k


K = modal_constants()
W = {n: 3.0 - math.sqrt(n) for n in range(9)}
KS = (0, 1, 2, 4, 5, 8)


def mode(*axes):
    return tuple(int(i in axes) for i in range(3))


def f32(x):
    return float(np.float32(x))


def roll(x, shift):
    shift = shift % 128
    return x if shift == 0 else pltpu.roll(x, shift, 1)


def lane_of(shape):
    return lax.broadcasted_iota(jnp.int32, shape, 1)


def z_next(a0, a1, lane, by=1):
    r0, r1 = roll(a0, -by), roll(a1, -by)
    edge = lane >= 128 - by
    return jnp.where(edge, r1, r0), jnp.where(edge, r0, r1)


def z_prev(a0, a1, lane, by=1):
    r0, r1 = roll(a0, by), roll(a1, by)
    edge = lane < by
    return jnp.where(edge, r1, r0), jnp.where(edge, r0, r1)


def modal_of(lo, hi):
    m = {}
    for (c, py, pz), low in lo.items():
        high = hi[c, py, pz]
        if py or pz:
            m[c, (0, py, pz)] = low + high
        m[c, (1, py, pz)] = high - low
    return m


def forces_of(m, e):
    ea, eb = e * f32(K["a"] - K["b"]), e * f32(K["b"])
    ep, er = e * f32(K["p"] - K["r"]), e * f32(K["r"])
    eg, eh = e * f32(K["g"]), e * f32(K["h"])
    ec, ed = e * f32(K["c"]), e * f32(K["d"])
    f = {}
    for first, second, pick in ((ea, eb, lambda c: mode(c)), (ep, er, lambda c: mode(*{0, 1, 2} - {c}))):
        vals = [m[c, pick(c)] for c in range(3)]
        shared = (vals[0] + vals[1] + vals[2]) * second
        for c in range(3):
            f[c, pick(c)] = vals[c] * first + shared
    for c, e2 in ((0, 1), (0, 2), (1, 2)):
        shared = (m[c, mode(e2)] + m[e2, mode(c)]) * eg
        f[c, mode(e2)] = shared
        f[e2, mode(c)] = shared
    for c in range(3):
        f[c, (1, 1, 1)] = m[c, (1, 1, 1)] * eh
    for e2 in range(3):
        c, o = [i for i in range(3) if i != e2]
        v1, v2 = m[c, mode(c, e2)], m[o, mode(o, e2)]
        f[c, mode(c, e2)] = v1 * ec + v2 * ed
        f[o, mode(o, e2)] = v2 * ec + v1 * ed
    return f


def energy_of(m):
    total = None
    for first, second, pick in (
        (K["a"] - K["b"], K["b"], lambda c: mode(c)),
        (K["p"] - K["r"], K["r"], lambda c: mode(*{0, 1, 2} - {c})),
    ):
        vals = [m[c, pick(c)] for c in range(3)]
        s = vals[0] + vals[1] + vals[2]
        part = (vals[0] * vals[0] + vals[1] * vals[1] + vals[2] * vals[2]) * f32(first) + s * s * f32(second)
        total = part if total is None else total + part
    shear = None
    for c, e2 in ((0, 1), (0, 2), (1, 2)):
        s = m[c, mode(e2)] + m[e2, mode(c)]
        shear = s * s if shear is None else shear + s * s
    total = total + shear * f32(K["g"])
    triple = None
    for c in range(3):
        v = m[c, (1, 1, 1)]
        triple = v * v if triple is None else triple + v * v
    total = total + triple * f32(K["h"])
    squares = cross = None
    for e2 in range(3):
        c, o = [i for i in range(3) if i != e2]
        v1, v2 = m[c, mode(c, e2)], m[o, mode(o, e2)]
        sq, cr = v1 * v1 + v2 * v2, v1 * v2
        squares = sq if squares is None else squares + sq
        cross = cr if cross is None else cross + cr
    return total + squares * f32(K["c"]) + cross * f32(2.0 * K["d"])


def x_parts(f0, f1, f2):
    out = {}
    for k in KS:
        v = f0 * f32(W[k])
        if k + 1 in W:
            v = v + f1 * f32(W[k + 1])
        if k + 4 in W:
            v = v + f2 * f32(W[k + 4])
        out[k] = v
    return out


def pack_z_kernel(load_hbm, design_hbm, load_ref, design_ref, out_ref, sems):
    copies = [pltpu.make_async_copy(load_hbm.at[c], load_ref.at[c], sems.at[c]) for c in range(3)]
    copies.append(pltpu.make_async_copy(design_hbm, design_ref, sems.at[3]))
    for one in copies:
        one.start()
    for one in copies:
        one.wait()
    lane = lane_of((NYL, 128))

    def step(pair, _):
        acc = jnp.zeros((NYL, 128), jnp.float32)
        for par in range(2):
            for fld in range(4):
                off = 64 * par + 16 * fld
                src = load_ref[fld, 2 * pair + par] if fld < 3 else design_ref[2 * pair + par]
                acc = jnp.where(((lane - off + 8) & 127) < 16, roll(src, off), acc)
        out_ref[pair] = acc
        return 0

    lax.fori_loop(0, 8, step, 0)


def halo_merge(high, low):
    lane = lane_of(high.shape)
    return jnp.where((lane & 15) < 8, high, low)


def pack_y_kernel(load_ref, design_ref, zhi_ref, zlo_ref, place_ref, lo_ref, hi_ref):
    del place_ref
    for dst, quad, one in ((lo_ref, 0, 4), (hi_ref, 12, 11)):
        rows = slice(quad, quad + 4)
        for x in range(16):
            dst[x, 0:4] = load_ref[0, x, rows]
            dst[x, 4:8] = load_ref[1, x, rows]
            dst[16 + x, 0:4] = load_ref[2, x, rows]
            dst[16 + x, 4:8] = design_ref[x, rows]
            dst[32 + x // 8, x % 8 : x % 8 + 1] = design_ref[x, one : one + 1]
        for k in range(8):
            dst[35 + k // 2, 4 * (k % 2) : 4 * (k % 2) + 4] = halo_merge(zhi_ref[k, rows], zlo_ref[k, rows])
            dst[34, k : k + 1] = halo_merge(zhi_ref[k, one : one + 1], zlo_ref[k, one : one + 1])


def pack_x_kernel(load_ref, design_ref, zhi_ref, zlo_ref, ylo_ref, yhi_ref, rx, rxt, dx, lo_ref, hi_ref, hx):
    none = jnp.zeros((8, 128), jnp.float32)
    for k in range(8):
        half = slice(4 * (k % 2), 4 * (k % 2) + 4)
        hx[k, 0:8] = none
        hx[k, 24:32] = none
        hx[k, 3:4] = ylo_ref[34, k : k + 1]
        hx[k, 4:8] = ylo_ref[35 + k // 2, half]
        hx[k, 8:24] = halo_merge(zhi_ref[k], zlo_ref[k])
        hx[k, 24:28] = yhi_ref[35 + k // 2, half]
        hx[k, 28:29] = yhi_ref[34, k : k + 1]
    for x in range(16):
        for c in range(3):
            tile, half = (x, slice(4 * c, 4 * c + 4)) if c < 2 else (16 + x, slice(0, 4))
            rx[c, x + 3, 0:4] = ylo_ref[tile, half]
            rx[c, x + 3, 4:20] = load_ref[c, x]
            rx[c, x + 3, 20:24] = yhi_ref[tile, half]
        one = slice(x % 8, x % 8 + 1)
        dx[x + 5, 0, 0:8] = none
        dx[x + 5, 0, 24:32] = none
        dx[x + 5, 0, 3:4] = ylo_ref[32 + x // 8, one]
        dx[x + 5, 0, 4:8] = ylo_ref[16 + x, 4:8]
        dx[x + 5, 0, 8:24] = design_ref[x]
        dx[x + 5, 0, 24:28] = yhi_ref[16 + x, 4:8]
        dx[x + 5, 0, 28:29] = yhi_ref[32 + x // 8, one]
    for i in range(5):
        lo_ref[288 + 32 * i : 320 + 32 * i] = dx[5 + i, 0]
        hi_ref[216 + 32 * i : 248 + 32 * i] = dx[16 + i, 0]
    for i in range(3):
        lo_ref[448 + 32 * i : 480 + 32 * i] = hx[i]
        hi_ref[376 + 32 * i : 408 + 32 * i] = hx[5 + i]
    for c in range(3):
        for i in range(4):
            lo_ref[24 * (4 * c + i) : 24 * (4 * c + i) + 24] = rx[c, 3 + i]
        for i in range(3):
            hi_ref[24 * (3 * c + i) : 24 * (3 * c + i) + 24] = rx[c, 16 + i]
    for k in range(8):
        spread_pair(hx[k], 2 * k, (2 * k, 2 * k + 1), rxt, dx, True)


def spread_pair(tile, x, wanted, rxt, dx, both):
    for par in range(2):
        if x + par in wanted:
            dx[x + par + 5, 1] = roll(tile, -(64 * par + 48))
            if both or -3 <= x + par <= 19:
                for c in range(3):
                    rxt[c, x + par + 3] = roll(tile, -(64 * par + 16 * c))[4:28]


def x_halos(xlo_ref, xhi_ref, rx, rxt, dx):
    for c in range(3):
        for i in range(4):
            rx[c, 19 + i] = xhi_ref[24 * (4 * c + i) : 24 * (4 * c + i) + 24]
        for i in range(3):
            rx[c, i] = xlo_ref[24 * (3 * c + i) : 24 * (3 * c + i) + 24]
    for i in range(5):
        dx[21 + i, 0] = xhi_ref[288 + 32 * i : 320 + 32 * i]
        dx[i, 0] = xlo_ref[216 + 32 * i : 248 + 32 * i]
    for i in range(3):
        spread_pair(xhi_ref[448 + 32 * i : 480 + 32 * i], 16 + 2 * i, range(16, 21), rxt, dx, False)
        spread_pair(xlo_ref[376 + 32 * i : 408 + 32 * i], -6 + 2 * i, range(-5, 0), rxt, dx, False)


def place_kernel(map_ref, order_ref, qk, fl, cl, *, sizes):
    del order_ref
    nx, ny, nz = sizes
    i_x, i_y, i_z = (lax.axis_index(a) for a in ALL)
    lane = lane_of((WIN, 128))
    row = lax.broadcasted_iota(jnp.int32, (WIN, 128), 0)
    y_at = i_y * NYL + row - 4
    z_at = [i_z * NZL + lane, i_z * NZL + jnp.where(lane < 64, lane + 128, lane - 128)]

    def inside(at, step, length):
        return jnp.where((at + step >= 0) & (at + step < length), 1.0, 0.0)

    y_in = [inside(y_at, 0, ny)] + [inside(y_at, s, ny) + inside(y_at, -s, ny) for s in (1, 2)]
    for t in range(2):
        z_in = [inside(z_at[t], 0, nz)] + [inside(z_at[t], s, nz) + inside(z_at[t], -s, nz) for s in (1, 2)]
        qk[0, t] = y_in[0] * z_in[0]
        qk[1, t] = y_in[1] * z_in[0] + y_in[0] * z_in[1]
        qk[2, t] = y_in[1] * z_in[1]
        qk[3, t] = y_in[2] * z_in[0] + y_in[0] * z_in[2]
        qk[4, t] = y_in[1] * z_in[2] + y_in[2] * z_in[1]
        qk[5, t] = y_in[2] * z_in[2]
        cl[t] = y_in[0] * z_in[0]
    gbx, gby, gbz = nx // BRICK, ny // BRICK, nz // BRICK
    bricks = NZL // BRICK

    def flag_at(bx, by, bz):
        ok = (bx >= 0) & (bx < gbx) & (by >= 0) & (by < gby) & (bz >= 0) & (bz < gbz)
        value = map_ref[jnp.clip(bx, 0, gbx - 1), jnp.clip(by, 0, gby - 1), jnp.clip(bz, 0, gbz - 1)]
        return jnp.where(ok, value, 0).astype(jnp.float32)

    for xc in range(3):
        lines = []
        for yc in range(3):
            flag = [flag_at(i_x + xc - 1, i_y + yc - 1, i_z * bricks + n - 1) for n in range(bricks + 2)]
            main = jnp.zeros((WIN, 128), jnp.float32)
            for n in range(bricks):
                main = jnp.where((lane >> 4) == n, flag[n + 1], main)
            lines.append((main, jnp.where(lane < 64, flag[bricks + 1], flag[0])))
        for t in range(2):
            fl[xc, t] = jnp.where(row < 4, lines[0][t], jnp.where(row < 20, lines[1][t], lines[2][t]))


def zy_plane(tile, zt, t_ref, slot, lane, tiles=2, base=0, blocks=3):
    for c in range(3):
        a0, a1 = tile(c, 0), tile(c, 1)
        n0, n1 = z_next(a0, a1, lane)
        zt[2 * c, 0, 0:24] = a0 + n0
        zt[2 * c + 1, 0, 0:24] = n0 - a0
        if tiles == 2:
            zt[2 * c, 1, 0:24] = a1 + n1
            zt[2 * c + 1, 1, 0:24] = n1 - a1
    for f in range(6):
        for t in range(tiles):
            for b in range(blocks):
                r = base + 8 * b
                lo, hi = zt[f, t, r : r + 8], zt[f, t, r + 1 : r + 9]
                t_ref[slot, 2 * f, t, 8 * b : 8 * b + 8] = lo + hi
                t_ref[slot, 2 * f + 1, t, 8 * b : 8 * b + 8] = hi - lo


def read_t(t_ref, slot, t, b):
    out = {}
    for c in range(3):
        for pz in range(2):
            for py in range(2):
                out[c, py, pz] = t_ref[slot, 4 * c + 2 * pz + py, t, 8 * b : 8 * b + 8]
    return out


LIFT = math.tanh(sharpness * threshold)
SCALE = LIFT + math.tanh(sharpness * (1.0 - threshold))


def cone_yz(av, t, rows):
    lo, hi = rows

    def at(n, step):
        return av[n, t, lo + step : hi + step]

    def both(n, step):
        return at(n, -step) + at(n, step)

    return [
        at(0, 0) + both(1, 1) + both(3, 2),
        at(1, 0) + both(2, 1) + both(4, 2),
        at(3, 0) + both(4, 1) + both(5, 2),
    ]


def density_planes(first, last, nx, dx, qk, fl, av, mo, gfs, dens_ref):
    lane = lane_of((WIN, 128))
    i_x = lax.axis_index(GX)

    def scalar_inside(at, step):
        return jnp.where((at + step >= 0) & (at + step < nx), 1.0, 0.0)

    def step(e, _):
        for t in range(2):
            f0 = dx[e + 2, t]
            f1 = dx[e + 1, t] + dx[e + 3, t]
            f2 = dx[e, t] + dx[e + 4, t]
            for n, part in enumerate(x_parts(f0, f1, f2).values()):
                av[n, t] = part
        x_at = i_x * NXL + e - 3
        x0 = scalar_inside(x_at, 0)
        x1 = scalar_inside(x_at, 1) + scalar_inside(x_at, -1)
        x2 = scalar_inside(x_at, 2) + scalar_inside(x_at, -2)
        cls = jnp.where(e < 3, 0, jnp.where(e < 19, 1, 2))
        b = [cone_yz(av, t, (4, 28)) for t in range(2)]
        n1, p1 = z_next(b[0][1], b[1][1], lane), z_prev(b[0][1], b[1][1], lane)
        n2, p2 = z_next(b[0][2], b[1][2], lane, 2), z_prev(b[0][2], b[1][2], lane, 2)
        weights = x_parts(x0, x1, x2)
        for t in range(2):
            cone = b[t][0] + (n1[t] + p1[t]) + (n2[t] + p2[t])
            ws = None
            for n, wk in enumerate(weights.values()):
                ws = qk[n, t] * wk if ws is None else ws + qk[n, t] * wk
            inv = 1.0 / jnp.maximum(ws, 1.0)
            th = jnp.tanh(sharpness * (cone * inv - threshold))
            dens = (LIFT + th) * f32(1.0 / SCALE)
            flag = fl[cls, t]
            sq = dens * dens
            mo[e, t] = (young_floor + sq * dens * (1.0 - young_floor)) * flag
            gfs[t][e] = sq * flag * (1.0 - th * th) * inv * f32(-3.0 * (1.0 - young_floor) * sharpness / SCALE)
            if t == 0:
                av[0, 0, 0:24] = dens

        @pl.when((e >= 3) & (e < 19))
        def _():
            dens_ref[e - 3] = av[0, 0, 4:20]

        return 0

    lax.fori_loop(first, last, step, 0)


def operate_planes(first, last, nx, rs, mo, cl, qs, zt, tt, gp, yp, yg):
    lane = lane_of((WIN, 128))
    i_x = lax.axis_index(GX)
    gp[...] = jnp.zeros((12, 2, 24, 128), jnp.float32)
    zy_plane(lambda c, t: rs[t][c, first], zt, tt, first & 1, lane)

    def step(e, _):
        new, old = (e + 1) & 1, e & 1
        zy_plane(lambda c, t: rs[t][c, e + 1], zt, tt, new, lane)
        for t in range(2):
            for b in range(3):
                rows = slice(8 * b, 8 * b + 8)
                force = forces_of(modal_of(read_t(tt, old, t, b), read_t(tt, new, t, b)), mo[e, t, rows])
                for c in range(3):
                    for pz in range(2):
                        n = []
                        for py in range(2):
                            fd = force[c, (1, py, pz)]
                            fs = force.get((c, (0, py, pz)))
                            at = 4 * c + 2 * pz + py
                            before = gp[at, t, rows]
                            if fs is None:
                                gp[at, t, rows] = fd
                                n.append(before - fd)
                            else:
                                gp[at, t, rows] = fs + fd
                                n.append((fs - fd) + before)
                        yp[2 * c + pz, t, rows] = n[0] - n[1]
                        yg[2 * c + pz, t, 8 + 8 * b : 16 + 8 * b] = n[0] + n[1]

        @pl.when(e > first)
        def _():
            x_on = jnp.where(i_x * NXL + e - 3 < nx, 1.0, 0.0)
            for c in range(3):
                p, g = [], []
                for t in range(2):
                    zs = yp[2 * c, t] + yg[2 * c, t, 7:31]
                    zd = yp[2 * c + 1, t] + yg[2 * c + 1, t, 7:31]
                    p.append(zs - zd)
                    g.append(zs + zd)
                gb = z_prev(g[0], g[1], lane)
                for t in range(2):
                    value = p[t] + gb[t] + rs[t][c, e] * spring_rate
                    qs[t][c, e - 1] = value * (cl[t] * x_on)

        return 0

    lax.fori_loop(first, last, step, 0)


def sum_planes(first, last, acc, rs, qs, mo, zt, tt):
    lane = lane_of((WIN, 128))
    zy_plane(lambda c, t: qs[t][c, first + 2], zt, tt, first & 1, lane, tiles=1, base=4, blocks=2)

    def step(x, acc):
        s0, s1, s2, s3 = acc
        new, old = (x + 1) & 1, x & 1
        zy_plane(lambda c, t: qs[t][c, x + 3], zt, tt, new, lane, tiles=1, base=4, blocks=2)
        for b in range(2):
            rows = slice(4 + 8 * b, 12 + 8 * b)
            for c in range(3):
                r, q = rs[0][c, x + 3, rows], qs[0][c, x + 2, rows]
                s0, s1, s2 = s0 + r * r, s1 + r * q, s2 + q * q
            m = modal_of(read_t(tt, old, 0, b), read_t(tt, new, 0, b))
            s3 = s3 + energy_of(m) * mo[x + 3, 0, rows]
        return s0, s1, s2, s3

    return lax.fori_loop(first, last, step, acc)


def clear_edges(zt, yg):
    zt[:, :, 24:32] = jnp.zeros((6, 2, 8, 128), jnp.float32)
    yg[:, :, 0:8] = jnp.zeros((6, 2, 8, 128), jnp.float32)


def inner_kernel(
    rx, rxt, dx, qk, fl, cl, mo, gf, gft, dens_ref, qx, qxt, acc_ref, av, zt, tt, gp, yp, yg, *, sizes
):
    nx = sizes[0]
    clear_edges(zt, yg)
    density_planes(5, 17, nx, dx, qk, fl, av, mo, (gf, gft), dens_ref)
    operate_planes(5, 17, nx, (rx, rxt), mo, cl, (qx, qxt), zt, tt, gp, yp, yg)
    zero = jnp.zeros((8, 128), jnp.float32)
    for n, part in enumerate(sum_planes(3, 13, (zero,) * 4, (rx, rxt), (qx, qxt), mo, zt, tt)):
        acc_ref[n] = part


def outer_kernel(
    rx_in, rxt_in, dx_in, mo_in, gf_in, gft_in, dens_in, qx_in, qxt_in, acc_ref, xlo_ref, xhi_ref, qk, fl, cl,
    rx, rxt, dx, mo, gf, gft, dens_ref, qx, qxt, rp, qp, gpk, sum_ref, av, zt, tt, gp, yp, yg, *, sizes
):
    del rx_in, rxt_in, dx_in, mo_in, gf_in, gft_in, dens_in, qx_in, qxt_in
    nx = sizes[0]
    rs, qs, gfs = (rx, rxt), (qx, qxt), (gf, gft)
    clear_edges(zt, yg)
    x_halos(xlo_ref, xhi_ref, rx, rxt, dx)
    density_planes(0, 5, nx, dx, qk, fl, av, mo, gfs, dens_ref)
    density_planes(17, 22, nx, dx, qk, fl, av, mo, gfs, dens_ref)
    operate_planes(0, 6, nx, rs, mo, cl, qs, zt, tt, gp, yp, yg)
    operate_planes(16, 22, nx, rs, mo, cl, qs, zt, tt, gp, yp, yg)
    acc = tuple(acc_ref[n] for n in range(4))
    acc = sum_planes(0, 3, acc, rs, qs, mo, zt, tt)
    acc = sum_planes(13, 16, acc, rs, qs, mo, zt, tt)
    line = jnp.zeros((8, 128), jnp.float32)
    lane = lane_of((8, 128))
    for n, part in enumerate(acc):
        total = jnp.sum(jnp.sum(part, axis=0, keepdims=True), axis=1, keepdims=True)
        line = jnp.where(lane == n, total, line)
    sum_ref[...] = line

    def pack_step(j, _):
        for c in range(3):
            rp[c, j] = pack_chunks([(rx[c, 4 * k + j + 1], rxt[c, 4 * k + j + 1]) for k in range(4)])
            qp[c, j] = pack_chunks([(qx[c, 4 * k + j], qxt[c, 4 * k + j]) for k in range(4)])
        return 0

    lax.fori_loop(0, 9, pack_step, 0)

    def pack_weights(j, _):
        gpk[j] = pack_chunks([(gf[4 * k + j + 1], gft[4 * k + j + 1]) for k in range(4)])
        return 0

    lax.fori_loop(0, 8, pack_weights, 0)


def pack_chunks(tiles):
    lane = lane_of((WIN, 128))
    out = None
    for k, (main, side) in enumerate(tiles):
        high = roll(jnp.where(lane >= 64, main, side), 32 * k + 4)
        low = roll(jnp.where(lane >= 64, side, main), 32 * k + 28)
        out = high if out is None else jnp.where(lane >= 32 * k, high, out)
        out = jnp.where(lane >= 32 * k + 16, low, out)
    return out


def cross_energy(m, o):
    total = None
    for first, second, pick in (
        (K["a"] - K["b"], K["b"], lambda c: mode(c)),
        (K["p"] - K["r"], K["r"], lambda c: mode(*{0, 1, 2} - {c})),
    ):
        vm, vo = [m[c, pick(c)] for c in range(3)], [o[c, pick(c)] for c in range(3)]
        sm, so = vm[0] + vm[1] + vm[2], vo[0] + vo[1] + vo[2]
        part = (vm[0] * vo[0] + vm[1] * vo[1] + vm[2] * vo[2]) * f32(first) + sm * so * f32(second)
        total = part if total is None else total + part
    shear = None
    for c, e2 in ((0, 1), (0, 2), (1, 2)):
        v = (m[c, mode(e2)] + m[e2, mode(c)]) * (o[c, mode(e2)] + o[e2, mode(c)])
        shear = v if shear is None else shear + v
    triple = None
    for c in range(3):
        v = m[c, (1, 1, 1)] * o[c, (1, 1, 1)]
        triple = v if triple is None else triple + v
    same = cross = None
    for e2 in range(3):
        c, d = [i for i in range(3) if i != e2]
        m1, m2 = m[c, mode(c, e2)], m[d, mode(d, e2)]
        o1, o2 = o[c, mode(c, e2)], o[d, mode(d, e2)]
        sq, cr = m1 * o1 + m2 * o2, m1 * o2 + m2 * o1
        same = sq if same is None else same + sq
        cross = cr if cross is None else cross + cr
    total = total + shear * f32(K["g"]) + triple * f32(K["h"])
    return total + same * f32(K["c"]) + cross * f32(K["d"])


def energy_kernel(rx, qx, gf, rp, qp, gpk, px, pp, zt, tr, tq):
    lane = lane_of((WIN, 128))
    edge = lane == 127
    zt[:, :, 24:32] = jnp.zeros((6, 2, 8, 128), jnp.float32)

    def half_plane(at, after, t_ref, slot):
        for c in range(3):
            a = at(c)
            n = after(c, a)
            zt[2 * c, 0, 0:24] = a + n
            zt[2 * c + 1, 0, 0:24] = n - a
        for f in range(6):
            for b in range(3):
                lo, hi = zt[f, 0, 8 * b : 8 * b + 8], zt[f, 0, 8 * b + 1 : 8 * b + 9]
                t_ref[slot, 2 * f, 0, 8 * b : 8 * b + 8] = lo + hi
                t_ref[slot, 2 * f + 1, 0, 8 * b : 8 * b + 8] = hi - lo

    def main_plane(i, slot):
        chunk = jnp.minimum(i >> 2, 3)
        j, shift = i - 4 * chunk, 123 - 32 * chunk

        def after(src):
            return lambda c, a: jnp.where(edge, pltpu.roll(src[c, j], shift, 1), roll(a, -1))

        half_plane(lambda c: rx[c, i + 1], after(rp), tr, slot)
        half_plane(lambda c: qx[c, i], after(qp), tq, slot)

    def end_plane(j, slot):
        half_plane(lambda c: rp[c, j], lambda c, a: roll(a, -1), tr, slot)
        half_plane(lambda c: qp[c, j], lambda c, a: roll(a, -1), tq, slot)

    def energies(i, g_ref, out):
        new, old = (i + 1) & 1, i & 1
        for b in range(3):
            rows = slice(8 * b, 8 * b + 8)
            m = modal_of(read_t(tr, old, 0, b), read_t(tr, new, 0, b))
            o = modal_of(read_t(tq, old, 0, b), read_t(tq, new, 0, b))
            g = g_ref[rows]
            out[0, i, rows] = energy_of(m) * g
            out[1, i, rows] = cross_energy(m, o) * (2.0 * g)
            out[2, i, rows] = energy_of(o) * g

    def main_step(i, _):
        main_plane(i + 1, (i + 1) & 1)
        energies(i, gf.at[i + 1], px)
        return 0

    def end_step(j, _):
        end_plane(j + 1, (j + 1) & 1)
        energies(j, gpk.at[j], pp)
        return 0

    main_plane(jnp.int32(0), 0)
    lax.fori_loop(0, 20, main_step, 0)
    end_plane(0, 0)
    lax.fori_loop(0, 8, end_step, 0)


def cones_kernel(px, pp, dens_in, order_ref, out_ref, dens_ref, av, ap, bp):
    del order_ref
    dens_ref[...] = dens_in[...]

    def parts_of(src, k, x, dst):
        f0 = src[k, x + 2]
        f1 = src[k, x + 1] + src[k, x + 3]
        f2 = src[k, x] + src[k, x + 4]
        for n, part in enumerate(x_parts(f0, f1, f2).values()):
            dst[k, n, 0, 0:24] = part

    def end_cone(j, _):
        for k in range(3):
            parts_of(pp, k, j, ap)
            b = cone_yz(ap.at[k], 0, (4, 20))
            bp[k, j, 0] = b[1]
            bp[k, j, 1] = b[2]
        return 0

    lax.fori_loop(0, 4, end_cone, 0)
    lane16 = lane_of((NYL, 128))
    for chunk in range(4):

        def cone_step(j, _):
            x = 4 * chunk + j
            for k in range(3):
                parts_of(px, k, x, av)
                b0, b1, b2 = cone_yz(av.at[k], 0, (4, 20))
                e1, e2 = bp[k, j, 0], bp[k, j, 1]
                n1 = jnp.where(lane16 == 127, roll(e1, 123 - 32 * chunk), roll(b1, -1))
                p1 = jnp.where(lane16 == 0, roll(e1, -(32 * chunk + 27)), roll(b1, 1))
                n2 = jnp.where(lane16 >= 126, roll(e2, 122 - 32 * chunk), roll(b2, -2))
                p2 = jnp.where(lane16 < 2, roll(e2, -(32 * chunk + 26)), roll(b2, 2))
                out_ref[k, x] = b0 + (n1 + p1) + (n2 + p2)
            return 0

        lax.fori_loop(0, 4, cone_step, 0)


def spread_pair_kernel(own_ref, other_ref, out_ref):
    out_ref[...] = jnp.broadcast_to(own_ref[0:1] + other_ref[0:1], out_ref.shape)


def spread_sum_kernel(in_ref, order_ref, out_ref):
    del order_ref
    out_ref[...] = jnp.broadcast_to(jnp.sum(in_ref[...], axis=0, keepdims=True), out_ref.shape)


def final_kernel(sum_ref, load_ref, qx, cones, disp_ref, sens_ref):
    line = jnp.sum(sum_ref[...], axis=0, keepdims=True)
    lane1 = lane_of((1, 128))
    m0, m1, m2, m3 = [jnp.sum(jnp.where(lane1 == n, line, 0.0), axis=1, keepdims=True) for n in range(4)]
    m3 = m3 + spring_rate * m2
    first = m0 / m1
    norm = m0 - 2.0 * first * m1 + first * first * m2
    grown = 1.0 + norm / m0
    second = norm / (grown * grown * m1 - 2.0 * first * grown * m2 + first * first * m3)
    c0 = jnp.broadcast_to(first + second * grown, (NYL, 128))
    c1 = jnp.broadcast_to(-second * first, (NYL, 128))

    def step(x, _):
        for c in range(3):
            disp_ref[c, x] = c0 * load_ref[c, x] + c1 * qx[c, x + 2, 4:20]
        sens_ref[x] = c0 * (c0 * cones[0, x] + c1 * cones[1, x]) + c1 * c1 * cones[2, x]
        return 0

    lax.fori_loop(0, 16, step, 0)


def s(*shape):
    return jax.ShapeDtypeStruct(shape, jnp.float32)


def v(*shape):
    return pltpu.VMEM(shape, jnp.float32)


def call(kernel, outs, scratch, *args, smem=0, hbm=0, flush=(), **kw):
    spec_s, spec_v = pl.BlockSpec(memory_space=pltpu.SMEM), pl.BlockSpec(memory_space=pltpu.VMEM)
    single = not isinstance(outs, (tuple, list))
    outs = [outs] if single else list(outs)
    if not INTERPRET:
        outs = [o if i in flush else pltpu.VMEM(o.shape, o.dtype) for i, o in enumerate(outs)]
        args = [
            a if i < smem else pltpu.with_memory_space_constraint(a, pltpu.HBM if i < smem + hbm else pltpu.VMEM)
            for i, a in enumerate(args)
        ]
    return pl.pallas_call(
        kernel,
        out_shape=outs[0] if single else outs,
        in_specs=[spec_s] * smem
        + [pl.BlockSpec(memory_space=pltpu.HBM)] * hbm
        + [spec_v] * (len(args) - smem - hbm),
        out_specs=spec_v if single else [spec_v] * len(outs),
        scratch_shapes=scratch,
        interpret=INTERPRET,
        compiler_params=pltpu.CompilerParams(vmem_limit_bytes=24 << 20),
        **kw,
    )(*args)


def moved(block, axis, step):
    count = lax.axis_size(axis)
    return lax.ppermute(block, axis, [(i, i - step) for i in range(count) if 0 <= i - step < count])


def body(load, design, solid_map):
    sizes = tuple(lax.axis_size(a) * n for a, n in zip(ALL, (NXL, NYL, NZL)))
    wide, long = ("gx_0", "gz"), ("gy",)
    wide_n, long_n = (math.prod(lax.axis_size(a) for a in axes) for axes in (wide, long))

    def sized(kernel):
        return lambda *refs: kernel(*refs, sizes=sizes)

    load_arg = load
    load, design, zc = call(
        pack_z_kernel, (s(3, 16, 16, 128), s(16, 16, 128), s(8, 16, 128)), [pltpu.SemaphoreType.DMA((4,))],
        load, design, hbm=2,
    )
    zhi, zlo = moved(zc, "gz", 1), moved(zc, "gz", -1)
    qk, fl, cl = call(
        sized(place_kernel), (s(6, 2, 24, 128), s(3, 2, 24, 128), s(2, 24, 128)), [], solid_map, zc, smem=1
    )
    ylo_s, yhi_s = call(pack_y_kernel, (s(39, 8, 128), s(39, 8, 128)), [], load, design, zhi, zlo, cl)
    yhi, ylo = moved(ylo_s, "gy", 1), moved(yhi_s, "gy", -1)
    rx_t, dx_t, mo_t, gf_t = s(3, 23, 24, 128), s(26, 2, 32, 128), s(22, 2, 24, 128), s(22, 24, 128)
    dens_t, qx_t = s(16, 16, 128), s(3, 21, 24, 128)
    rx, rxt, dx, xlo_s, xhi_s = call(
        pack_x_kernel, (rx_t, rx_t, dx_t, s(544, 128), s(472, 128)), [v(8, 32, 128)],
        load, design, zhi, zlo, ylo, yhi,
    )
    xhi, xlo = moved(xlo_s, GX, 1), moved(xhi_s, GX, -1)
    scratch = [
        v(6, 2, 32, 128), v(6, 2, 32, 128), v(2, 12, 2, 24, 128), v(12, 2, 24, 128), v(6, 2, 24, 128), v(6, 2, 32, 128),
    ]
    mo, gf, gft, dens, qx, qxt, acc = call(
        sized(inner_kernel), (mo_t, gf_t, gf_t, dens_t, qx_t, qx_t, s(4, 8, 128)), scratch, rx, rxt, dx, qk, fl, cl
    )
    held = rx_t, rx_t, dx_t, mo_t, gf_t, gf_t, dens_t, qx_t, qx_t
    rx, _, _, _, gf, _, dens, qx, _, rp, qp, gpk, part = call(
        sized(outer_kernel),
        (*held, s(3, 9, 24, 128), s(3, 9, 24, 128), s(8, 24, 128), s(8, 128)), scratch,
        rx, rxt, dx, mo, gf, gft, dens, qx, qxt, acc, xlo, xhi, qk, fl, cl,
        input_output_aliases={n: n for n in range(len(held))},
    )
    other = lax.ppermute(part, "gx_1", [(0, 1), (1, 0)])
    part = call(spread_pair_kernel, s(wide_n, 128), [], part, other)
    part = lax.all_to_all(part, wide, 0, 0, tiled=True)
    px, pp = call(
        energy_kernel, (s(3, 20, 24, 128), s(3, 8, 24, 128)),
        [v(6, 2, 32, 128), v(2, 12, 1, 24, 128), v(2, 12, 1, 24, 128)],
        rx, qx, gf, rp, qp, gpk,
    )
    part = call(spread_sum_kernel, s(long_n, 128), [], part, px)
    sums = lax.all_to_all(part, long, 0, 0, tiled=True)
    cones, dens = call(
        cones_kernel, (s(3, 16, 16, 128), dens_t),
        [v(3, 6, 1, 32, 128), v(3, 6, 1, 32, 128), v(3, 4, 2, 16, 128)],
        px, pp, dens, part, flush=(1,),
    )
    disp, sens = call(
        final_kernel, (s(3, 16, 16, 128), s(16, 16, 128)), [], sums, load_arg, qx, cones, flush=(0, 1)
    )
    return disp, sens, dens


def solution(mesh):
    cores = 2
    split = Mesh(
        mesh.devices.reshape(mesh.shape["gx"] // cores, cores, mesh.shape["gy"], mesh.shape["gz"]),
        (*GX, "gy", "gz"),
    )
    nodal, cell = P(None, GX, "gy", "gz"), P(GX, "gy", "gz")
    return jax.shard_map(
        body, mesh=split, in_specs=(nodal, cell, P()), out_specs=(nodal, cell, cell), check_vma=False
    )
```

```python
import math

import jax
import jax.numpy as jnp
import numpy as np
from jax import lax
from jax.experimental import pallas as pl
from jax.experimental.pallas import tpu as pltpu
from jax.sharding import PartitionSpec as P


BRICK = 16
young_floor = 0.001
spring_rate = 0.05
sharpness = 8.0
threshold = 0.5
poisson = 0.3
ALL = ("gx", "gy", "gz")
INTERPRET = False

NXL, NYL, NZL = 16, 16, 128
WIN = 24


def element_matrix():
    lame_first = poisson / ((1.0 + poisson) * (1.0 - 2.0 * poisson))
    shear_mod = 1.0 / (2.0 * (1.0 + poisson))
    elastic = np.zeros((6, 6))
    elastic[:3, :3] = lame_first
    for axis_one in range(3):
        elastic[axis_one, axis_one] += 2.0 * shear_mod
        elastic[axis_one + 3, axis_one + 3] = shear_mod
    gauss_point = 1.0 / math.sqrt(3.0)
    stiffness = np.zeros((24, 24))
    for point_x in (-gauss_point, gauss_point):
        for point_y in (-gauss_point, gauss_point):
            for point_z in (-gauss_point, gauss_point):
                strain = np.zeros((6, 24))
                for corner in range(8):
                    sign_a = 2 * (corner // 4) - 1
                    sign_b = 2 * (corner // 2 % 2) - 1
                    sign_c = 2 * (corner % 2) - 1
                    along_x = 0.25 * sign_a * (1 + sign_b * point_y) * (1 + sign_c * point_z)
                    along_y = 0.25 * (1 + sign_a * point_x) * sign_b * (1 + sign_c * point_z)
                    along_z = 0.25 * (1 + sign_a * point_x) * (1 + sign_b * point_y) * sign_c
                    column = 3 * corner
                    strain[0, column] = along_x
                    strain[1, column + 1] = along_y
                    strain[2, column + 2] = along_z
                    strain[3, column + 1] = along_z
                    strain[3, column + 2] = along_y
                    strain[4, column] = along_z
                    strain[4, column + 2] = along_x
                    strain[5, column] = along_y
                    strain[5, column + 1] = along_x
                stiffness += strain.T @ elastic @ strain * 0.125
    return stiffness


def modal_constants():
    modes = [(px, py, pz) for px in (0, 1) for py in (0, 1) for pz in (0, 1)]
    change = np.zeros((24, 24))
    for c in range(3):
        for m, mode in enumerate(modes):
            for q in range(8):
                corner = (q // 4, q // 2 % 2, q % 2)
                sign = 1.0
                for axis in range(3):
                    if mode[axis] and not corner[axis]:
                        sign = -sign
                change[8 * c + m, 3 * q + c] = sign
    hat = change @ element_matrix() @ change.T / 64.0

    def at(c1, m1, c2, m2):
        return hat[8 * c1 + modes.index(m1), 8 * c2 + modes.index(m2)]

    k = {
        "a": at(0, (1, 0, 0), 0, (1, 0, 0)),
        "b": at(0, (1, 0, 0), 1, (0, 1, 0)),
        "p": at(0, (0, 1, 1), 0, (0, 1, 1)),
        "r": at(0, (0, 1, 1), 1, (1, 0, 1)),
        "g": at(0, (0, 1, 0), 1, (1, 0, 0)),
        "h": at(2, (1, 1, 1), 2, (1, 1, 1)),
        "c": at(1, (1, 1, 0), 1, (1, 1, 0)),
        "d": at(1, (1, 1, 0), 2, (1, 0, 1)),
    }
    made = np.zeros((24, 24))

    def put(c1, m1, c2, m2, v):
        made[8 * c1 + modes.index(m1), 8 * c2 + modes.index(m2)] += v

    for c in range(3):
        unit = tuple(int(i == c) for i in range(3))
        anti = tuple(int(i != c) for i in range(3))
        put(c, (1, 1, 1), c, (1, 1, 1), k["h"])
        for e in range(3):
            unit_e = tuple(int(i == e) for i in range(3))
            anti_e = tuple(int(i != e) for i in range(3))
            put(c, unit, e, unit_e, k["a"] if c == e else k["b"])
            put(c, anti, e, anti_e, k["p"] if c == e else k["r"])
            if c != e:
                put(c, unit_e, c, unit_e, k["g"])
                put(c, unit_e, e, unit, k["g"])
                both = tuple(int(i in (c, e)) for i in range(3))
                o = 3 - c - e
                both_o = tuple(int(i in (o, e)) for i in range(3))
                put(c, both, c, both, k["c"])
                put(c, both, o, both_o, k["d"])
    assert np.abs(made - hat).max() < 1e-12
    return k


K = modal_constants()
W = {n: 3.0 - math.sqrt(n) for n in range(9)}
KS = (0, 1, 2, 4, 5, 8)


def mode(*axes):
    return tuple(int(i in axes) for i in range(3))


def f32(x):
    return float(np.float32(x))


def roll(x, shift):
    shift = shift % 128
    return x if shift == 0 else pltpu.roll(x, shift, 1)


def lane_of(shape):
    return lax.broadcasted_iota(jnp.int32, shape, 1)


def z_next(a0, a1, lane, by=1):
    r0, r1 = roll(a0, -by), roll(a1, -by)
    edge = lane >= 128 - by
    return jnp.where(edge, r1, r0), jnp.where(edge, r0, r1)


def z_prev(a0, a1, lane, by=1):
    r0, r1 = roll(a0, by), roll(a1, by)
    edge = lane < by
    return jnp.where(edge, r1, r0), jnp.where(edge, r0, r1)


def modal_of(lo, hi):
    m = {}
    for (c, py, pz), low in lo.items():
        high = hi[c, py, pz]
        if py or pz:
            m[c, (0, py, pz)] = low + high
        m[c, (1, py, pz)] = high - low
    return m


def forces_of(m, e):
    ea, eb = e * f32(K["a"] - K["b"]), e * f32(K["b"])
    ep, er = e * f32(K["p"] - K["r"]), e * f32(K["r"])
    eg, eh = e * f32(K["g"]), e * f32(K["h"])
    ec, ed = e * f32(K["c"]), e * f32(K["d"])
    f = {}
    for first, second, pick in ((ea, eb, lambda c: mode(c)), (ep, er, lambda c: mode(*{0, 1, 2} - {c}))):
        vals = [m[c, pick(c)] for c in range(3)]
        shared = (vals[0] + vals[1] + vals[2]) * second
        for c in range(3):
            f[c, pick(c)] = vals[c] * first + shared
    for c, e2 in ((0, 1), (0, 2), (1, 2)):
        shared = (m[c, mode(e2)] + m[e2, mode(c)]) * eg
        f[c, mode(e2)] = shared
        f[e2, mode(c)] = shared
    for c in range(3):
        f[c, (1, 1, 1)] = m[c, (1, 1, 1)] * eh
    for e2 in range(3):
        c, o = [i for i in range(3) if i != e2]
        v1, v2 = m[c, mode(c, e2)], m[o, mode(o, e2)]
        f[c, mode(c, e2)] = v1 * ec + v2 * ed
        f[o, mode(o, e2)] = v2 * ec + v1 * ed
    return f


def energy_of(m):
    total = None
    for first, second, pick in (
        (K["a"] - K["b"], K["b"], lambda c: mode(c)),
        (K["p"] - K["r"], K["r"], lambda c: mode(*{0, 1, 2} - {c})),
    ):
        vals = [m[c, pick(c)] for c in range(3)]
        s = vals[0] + vals[1] + vals[2]
        part = (vals[0] * vals[0] + vals[1] * vals[1] + vals[2] * vals[2]) * f32(first) + s * s * f32(second)
        total = part if total is None else total + part
    shear = None
    for c, e2 in ((0, 1), (0, 2), (1, 2)):
        s = m[c, mode(e2)] + m[e2, mode(c)]
        shear = s * s if shear is None else shear + s * s
    total = total + shear * f32(K["g"])
    triple = None
    for c in range(3):
        v = m[c, (1, 1, 1)]
        triple = v * v if triple is None else triple + v * v
    total = total + triple * f32(K["h"])
    squares = cross = None
    for e2 in range(3):
        c, o = [i for i in range(3) if i != e2]
        v1, v2 = m[c, mode(c, e2)], m[o, mode(o, e2)]
        sq, cr = v1 * v1 + v2 * v2, v1 * v2
        squares = sq if squares is None else squares + sq
        cross = cr if cross is None else cross + cr
    return total + squares * f32(K["c"]) + cross * f32(2.0 * K["d"])


def x_parts(f0, f1, f2):
    out = {}
    for k in KS:
        v = f0 * f32(W[k])
        if k + 1 in W:
            v = v + f1 * f32(W[k + 1])
        if k + 4 in W:
            v = v + f2 * f32(W[k + 4])
        out[k] = v
    return out


def pack_z_kernel(load_hbm, design_hbm, load_ref, design_ref, out_ref, sems):
    copies = [pltpu.make_async_copy(load_hbm.at[c], load_ref.at[c], sems.at[c]) for c in range(3)]
    copies.append(pltpu.make_async_copy(design_hbm, design_ref, sems.at[3]))
    for one in copies:
        one.start()
    for one in copies:
        one.wait()
    lane = lane_of((NYL, 128))

    def step(pair, _):
        acc = jnp.zeros((NYL, 128), jnp.float32)
        for par in range(2):
            for fld in range(4):
                off = 64 * par + 16 * fld
                src = load_ref[fld, 2 * pair + par] if fld < 3 else design_ref[2 * pair + par]
                acc = jnp.where(((lane - off + 8) & 127) < 16, roll(src, off), acc)
        out_ref[pair] = acc
        return 0

    lax.fori_loop(0, 8, step, 0)


def halo_merge(high, low):
    lane = lane_of(high.shape)
    return jnp.where((lane & 15) < 8, high, low)


def pack_y_kernel(load_ref, design_ref, zhi_ref, zlo_ref, place_ref, lo_ref, hi_ref):
    del place_ref
    for dst, quad, one in ((lo_ref, 0, 4), (hi_ref, 12, 11)):
        rows = slice(quad, quad + 4)
        for x in range(16):
            dst[x, 0:4] = load_ref[0, x, rows]
            dst[x, 4:8] = load_ref[1, x, rows]
            dst[16 + x, 0:4] = load_ref[2, x, rows]
            dst[16 + x, 4:8] = design_ref[x, rows]
            dst[32 + x // 8, x % 8 : x % 8 + 1] = design_ref[x, one : one + 1]
        for k in range(8):
            dst[35 + k // 2, 4 * (k % 2) : 4 * (k % 2) + 4] = halo_merge(zhi_ref[k, rows], zlo_ref[k, rows])
            dst[34, k : k + 1] = halo_merge(zhi_ref[k, one : one + 1], zlo_ref[k, one : one + 1])


def pack_x_kernel(load_ref, design_ref, zhi_ref, zlo_ref, ylo_ref, yhi_ref, rx, rxt, dx, lo_ref, hi_ref, hx):
    none = jnp.zeros((8, 128), jnp.float32)
    for k in range(8):
        half = slice(4 * (k % 2), 4 * (k % 2) + 4)
        hx[k, 0:8] = none
        hx[k, 24:32] = none
        hx[k, 3:4] = ylo_ref[34, k : k + 1]
        hx[k, 4:8] = ylo_ref[35 + k // 2, half]
        hx[k, 8:24] = halo_merge(zhi_ref[k], zlo_ref[k])
        hx[k, 24:28] = yhi_ref[35 + k // 2, half]
        hx[k, 28:29] = yhi_ref[34, k : k + 1]
    for x in range(16):
        for c in range(3):
            tile, half = (x, slice(4 * c, 4 * c + 4)) if c < 2 else (16 + x, slice(0, 4))
            rx[c, x + 3, 0:4] = ylo_ref[tile, half]
            rx[c, x + 3, 4:20] = load_ref[c, x]
            rx[c, x + 3, 20:24] = yhi_ref[tile, half]
        one = slice(x % 8, x % 8 + 1)
        dx[x + 5, 0, 0:8] = none
        dx[x + 5, 0, 24:32] = none
        dx[x + 5, 0, 3:4] = ylo_ref[32 + x // 8, one]
        dx[x + 5, 0, 4:8] = ylo_ref[16 + x, 4:8]
        dx[x + 5, 0, 8:24] = design_ref[x]
        dx[x + 5, 0, 24:28] = yhi_ref[16 + x, 4:8]
        dx[x + 5, 0, 28:29] = yhi_ref[32 + x // 8, one]
    for i in range(5):
        lo_ref[288 + 32 * i : 320 + 32 * i] = dx[5 + i, 0]
        hi_ref[216 + 32 * i : 248 + 32 * i] = dx[16 + i, 0]
    for i in range(3):
        lo_ref[448 + 32 * i : 480 + 32 * i] = hx[i]
        hi_ref[376 + 32 * i : 408 + 32 * i] = hx[5 + i]
    for c in range(3):
        for i in range(4):
            lo_ref[24 * (4 * c + i) : 24 * (4 * c + i) + 24] = rx[c, 3 + i]
        for i in range(3):
            hi_ref[24 * (3 * c + i) : 24 * (3 * c + i) + 24] = rx[c, 16 + i]
    for k in range(8):
        spread_pair(hx[k], 2 * k, (2 * k, 2 * k + 1), rxt, dx, True)


def spread_pair(tile, x, wanted, rxt, dx, both):
    for par in range(2):
        if x + par in wanted:
            dx[x + par + 5, 1] = roll(tile, -(64 * par + 48))
            if both or -3 <= x + par <= 19:
                for c in range(3):
                    rxt[c, x + par + 3] = roll(tile, -(64 * par + 16 * c))[4:28]


def x_halos(xlo_ref, xhi_ref, rx, rxt, dx):
    for c in range(3):
        for i in range(4):
            rx[c, 19 + i] = xhi_ref[24 * (4 * c + i) : 24 * (4 * c + i) + 24]
        for i in range(3):
            rx[c, i] = xlo_ref[24 * (3 * c + i) : 24 * (3 * c + i) + 24]
    for i in range(5):
        dx[21 + i, 0] = xhi_ref[288 + 32 * i : 320 + 32 * i]
        dx[i, 0] = xlo_ref[216 + 32 * i : 248 + 32 * i]
    for i in range(3):
        spread_pair(xhi_ref[448 + 32 * i : 480 + 32 * i], 16 + 2 * i, range(16, 21), rxt, dx, False)
        spread_pair(xlo_ref[376 + 32 * i : 408 + 32 * i], -6 + 2 * i, range(-5, 0), rxt, dx, False)


def place_kernel(map_ref, order_ref, qk, fl, cl, *, sizes):
    del order_ref
    nx, ny, nz = sizes
    i_x, i_y, i_z = (lax.axis_index(a) for a in ALL)
    lane = lane_of((WIN, 128))
    row = lax.broadcasted_iota(jnp.int32, (WIN, 128), 0)
    y_at = i_y * NYL + row - 4
    z_at = [i_z * NZL + lane, i_z * NZL + jnp.where(lane < 64, lane + 128, lane - 128)]

    def inside(at, step, length):
        return jnp.where((at + step >= 0) & (at + step < length), 1.0, 0.0)

    y_in = [inside(y_at, 0, ny)] + [inside(y_at, s, ny) + inside(y_at, -s, ny) for s in (1, 2)]
    for t in range(2):
        z_in = [inside(z_at[t], 0, nz)] + [inside(z_at[t], s, nz) + inside(z_at[t], -s, nz) for s in (1, 2)]
        qk[0, t] = y_in[0] * z_in[0]
        qk[1, t] = y_in[1] * z_in[0] + y_in[0] * z_in[1]
        qk[2, t] = y_in[1] * z_in[1]
        qk[3, t] = y_in[2] * z_in[0] + y_in[0] * z_in[2]
        qk[4, t] = y_in[1] * z_in[2] + y_in[2] * z_in[1]
        qk[5, t] = y_in[2] * z_in[2]
        cl[t] = y_in[0] * z_in[0]
    gbx, gby, gbz = nx // BRICK, ny // BRICK, nz // BRICK
    bricks = NZL // BRICK

    def flag_at(bx, by, bz):
        ok = (bx >= 0) & (bx < gbx) & (by >= 0) & (by < gby) & (bz >= 0) & (bz < gbz)
        value = map_ref[jnp.clip(bx, 0, gbx - 1), jnp.clip(by, 0, gby - 1), jnp.clip(bz, 0, gbz - 1)]
        return jnp.where(ok, value, 0).astype(jnp.float32)

    for xc in range(3):
        lines = []
        for yc in range(3):
            flag = [flag_at(i_x + xc - 1, i_y + yc - 1, i_z * bricks + n - 1) for n in range(bricks + 2)]
            main = jnp.zeros((WIN, 128), jnp.float32)
            for n in range(bricks):
                main = jnp.where((lane >> 4) == n, flag[n + 1], main)
            lines.append((main, jnp.where(lane < 64, flag[bricks + 1], flag[0])))
        for t in range(2):
            fl[xc, t] = jnp.where(row < 4, lines[0][t], jnp.where(row < 20, lines[1][t], lines[2][t]))


def zy_plane(tile, zt, t_ref, slot, lane, tiles=2, base=0, blocks=3):
    for c in range(3):
        a0, a1 = tile(c, 0), tile(c, 1)
        n0, n1 = z_next(a0, a1, lane)
        zt[2 * c, 0, 0:24] = a0 + n0
        zt[2 * c + 1, 0, 0:24] = n0 - a0
        if tiles == 2:
            zt[2 * c, 1, 0:24] = a1 + n1
            zt[2 * c + 1, 1, 0:24] = n1 - a1
    for f in range(6):
        for t in range(tiles):
            for b in range(blocks):
                r = base + 8 * b
                lo, hi = zt[f, t, r : r + 8], zt[f, t, r + 1 : r + 9]
                t_ref[slot, 2 * f, t, 8 * b : 8 * b + 8] = lo + hi
                t_ref[slot, 2 * f + 1, t, 8 * b : 8 * b + 8] = hi - lo


def read_t(t_ref, slot, t, b):
    out = {}
    for c in range(3):
        for pz in range(2):
            for py in range(2):
                out[c, py, pz] = t_ref[slot, 4 * c + 2 * pz + py, t, 8 * b : 8 * b + 8]
    return out


LIFT = math.tanh(sharpness * threshold)
SCALE = LIFT + math.tanh(sharpness * (1.0 - threshold))


def cone_yz(av, t, rows):
    lo, hi = rows

    def at(n, step):
        return av[n, t, lo + step : hi + step]

    def both(n, step):
        return at(n, -step) + at(n, step)

    return [
        at(0, 0) + both(1, 1) + both(3, 2),
        at(1, 0) + both(2, 1) + both(4, 2),
        at(3, 0) + both(4, 1) + both(5, 2),
    ]


def density_plane(e, own, nx, dx, qk, fl, av, mo, gfs, dens_ref):
    lane = lane_of((WIN, 128))
    x_at = lax.axis_index("gx") * NXL + e - 3

    def scalar_inside(at, step):
        return jnp.where((at + step >= 0) & (at + step < nx), 1.0, 0.0)

    for t in range(2):
        f0 = dx[e + 2, t]
        f1 = dx[e + 1, t] + dx[e + 3, t]
        f2 = dx[e, t] + dx[e + 4, t]
        for n, part in enumerate(x_parts(f0, f1, f2).values()):
            av[n, t] = part
    x0 = scalar_inside(x_at, 0)
    x1 = scalar_inside(x_at, 1) + scalar_inside(x_at, -1)
    x2 = scalar_inside(x_at, 2) + scalar_inside(x_at, -2)
    cls = jnp.where(e < 3, 0, jnp.where(e < 19, 1, 2))
    b = [cone_yz(av, t, (4, 28)) for t in range(2)]
    n1, p1 = z_next(b[0][1], b[1][1], lane), z_prev(b[0][1], b[1][1], lane)
    n2, p2 = z_next(b[0][2], b[1][2], lane, 2), z_prev(b[0][2], b[1][2], lane, 2)
    weights = x_parts(x0, x1, x2)
    for t in range(2):
        cone = b[t][0] + (n1[t] + p1[t]) + (n2[t] + p2[t])
        ws = None
        for n, wk in enumerate(weights.values()):
            ws = qk[n, t] * wk if ws is None else ws + qk[n, t] * wk
        inv = 1.0 / jnp.maximum(ws, 1.0)
        th = jnp.tanh(sharpness * (cone * inv - threshold))
        dens = (LIFT + th) * f32(1.0 / SCALE)
        flag = fl[cls, t]
        sq = dens * dens
        mo[e, t] = (young_floor + sq * dens * (1.0 - young_floor)) * flag
        gfs[t][e] = sq * flag * (1.0 - th * th) * inv * f32(-3.0 * (1.0 - young_floor) * sharpness / SCALE)
        if t == 0:
            av[6, 0, 0:24] = dens
    dens_ref[own] = av[6, 0, 4:20]


def operate_planes(firsts, count, nx, rs, mo, cl, qs, zt, tt, gp, yp, yg):
    lane = lane_of((WIN, 128))
    i_x = lax.axis_index("gx")
    for n, first in enumerate(firsts):
        gp[n] = jnp.zeros((12, 2, 24, 128), jnp.float32)
        zy_plane(lambda c, t: rs[t][c, first], zt.at[n], tt.at[n], 0, lane)

    def transposes(n, first, i):
        e = first + jnp.maximum(i, 0)
        slot = i & 1
        x_on = jnp.where(i_x * NXL + e - 3 < nx, 1.0, 0.0)
        to = first + jnp.maximum(i - 1, 0)
        for c in range(3):
            p, g = [], []
            for t in range(2):
                zs = yp[n, slot, 2 * c, t] + yg[n, slot, 2 * c, t, 7:31]
                zd = yp[n, slot, 2 * c + 1, t] + yg[n, slot, 2 * c + 1, t, 7:31]
                p.append(zs - zd)
                g.append(zs + zd)
            gb = z_prev(g[0], g[1], lane)
            for t in range(2):
                value = p[t] + gb[t] + rs[t][c, e] * spring_rate
                qs[t][c, to] = value * (cl[t] * x_on)

    def forces(n, first, i):
        new, old = (i + 1) & 1, i & 1
        e = first + i
        zy_plane(lambda c, t: rs[t][c, e + 1], zt.at[n], tt.at[n], new, lane)
        for t in range(2):
            for b in range(3):
                rows = slice(8 * b, 8 * b + 8)
                force = forces_of(
                    modal_of(read_t(tt.at[n], old, t, b), read_t(tt.at[n], new, t, b)), mo[e, t, rows]
                )
                for c in range(3):
                    for pz in range(2):
                        m = []
                        for py in range(2):
                            fd = force[c, (1, py, pz)]
                            fs = force.get((c, (0, py, pz)))
                            at = 4 * c + 2 * pz + py
                            before = gp[n, at, t, rows]
                            if fs is None:
                                gp[n, at, t, rows] = fd
                                m.append(before - fd)
                            else:
                                gp[n, at, t, rows] = fs + fd
                                m.append((fs - fd) + before)
                        yp[n, old, 2 * c + pz, t, rows] = m[0] - m[1]
                        yg[n, old, 2 * c + pz, t, 8 + 8 * b : 16 + 8 * b] = m[0] + m[1]

    def step(i, _):
        for n, first in enumerate(firsts):
            transposes(n, first, i - 1)
            forces(n, first, i)
        return 0

    lax.fori_loop(0, count, step, 0)
    for n, first in enumerate(firsts):
        transposes(n, first, jnp.int32(count - 1))


def sum_planes(firsts, count, acc, rs, qs, mo, zt, tt):
    lane = lane_of((WIN, 128))

    def plane(n, x, slot):
        zy_plane(lambda c, t: qs[t][c, x + 2], zt.at[n], tt.at[n], slot, lane, tiles=1, base=4, blocks=2)

    for n, first in enumerate(firsts):
        plane(n, first, 0)

    def step(i, acc):
        s0, s1, s2, s3 = acc
        new, old = (i + 1) & 1, i & 1
        for n, first in enumerate(firsts):
            x = first + i
            plane(n, x + 1, new)
            for b in range(2):
                rows = slice(4 + 8 * b, 12 + 8 * b)
                for c in range(3):
                    r, q = rs[0][c, x + 3, rows], qs[0][c, x + 2, rows]
                    s0, s1, s2 = s0 + r * r, s1 + r * q, s2 + q * q
                m = modal_of(read_t(tt.at[n], old, 0, b), read_t(tt.at[n], new, 0, b))
                s3 = s3 + energy_of(m) * mo[x + 3, 0, rows]
        return s0, s1, s2, s3

    return lax.fori_loop(0, count, step, acc)


def clear_edges(zt, yg):
    for n in range(2):
        zt[n, :, :, 24:32] = jnp.zeros((6, 2, 8, 128), jnp.float32)
        for slot in range(2):
            yg[n, slot, :, :, 0:8] = jnp.zeros((6, 2, 8, 128), jnp.float32)


def inner_kernel(
    rx, rxt, dx, qk, fl, cl, mo, gf, gft, dens_ref, qx, qxt, acc_ref, av, zt, tt, gp, yp, yg, *, sizes
):
    nx = sizes[0]
    clear_edges(zt, yg)

    def density_step(i, _):
        for n in range(2):
            e = 5 + i + 6 * n
            density_plane(e, e - 3, nx, dx, qk, fl, av.at[n], mo, (gf, gft), dens_ref)
        return 0

    lax.fori_loop(0, 6, density_step, 0)
    operate_planes((5,), 12, nx, (rx, rxt), mo, cl, (qx, qxt), zt, tt, gp, yp, yg)
    zero = jnp.zeros((8, 128), jnp.float32)
    for n, part in enumerate(sum_planes((3, 8), 5, (zero,) * 4, (rx, rxt), (qx, qxt), mo, zt, tt)):
        acc_ref[n] = part


def outer_kernel(
    rx_in, rxt_in, dx_in, mo_in, gf_in, gft_in, dens_in, qx_in, qxt_in, acc_ref, xlo_ref, xhi_ref, qk, fl, cl,
    rx, rxt, dx, mo, gf, gft, dens_ref, qx, qxt, rp, qp, gpk, sum_ref, av, zt, tt, gp, yp, yg, *, sizes
):
    del rx_in, rxt_in, dx_in, mo_in, gf_in, gft_in, dens_in, qx_in, qxt_in
    nx = sizes[0]
    rs, qs, gfs = (rx, rxt), (qx, qxt), (gf, gft)
    clear_edges(zt, yg)
    x_halos(xlo_ref, xhi_ref, rx, rxt, dx)

    def density_step(i, _):
        density_plane(i, jnp.maximum(i - 3, 0), nx, dx, qk, fl, av.at[0], mo, gfs, dens_ref)
        density_plane(21 - i, jnp.minimum(18 - i, 15), nx, dx, qk, fl, av.at[1], mo, gfs, dens_ref)
        return 0

    lax.fori_loop(0, 5, density_step, 0)
    operate_planes((0, 16), 6, nx, rs, mo, cl, qs, zt, tt, gp, yp, yg)
    acc = tuple(acc_ref[n] for n in range(4))
    acc = sum_planes((0, 13), 3, acc, rs, qs, mo, zt, tt)
    line = jnp.zeros((8, 128), jnp.float32)
    lane = lane_of((8, 128))
    for n, part in enumerate(acc):
        total = jnp.sum(jnp.sum(part, axis=0, keepdims=True), axis=1, keepdims=True)
        line = jnp.where(lane == n, total, line)
    for n in range(sum_ref.shape[0] // 8):
        sum_ref[8 * n : 8 * n + 8] = line

    def pack_step(j, _):
        for c in range(3):
            rp[c, j] = pack_chunks([(rx[c, 4 * k + j + 1], rxt[c, 4 * k + j + 1]) for k in range(4)])
            qp[c, j] = pack_chunks([(qx[c, 4 * k + j], qxt[c, 4 * k + j]) for k in range(4)])
        return 0

    lax.fori_loop(0, 9, pack_step, 0)

    def pack_weights(j, _):
        gpk[j] = pack_chunks([(gf[4 * k + j + 1], gft[4 * k + j + 1]) for k in range(4)])
        return 0

    lax.fori_loop(0, 8, pack_weights, 0)


def pack_chunks(tiles):
    lane = lane_of((WIN, 128))
    out = None
    for k, (main, side) in enumerate(tiles):
        high = roll(side, 32 * k)
        low = roll(jnp.where(lane >= 64, side, main), 32 * k + 28)
        out = high if out is None else jnp.where(lane >= 32 * k, high, out)
        out = jnp.where(lane >= 32 * k + 16, low, out)
    return out


def cross_energy(m, o):
    total = None
    for first, second, pick in (
        (K["a"] - K["b"], K["b"], lambda c: mode(c)),
        (K["p"] - K["r"], K["r"], lambda c: mode(*{0, 1, 2} - {c})),
    ):
        vm, vo = [m[c, pick(c)] for c in range(3)], [o[c, pick(c)] for c in range(3)]
        sm, so = vm[0] + vm[1] + vm[2], vo[0] + vo[1] + vo[2]
        part = (vm[0] * vo[0] + vm[1] * vo[1] + vm[2] * vo[2]) * f32(first) + sm * so * f32(second)
        total = part if total is None else total + part
    shear = None
    for c, e2 in ((0, 1), (0, 2), (1, 2)):
        v = (m[c, mode(e2)] + m[e2, mode(c)]) * (o[c, mode(e2)] + o[e2, mode(c)])
        shear = v if shear is None else shear + v
    triple = None
    for c in range(3):
        v = m[c, (1, 1, 1)] * o[c, (1, 1, 1)]
        triple = v if triple is None else triple + v
    same = cross = None
    for e2 in range(3):
        c, d = [i for i in range(3) if i != e2]
        m1, m2 = m[c, mode(c, e2)], m[d, mode(d, e2)]
        o1, o2 = o[c, mode(c, e2)], o[d, mode(d, e2)]
        sq, cr = m1 * o1 + m2 * o2, m1 * o2 + m2 * o1
        same = sq if same is None else same + sq
        cross = cr if cross is None else cross + cr
    total = total + shear * f32(K["g"]) + triple * f32(K["h"])
    return total + same * f32(K["c"]) + cross * f32(K["d"])


def tail_kernel(rx, qx, gf, rp, qp, gpk, dens_in, out_ref, dens_ref, px, pp, zt, tr, tq, av, ap, bp):
    dens_ref[...] = dens_in[...]
    lane = lane_of((WIN, 128))
    edge = lane == 127
    zt[:, :, 24:32] = jnp.zeros((6, 2, 8, 128), jnp.float32)

    def half_plane(at, after, t_ref, slot):
        for c in range(3):
            a = at(c)
            n = after(c, a)
            zt[2 * c, 0, 0:24] = a + n
            zt[2 * c + 1, 0, 0:24] = n - a
        for f in range(6):
            for b in range(3):
                lo, hi = zt[f, 0, 8 * b : 8 * b + 8], zt[f, 0, 8 * b + 1 : 8 * b + 9]
                t_ref[slot, 2 * f, 0, 8 * b : 8 * b + 8] = lo + hi
                t_ref[slot, 2 * f + 1, 0, 8 * b : 8 * b + 8] = hi - lo

    def main_plane(i, slot):
        chunk = jnp.minimum(i >> 2, 3)
        j, shift = i - 4 * chunk, 127 - 32 * chunk

        def after(src):
            return lambda c, a: jnp.where(edge, pltpu.roll(src[c, j], shift, 1), roll(a, -1))

        half_plane(lambda c: rx[c, i + 1], after(rp), tr, slot)
        half_plane(lambda c: qx[c, i], after(qp), tq, slot)

    def end_plane(j, slot):
        half_plane(lambda c: rp[c, j], lambda c, a: roll(a, -1), tr, slot)
        half_plane(lambda c: qp[c, j], lambda c, a: roll(a, -1), tq, slot)

    def energies(i, g_ref, out):
        new, old = (i + 1) & 1, i & 1
        for b in range(3):
            rows = slice(8 * b, 8 * b + 8)
            m = modal_of(read_t(tr, old, 0, b), read_t(tr, new, 0, b))
            o = modal_of(read_t(tq, old, 0, b), read_t(tq, new, 0, b))
            g = g_ref[rows]
            out[0, i, rows] = energy_of(m) * g
            out[1, i, rows] = cross_energy(m, o) * (2.0 * g)
            out[2, i, rows] = energy_of(o) * g

    def main_step(i, _):
        main_plane(i + 1, (i + 1) & 1)
        energies(i, gf.at[i + 1], px)
        return 0

    def end_step(j, _):
        end_plane(j + 1, (j + 1) & 1)
        energies(j, gpk.at[j], pp)
        return 0

    main_plane(jnp.int32(0), 0)
    lax.fori_loop(0, 20, main_step, 0)
    end_plane(0, 0)
    lax.fori_loop(0, 8, end_step, 0)

    def parts_of(src, k, x, dst):
        f0 = src[k, x + 2]
        f1 = src[k, x + 1] + src[k, x + 3]
        f2 = src[k, x] + src[k, x + 4]
        for n, part in enumerate(x_parts(f0, f1, f2).values()):
            dst[k, n, 0, 0:24] = part

    def end_cone(j, _):
        for k in range(3):
            parts_of(pp, k, j, ap)
            b = cone_yz(ap.at[k], 0, (4, 20))
            bp[k, j, 0] = b[1]
            bp[k, j, 1] = b[2]
        return 0

    lax.fori_loop(0, 4, end_cone, 0)
    lane16 = lane_of((NYL, 128))
    for chunk in range(4):

        def cone_step(j, _):
            x = 4 * chunk + j
            for k in range(3):
                parts_of(px, k, x, av)
                b0, b1, b2 = cone_yz(av.at[k], 0, (4, 20))
                e1, e2 = bp[k, j, 0], bp[k, j, 1]
                n1 = jnp.where(lane16 == 127, roll(e1, 127 - 32 * chunk), roll(b1, -1))
                p1 = jnp.where(lane16 == 0, roll(e1, -(32 * chunk + 27)), roll(b1, 1))
                n2 = jnp.where(lane16 >= 126, roll(e2, 126 - 32 * chunk), roll(b2, -2))
                p2 = jnp.where(lane16 < 2, roll(e2, -(32 * chunk + 26)), roll(b2, 2))
                out_ref[k, x] = b0 + (n1 + p1) + (n2 + p2)
            return 0

        lax.fori_loop(0, 4, cone_step, 0)


def final_kernel(sum_ref, rx, qx, cones, disp_ref, sens_ref):
    line = jnp.sum(sum_ref[...], axis=0, keepdims=True)
    lane1 = lane_of((1, 128))
    m0, m1, m2, m3 = [jnp.sum(jnp.where(lane1 == n, line, 0.0), axis=1, keepdims=True) for n in range(4)]
    m3 = m3 + spring_rate * m2
    first = m0 / m1
    norm = m0 - 2.0 * first * m1 + first * first * m2
    grown = 1.0 + norm / m0
    second = norm / (grown * grown * m1 - 2.0 * first * grown * m2 + first * first * m3)
    c0 = jnp.broadcast_to(first + second * grown, (NYL, 128))
    c1 = jnp.broadcast_to(-second * first, (NYL, 128))

    def step(x, _):
        for c in range(3):
            disp_ref[c, x] = c0 * rx[c, x + 3, 4:20] + c1 * qx[c, x + 2, 4:20]
        sens_ref[x] = c0 * (c0 * cones[0, x] + c1 * cones[1, x]) + c1 * c1 * cones[2, x]
        return 0

    lax.fori_loop(0, 16, step, 0)


def s(*shape):
    return jax.ShapeDtypeStruct(shape, jnp.float32)


def v(*shape):
    return pltpu.VMEM(shape, jnp.float32)


def call(kernel, outs, scratch, *args, smem=0, hbm=0, flush=(), **kw):
    spec_s, spec_v = pl.BlockSpec(memory_space=pltpu.SMEM), pl.BlockSpec(memory_space=pltpu.VMEM)
    single = not isinstance(outs, (tuple, list))
    outs = [outs] if single else list(outs)
    if not INTERPRET:
        outs = [o if i in flush else pltpu.VMEM(o.shape, o.dtype) for i, o in enumerate(outs)]
        args = [
            a if i < smem else pltpu.with_memory_space_constraint(a, pltpu.HBM if i < smem + hbm else pltpu.VMEM)
            for i, a in enumerate(args)
        ]
    return pl.pallas_call(
        kernel,
        out_shape=outs[0] if single else outs,
        in_specs=[spec_s] * smem
        + [pl.BlockSpec(memory_space=pltpu.HBM)] * hbm
        + [spec_v] * (len(args) - smem - hbm),
        out_specs=spec_v if single else [spec_v] * len(outs),
        scratch_shapes=scratch,
        interpret=INTERPRET,
        compiler_params=pltpu.CompilerParams(vmem_limit_bytes=24 << 20),
        **kw,
    )(*args)


def moved(block, axis, step):
    count = lax.axis_size(axis)
    return lax.ppermute(block, axis, [(i, i - step) for i in range(count) if 0 <= i - step < count])


def body(load, design, solid_map):
    sizes = tuple(lax.axis_size(a) * n for a, n in zip(ALL, (NXL, NYL, NZL)))
    count = lax.axis_size("gx") * lax.axis_size("gy") * lax.axis_size("gz")

    def sized(kernel):
        return lambda *refs: kernel(*refs, sizes=sizes)

    load, design, zc = call(
        pack_z_kernel, (s(3, 16, 16, 128), s(16, 16, 128), s(8, 16, 128)), [pltpu.SemaphoreType.DMA((4,))],
        load, design, hbm=2,
    )
    zhi, zlo = moved(zc, "gz", 1), moved(zc, "gz", -1)
    qk, fl, cl = call(
        sized(place_kernel), (s(6, 2, 24, 128), s(3, 2, 24, 128), s(2, 24, 128)), [], solid_map, zc, smem=1
    )
    ylo_s, yhi_s = call(pack_y_kernel, (s(39, 8, 128), s(39, 8, 128)), [], load, design, zhi, zlo, cl)
    yhi, ylo = moved(ylo_s, "gy", 1), moved(yhi_s, "gy", -1)
    rx_t, dx_t, mo_t, gf_t = s(3, 23, 24, 128), s(26, 2, 32, 128), s(22, 2, 24, 128), s(22, 24, 128)
    dens_t, qx_t = s(16, 16, 128), s(3, 21, 24, 128)
    rx, rxt, dx, xlo_s, xhi_s = call(
        pack_x_kernel, (rx_t, rx_t, dx_t, s(544, 128), s(472, 128)), [v(8, 32, 128)],
        load, design, zhi, zlo, ylo, yhi,
    )
    xhi, xlo = moved(xlo_s, "gx", 1), moved(xhi_s, "gx", -1)
    scratch = [
        v(2, 7, 2, 32, 128), v(2, 6, 2, 32, 128), v(2, 2, 12, 2, 24, 128), v(2, 12, 2, 24, 128),
        v(2, 2, 6, 2, 24, 128), v(2, 2, 6, 2, 32, 128),
    ]
    mo, gf, gft, dens, qx, qxt, acc = call(
        sized(inner_kernel), (mo_t, gf_t, gf_t, dens_t, qx_t, qx_t, s(4, 8, 128)), scratch, rx, rxt, dx, qk, fl, cl
    )
    held = rx_t, rx_t, dx_t, mo_t, gf_t, gf_t, dens_t, qx_t, qx_t
    rx, _, _, _, gf, _, dens, qx, _, rp, qp, gpk, part = call(
        sized(outer_kernel),
        (*held, s(3, 9, 24, 128), s(3, 9, 24, 128), s(8, 24, 128), s(count, 128)), scratch,
        rx, rxt, dx, mo, gf, gft, dens, qx, qxt, acc, xlo, xhi, qk, fl, cl,
        flush=(12,), input_output_aliases={n: n for n in range(len(held))},
    )
    sums = lax.all_to_all(part, ALL, 0, 0, tiled=True)
    cones, dens = call(
        tail_kernel, (s(3, 16, 16, 128), dens_t),
        [
            v(3, 20, 24, 128), v(3, 8, 24, 128), v(6, 2, 32, 128), v(2, 12, 1, 24, 128), v(2, 12, 1, 24, 128),
            v(3, 6, 1, 32, 128), v(3, 6, 1, 32, 128), v(3, 4, 2, 16, 128),
        ],
        rx, qx, gf, rp, qp, gpk, dens, flush=(1,),
    )
    disp, sens = call(
        final_kernel, (s(3, 16, 16, 128), s(16, 16, 128)), [], sums, rx, qx, cones, flush=(0, 1)
    )
    return disp, sens, dens


def solution(mesh):
    nodal, cell = P(None, "gx", "gy", "gz"), P("gx", "gy", "gz")
    return jax.shard_map(
        body, mesh=mesh, in_specs=(nodal, cell, P()), out_specs=(nodal, cell, cell), check_vma=False
    )
```

```python
import math

import jax
import jax.numpy as jnp
import numpy as np
from jax import lax
from jax.experimental import pallas as pl
from jax.experimental.pallas import tpu as pltpu
from jax.sharding import PartitionSpec as P


BRICK = 16
young_floor = 0.001
spring_rate = 0.05
sharpness = 8.0
threshold = 0.5
poisson = 0.3
ALL = ("gx", "gy", "gz")
INTERPRET = False

NXL, NYL, NZL = 16, 16, 128
WIN = 24


def element_matrix():
    lame_first = poisson / ((1.0 + poisson) * (1.0 - 2.0 * poisson))
    shear_mod = 1.0 / (2.0 * (1.0 + poisson))
    elastic = np.zeros((6, 6))
    elastic[:3, :3] = lame_first
    for axis_one in range(3):
        elastic[axis_one, axis_one] += 2.0 * shear_mod
        elastic[axis_one + 3, axis_one + 3] = shear_mod
    gauss_point = 1.0 / math.sqrt(3.0)
    stiffness = np.zeros((24, 24))
    for point_x in (-gauss_point, gauss_point):
        for point_y in (-gauss_point, gauss_point):
            for point_z in (-gauss_point, gauss_point):
                strain = np.zeros((6, 24))
                for corner in range(8):
                    sign_a = 2 * (corner // 4) - 1
                    sign_b = 2 * (corner // 2 % 2) - 1
                    sign_c = 2 * (corner % 2) - 1
                    along_x = 0.25 * sign_a * (1 + sign_b * point_y) * (1 + sign_c * point_z)
                    along_y = 0.25 * (1 + sign_a * point_x) * sign_b * (1 + sign_c * point_z)
                    along_z = 0.25 * (1 + sign_a * point_x) * (1 + sign_b * point_y) * sign_c
                    column = 3 * corner
                    strain[0, column] = along_x
                    strain[1, column + 1] = along_y
                    strain[2, column + 2] = along_z
                    strain[3, column + 1] = along_z
                    strain[3, column + 2] = along_y
                    strain[4, column] = along_z
                    strain[4, column + 2] = along_x
                    strain[5, column] = along_y
                    strain[5, column + 1] = along_x
                stiffness += strain.T @ elastic @ strain * 0.125
    return stiffness


def modal_constants():
    modes = [(px, py, pz) for px in (0, 1) for py in (0, 1) for pz in (0, 1)]
    change = np.zeros((24, 24))
    for c in range(3):
        for m, mode in enumerate(modes):
            for q in range(8):
                corner = (q // 4, q // 2 % 2, q % 2)
                sign = 1.0
                for axis in range(3):
                    if mode[axis] and not corner[axis]:
                        sign = -sign
                change[8 * c + m, 3 * q + c] = sign
    hat = change @ element_matrix() @ change.T / 64.0

    def at(c1, m1, c2, m2):
        return hat[8 * c1 + modes.index(m1), 8 * c2 + modes.index(m2)]

    k = {
        "a": at(0, (1, 0, 0), 0, (1, 0, 0)),
        "b": at(0, (1, 0, 0), 1, (0, 1, 0)),
        "p": at(0, (0, 1, 1), 0, (0, 1, 1)),
        "r": at(0, (0, 1, 1), 1, (1, 0, 1)),
        "g": at(0, (0, 1, 0), 1, (1, 0, 0)),
        "h": at(2, (1, 1, 1), 2, (1, 1, 1)),
        "c": at(1, (1, 1, 0), 1, (1, 1, 0)),
        "d": at(1, (1, 1, 0), 2, (1, 0, 1)),
    }
    made = np.zeros((24, 24))

    def put(c1, m1, c2, m2, v):
        made[8 * c1 + modes.index(m1), 8 * c2 + modes.index(m2)] += v

    for c in range(3):
        unit = tuple(int(i == c) for i in range(3))
        anti = tuple(int(i != c) for i in range(3))
        put(c, (1, 1, 1), c, (1, 1, 1), k["h"])
        for e in range(3):
            unit_e = tuple(int(i == e) for i in range(3))
            anti_e = tuple(int(i != e) for i in range(3))
            put(c, unit, e, unit_e, k["a"] if c == e else k["b"])
            put(c, anti, e, anti_e, k["p"] if c == e else k["r"])
            if c != e:
                put(c, unit_e, c, unit_e, k["g"])
                put(c, unit_e, e, unit, k["g"])
                both = tuple(int(i in (c, e)) for i in range(3))
                o = 3 - c - e
                both_o = tuple(int(i in (o, e)) for i in range(3))
                put(c, both, c, both, k["c"])
                put(c, both, o, both_o, k["d"])
    assert np.abs(made - hat).max() < 1e-12
    return k


K = modal_constants()
W = {n: 3.0 - math.sqrt(n) for n in range(9)}
KS = (0, 1, 2, 4, 5, 8)


def mode(*axes):
    return tuple(int(i in axes) for i in range(3))


def f32(x):
    return float(np.float32(x))


def roll(x, shift):
    shift = shift % 128
    return x if shift == 0 else pltpu.roll(x, shift, 1)


def lane_of(shape):
    return lax.broadcasted_iota(jnp.int32, shape, 1)


def z_next(a0, a1, lane, by=1):
    r0, r1 = roll(a0, -by), roll(a1, -by)
    edge = lane >= 128 - by
    return jnp.where(edge, r1, r0), jnp.where(edge, r0, r1)


def z_prev(a0, a1, lane, by=1):
    r0, r1 = roll(a0, by), roll(a1, by)
    edge = lane < by
    return jnp.where(edge, r1, r0), jnp.where(edge, r0, r1)


def modal_of(lo, hi):
    m = {}
    for (c, py, pz), low in lo.items():
        high = hi[c, py, pz]
        if py or pz:
            m[c, (0, py, pz)] = low + high
        m[c, (1, py, pz)] = high - low
    return m


def forces_of(m, e):
    ea, eb = e * f32(K["a"] - K["b"]), e * f32(K["b"])
    ep, er = e * f32(K["p"] - K["r"]), e * f32(K["r"])
    eg, eh = e * f32(K["g"]), e * f32(K["h"])
    ec, ed = e * f32(K["c"]), e * f32(K["d"])
    f = {}
    for first, second, pick in ((ea, eb, lambda c: mode(c)), (ep, er, lambda c: mode(*{0, 1, 2} - {c}))):
        vals = [m[c, pick(c)] for c in range(3)]
        shared = (vals[0] + vals[1] + vals[2]) * second
        for c in range(3):
            f[c, pick(c)] = vals[c] * first + shared
    for c, e2 in ((0, 1), (0, 2), (1, 2)):
        shared = (m[c, mode(e2)] + m[e2, mode(c)]) * eg
        f[c, mode(e2)] = shared
        f[e2, mode(c)] = shared
    for c in range(3):
        f[c, (1, 1, 1)] = m[c, (1, 1, 1)] * eh
    for e2 in range(3):
        c, o = [i for i in range(3) if i != e2]
        v1, v2 = m[c, mode(c, e2)], m[o, mode(o, e2)]
        f[c, mode(c, e2)] = v1 * ec + v2 * ed
        f[o, mode(o, e2)] = v2 * ec + v1 * ed
    return f


def energy_of(m):
    total = None
    for first, second, pick in (
        (K["a"] - K["b"], K["b"], lambda c: mode(c)),
        (K["p"] - K["r"], K["r"], lambda c: mode(*{0, 1, 2} - {c})),
    ):
        vals = [m[c, pick(c)] for c in range(3)]
        s = vals[0] + vals[1] + vals[2]
        part = (vals[0] * vals[0] + vals[1] * vals[1] + vals[2] * vals[2]) * f32(first) + s * s * f32(second)
        total = part if total is None else total + part
    shear = None
    for c, e2 in ((0, 1), (0, 2), (1, 2)):
        s = m[c, mode(e2)] + m[e2, mode(c)]
        shear = s * s if shear is None else shear + s * s
    total = total + shear * f32(K["g"])
    triple = None
    for c in range(3):
        v = m[c, (1, 1, 1)]
        triple = v * v if triple is None else triple + v * v
    total = total + triple * f32(K["h"])
    squares = cross = None
    for e2 in range(3):
        c, o = [i for i in range(3) if i != e2]
        v1, v2 = m[c, mode(c, e2)], m[o, mode(o, e2)]
        sq, cr = v1 * v1 + v2 * v2, v1 * v2
        squares = sq if squares is None else squares + sq
        cross = cr if cross is None else cross + cr
    return total + squares * f32(K["c"]) + cross * f32(2.0 * K["d"])


def x_parts(f0, f1, f2):
    out = {}
    for k in KS:
        v = f0 * f32(W[k])
        if k + 1 in W:
            v = v + f1 * f32(W[k + 1])
        if k + 4 in W:
            v = v + f2 * f32(W[k + 4])
        out[k] = v
    return out


def pack_z_kernel(load_hbm, design_hbm, load_ref, design_ref, out_ref, sems):
    copies = [pltpu.make_async_copy(load_hbm.at[c], load_ref.at[c], sems.at[c]) for c in range(3)]
    copies.append(pltpu.make_async_copy(design_hbm, design_ref, sems.at[3]))
    for one in copies:
        one.start()
    for one in copies:
        one.wait()
    lane = lane_of((NYL, 128))

    def step(pair, _):
        acc = jnp.zeros((NYL, 128), jnp.float32)
        for par in range(2):
            for fld in range(4):
                off = 64 * par + 16 * fld
                src = load_ref[fld, 2 * pair + par] if fld < 3 else design_ref[2 * pair + par]
                acc = jnp.where(((lane - off + 8) & 127) < 16, roll(src, off), acc)
        out_ref[pair] = acc
        return 0

    lax.fori_loop(0, 8, step, 0)


def halo_merge(high, low):
    lane = lane_of(high.shape)
    return jnp.where((lane & 15) < 8, high, low)


def pack_y_kernel(load_ref, design_ref, zhi_ref, zlo_ref, place_ref, lo_ref, hi_ref):
    del place_ref
    for dst, quad, one in ((lo_ref, 0, 4), (hi_ref, 12, 11)):
        rows = slice(quad, quad + 4)
        for x in range(16):
            dst[x, 0:4] = load_ref[0, x, rows]
            dst[x, 4:8] = load_ref[1, x, rows]
            dst[16 + x, 0:4] = load_ref[2, x, rows]
            dst[16 + x, 4:8] = design_ref[x, rows]
            dst[32 + x // 8, x % 8 : x % 8 + 1] = design_ref[x, one : one + 1]
        for k in range(8):
            dst[35 + k // 2, 4 * (k % 2) : 4 * (k % 2) + 4] = halo_merge(zhi_ref[k, rows], zlo_ref[k, rows])
            dst[34, k : k + 1] = halo_merge(zhi_ref[k, one : one + 1], zlo_ref[k, one : one + 1])


def pack_x_kernel(load_ref, design_ref, zhi_ref, zlo_ref, ylo_ref, yhi_ref, rx, rxt, dx, lo_ref, hi_ref, hx):
    none = jnp.zeros((8, 128), jnp.float32)
    for k in range(8):
        half = slice(4 * (k % 2), 4 * (k % 2) + 4)
        hx[k, 0:8] = none
        hx[k, 24:32] = none
        hx[k, 3:4] = ylo_ref[34, k : k + 1]
        hx[k, 4:8] = ylo_ref[35 + k // 2, half]
        hx[k, 8:24] = halo_merge(zhi_ref[k], zlo_ref[k])
        hx[k, 24:28] = yhi_ref[35 + k // 2, half]
        hx[k, 28:29] = yhi_ref[34, k : k + 1]
    for x in range(16):
        for c in range(3):
            tile, half = (x, slice(4 * c, 4 * c + 4)) if c < 2 else (16 + x, slice(0, 4))
            rx[c, x + 3, 0:4] = ylo_ref[tile, half]
            rx[c, x + 3, 4:20] = load_ref[c, x]
            rx[c, x + 3, 20:24] = yhi_ref[tile, half]
        one = slice(x % 8, x % 8 + 1)
        dx[x + 5, 0, 0:8] = none
        dx[x + 5, 0, 24:32] = none
        dx[x + 5, 0, 3:4] = ylo_ref[32 + x // 8, one]
        dx[x + 5, 0, 4:8] = ylo_ref[16 + x, 4:8]
        dx[x + 5, 0, 8:24] = design_ref[x]
        dx[x + 5, 0, 24:28] = yhi_ref[16 + x, 4:8]
        dx[x + 5, 0, 28:29] = yhi_ref[32 + x // 8, one]
    for i in range(5):
        lo_ref[288 + 32 * i : 320 + 32 * i] = dx[5 + i, 0]
        hi_ref[216 + 32 * i : 248 + 32 * i] = dx[16 + i, 0]
    for i in range(3):
        lo_ref[448 + 32 * i : 480 + 32 * i] = hx[i]
        hi_ref[376 + 32 * i : 408 + 32 * i] = hx[5 + i]
    for c in range(3):
        for i in range(4):
            lo_ref[24 * (4 * c + i) : 24 * (4 * c + i) + 24] = rx[c, 3 + i]
        for i in range(3):
            hi_ref[24 * (3 * c + i) : 24 * (3 * c + i) + 24] = rx[c, 16 + i]
    for k in range(8):
        spread_pair(hx[k], 2 * k, (2 * k, 2 * k + 1), rxt, dx, True)


def spread_pair(tile, x, wanted, rxt, dx, both):
    for par in range(2):
        if x + par in wanted:
            dx[x + par + 5, 1] = roll(tile, -(64 * par + 48))
            if both or -3 <= x + par <= 19:
                for c in range(3):
                    rxt[c, x + par + 3] = roll(tile, -(64 * par + 16 * c))[4:28]


def x_halos(xlo_ref, xhi_ref, rx, rxt, dx):
    for c in range(3):
        for i in range(4):
            rx[c, 19 + i] = xhi_ref[24 * (4 * c + i) : 24 * (4 * c + i) + 24]
        for i in range(3):
            rx[c, i] = xlo_ref[24 * (3 * c + i) : 24 * (3 * c + i) + 24]
    for i in range(5):
        dx[21 + i, 0] = xhi_ref[288 + 32 * i : 320 + 32 * i]
        dx[i, 0] = xlo_ref[216 + 32 * i : 248 + 32 * i]
    for i in range(3):
        spread_pair(xhi_ref[448 + 32 * i : 480 + 32 * i], 16 + 2 * i, range(16, 21), rxt, dx, False)
        spread_pair(xlo_ref[376 + 32 * i : 408 + 32 * i], -6 + 2 * i, range(-5, 0), rxt, dx, False)


def place_kernel(map_ref, order_ref, qk, fl, cl, *, sizes):
    del order_ref
    nx, ny, nz = sizes
    i_x, i_y, i_z = (lax.axis_index(a) for a in ALL)
    lane = lane_of((WIN, 128))
    row = lax.broadcasted_iota(jnp.int32, (WIN, 128), 0)
    y_at = i_y * NYL + row - 4
    z_at = [i_z * NZL + lane, i_z * NZL + jnp.where(lane < 64, lane + 128, lane - 128)]

    def inside(at, step, length):
        return jnp.where((at + step >= 0) & (at + step < length), 1.0, 0.0)

    y_in = [inside(y_at, 0, ny)] + [inside(y_at, s, ny) + inside(y_at, -s, ny) for s in (1, 2)]
    for t in range(2):
        z_in = [inside(z_at[t], 0, nz)] + [inside(z_at[t], s, nz) + inside(z_at[t], -s, nz) for s in (1, 2)]
        qk[0, t] = y_in[0] * z_in[0]
        qk[1, t] = y_in[1] * z_in[0] + y_in[0] * z_in[1]
        qk[2, t] = y_in[1] * z_in[1]
        qk[3, t] = y_in[2] * z_in[0] + y_in[0] * z_in[2]
        qk[4, t] = y_in[1] * z_in[2] + y_in[2] * z_in[1]
        qk[5, t] = y_in[2] * z_in[2]
        cl[t] = y_in[0] * z_in[0]
    gbx, gby, gbz = nx // BRICK, ny // BRICK, nz // BRICK
    bricks = NZL // BRICK

    def flag_at(bx, by, bz):
        ok = (bx >= 0) & (bx < gbx) & (by >= 0) & (by < gby) & (bz >= 0) & (bz < gbz)
        value = map_ref[jnp.clip(bx, 0, gbx - 1), jnp.clip(by, 0, gby - 1), jnp.clip(bz, 0, gbz - 1)]
        return jnp.where(ok, value, 0).astype(jnp.float32)

    for xc in range(3):
        lines = []
        for yc in range(3):
            flag = [flag_at(i_x + xc - 1, i_y + yc - 1, i_z * bricks + n - 1) for n in range(bricks + 2)]
            main = jnp.zeros((WIN, 128), jnp.float32)
            for n in range(bricks):
                main = jnp.where((lane >> 4) == n, flag[n + 1], main)
            lines.append((main, jnp.where(lane < 64, flag[bricks + 1], flag[0])))
        for t in range(2):
            fl[xc, t] = jnp.where(row < 4, lines[0][t], jnp.where(row < 20, lines[1][t], lines[2][t]))


def zy_plane(tile, zt, t_ref, slot, lane, tiles=2, base=0, blocks=3):
    for c in range(3):
        a0, a1 = tile(c, 0), tile(c, 1)
        n0, n1 = z_next(a0, a1, lane)
        zt[2 * c, 0, 0:24] = a0 + n0
        zt[2 * c + 1, 0, 0:24] = n0 - a0
        if tiles == 2:
            zt[2 * c, 1, 0:24] = a1 + n1
            zt[2 * c + 1, 1, 0:24] = n1 - a1
    for f in range(6):
        for t in range(tiles):
            for b in range(blocks):
                r = base + 8 * b
                lo, hi = zt[f, t, r : r + 8], zt[f, t, r + 1 : r + 9]
                t_ref[slot, 2 * f, t, 8 * b : 8 * b + 8] = lo + hi
                t_ref[slot, 2 * f + 1, t, 8 * b : 8 * b + 8] = hi - lo


def read_t(t_ref, slot, t, b):
    out = {}
    for c in range(3):
        for pz in range(2):
            for py in range(2):
                out[c, py, pz] = t_ref[slot, 4 * c + 2 * pz + py, t, 8 * b : 8 * b + 8]
    return out


LIFT = math.tanh(sharpness * threshold)
SCALE = LIFT + math.tanh(sharpness * (1.0 - threshold))


def cone_yz(av, t, rows):
    lo, hi = rows

    def at(n, step):
        return av[n, t, lo + step : hi + step]

    def both(n, step):
        return at(n, -step) + at(n, step)

    return [
        at(0, 0) + both(1, 1) + both(3, 2),
        at(1, 0) + both(2, 1) + both(4, 2),
        at(3, 0) + both(4, 1) + both(5, 2),
    ]


def density_plane(e, own, nx, dx, qk, fl, av, mo, gfs, dens_ref):
    lane = lane_of((WIN, 128))
    x_at = lax.axis_index("gx") * NXL + e - 3

    def scalar_inside(at, step):
        return jnp.where((at + step >= 0) & (at + step < nx), 1.0, 0.0)

    for t in range(2):
        f0 = dx[e + 2, t]
        f1 = dx[e + 1, t] + dx[e + 3, t]
        f2 = dx[e, t] + dx[e + 4, t]
        for n, part in enumerate(x_parts(f0, f1, f2).values()):
            av[n, t] = part
    x0 = scalar_inside(x_at, 0)
    x1 = scalar_inside(x_at, 1) + scalar_inside(x_at, -1)
    x2 = scalar_inside(x_at, 2) + scalar_inside(x_at, -2)
    cls = jnp.where(e < 3, 0, jnp.where(e < 19, 1, 2))
    b = [cone_yz(av, t, (4, 28)) for t in range(2)]
    n1, p1 = z_next(b[0][1], b[1][1], lane), z_prev(b[0][1], b[1][1], lane)
    n2, p2 = z_next(b[0][2], b[1][2], lane, 2), z_prev(b[0][2], b[1][2], lane, 2)
    weights = x_parts(x0, x1, x2)
    for t in range(2):
        cone = b[t][0] + (n1[t] + p1[t]) + (n2[t] + p2[t])
        ws = None
        for n, wk in enumerate(weights.values()):
            ws = qk[n, t] * wk if ws is None else ws + qk[n, t] * wk
        inv = 1.0 / jnp.maximum(ws, 1.0)
        th = jnp.tanh(sharpness * (cone * inv - threshold))
        dens = (LIFT + th) * f32(1.0 / SCALE)
        flag = fl[cls, t]
        sq = dens * dens
        mo[e, t] = (young_floor + sq * dens * (1.0 - young_floor)) * flag
        gfs[t][e] = sq * flag * (1.0 - th * th) * inv * f32(-3.0 * (1.0 - young_floor) * sharpness / SCALE)
        if t == 0:
            av[6, 0, 0:24] = dens
    dens_ref[own] = av[6, 0, 4:20]


def operate_planes(firsts, count, nx, rs, mo, cl, qs, zt, tt, gp, yp, yg):
    lane = lane_of((WIN, 128))
    i_x = lax.axis_index("gx")
    for n, first in enumerate(firsts):
        zy_plane(lambda c, t: rs[t][c, first], zt.at[n], tt.at[n], 0, lane)

    def transposes(n, first, i):
        e = first + jnp.maximum(i, 0)
        slot = i & 1
        x_on = jnp.where(i_x * NXL + e - 3 < nx, 1.0, 0.0)
        to = first + jnp.maximum(i - 1, 0)
        for c in range(3):
            p, g = [], []
            for t in range(2):
                zs = yp[n, slot, 2 * c, t] + yg[n, slot, 2 * c, t, 7:31]
                zd = yp[n, slot, 2 * c + 1, t] + yg[n, slot, 2 * c + 1, t, 7:31]
                p.append(zs - zd)
                g.append(zs + zd)
            gb = z_prev(g[0], g[1], lane)
            for t in range(2):
                value = p[t] + gb[t] + rs[t][c, e] * spring_rate
                qs[t][c, to] = value * (cl[t] * x_on)

    def forces(n, first, i):
        new, old = (i + 1) & 1, i & 1
        e = first + i
        zy_plane(lambda c, t: rs[t][c, e + 1], zt.at[n], tt.at[n], new, lane)
        for t in range(2):
            for b in range(3):
                rows = slice(8 * b, 8 * b + 8)
                force = forces_of(
                    modal_of(read_t(tt.at[n], old, t, b), read_t(tt.at[n], new, t, b)), mo[e, t, rows]
                )
                for c in range(3):
                    for pz in range(2):
                        m = []
                        for py in range(2):
                            fd = force[c, (1, py, pz)]
                            fs = force.get((c, (0, py, pz)))
                            at = 4 * c + 2 * pz + py
                            before = gp[n, at, t, rows]
                            if fs is None:
                                gp[n, at, t, rows] = fd
                                m.append(before - fd)
                            else:
                                gp[n, at, t, rows] = fs + fd
                                m.append((fs - fd) + before)
                        yp[n, old, 2 * c + pz, t, rows] = m[0] - m[1]
                        yg[n, old, 2 * c + pz, t, 8 + 8 * b : 16 + 8 * b] = m[0] + m[1]

    def step(i, _):
        for n, first in enumerate(firsts):
            transposes(n, first, i - 1)
            forces(n, first, i)
        return 0

    lax.fori_loop(0, count, step, 0)
    for n, first in enumerate(firsts):
        transposes(n, first, jnp.int32(count - 1))


def sum_planes(firsts, count, acc, rs, qs, mo, zt, tt):
    lane = lane_of((WIN, 128))

    def plane(n, x, slot):
        zy_plane(lambda c, t: qs[t][c, x + 2], zt.at[n], tt.at[n], slot, lane, tiles=1, base=4, blocks=2)

    for n, first in enumerate(firsts):
        plane(n, first, 0)

    def step(i, acc):
        s0, s1, s2, s3 = acc
        new, old = (i + 1) & 1, i & 1
        for n, first in enumerate(firsts):
            x = first + i
            plane(n, x + 1, new)
            for b in range(2):
                rows = slice(4 + 8 * b, 12 + 8 * b)
                for c in range(3):
                    r, q = rs[0][c, x + 3, rows], qs[0][c, x + 2, rows]
                    s0, s1, s2 = s0 + r * r, s1 + r * q, s2 + q * q
                m = modal_of(read_t(tt.at[n], old, 0, b), read_t(tt.at[n], new, 0, b))
                s3 = s3 + energy_of(m) * mo[x + 3, 0, rows]
        return s0, s1, s2, s3

    return lax.fori_loop(0, count, step, acc)


def inner_kernel(
    rx, rxt, dx, qk, fl, cl, mo, gf, gft, dens_ref, qx, qxt, acc_ref, av, zt, tt, gp, yp, yg, *, sizes
):
    nx = sizes[0]

    def density_step(i, _):
        for n in range(2):
            e = 5 + i + 6 * n
            density_plane(e, e - 3, nx, dx, qk, fl, av.at[n], mo, (gf, gft), dens_ref)
        return 0

    lax.fori_loop(0, 6, density_step, 0)
    operate_planes((5,), 12, nx, (rx, rxt), mo, cl, (qx, qxt), zt, tt, gp, yp, yg)
    zero = jnp.zeros((8, 128), jnp.float32)
    for n, part in enumerate(sum_planes((3, 8), 5, (zero,) * 4, (rx, rxt), (qx, qxt), mo, zt, tt)):
        acc_ref[n] = part


def outer_kernel(
    rx_in, rxt_in, dx_in, mo_in, gf_in, gft_in, dens_in, qx_in, qxt_in, acc_ref, xlo_ref, xhi_ref, qk, fl, cl,
    rx, rxt, dx, mo, gf, gft, dens_ref, qx, qxt, rp, qp, gpk, sum_ref, av, zt, tt, gp, yp, yg, *, sizes
):
    del rx_in, rxt_in, dx_in, mo_in, gf_in, gft_in, dens_in, qx_in, qxt_in
    nx = sizes[0]
    rs, qs, gfs = (rx, rxt), (qx, qxt), (gf, gft)
    x_halos(xlo_ref, xhi_ref, rx, rxt, dx)

    def density_step(i, _):
        density_plane(i, jnp.maximum(i - 3, 0), nx, dx, qk, fl, av.at[0], mo, gfs, dens_ref)
        density_plane(21 - i, jnp.minimum(18 - i, 15), nx, dx, qk, fl, av.at[1], mo, gfs, dens_ref)
        return 0

    lax.fori_loop(0, 5, density_step, 0)
    operate_planes((0, 16), 6, nx, rs, mo, cl, qs, zt, tt, gp, yp, yg)
    acc = tuple(acc_ref[n] for n in range(4))
    acc = sum_planes((0, 13), 3, acc, rs, qs, mo, zt, tt)
    line = jnp.zeros((8, 128), jnp.float32)
    lane = lane_of((8, 128))
    for n, part in enumerate(acc):
        total = jnp.sum(jnp.sum(part, axis=0, keepdims=True), axis=1, keepdims=True)
        line = jnp.where(lane == n, total, line)
    for n in range(sum_ref.shape[0] // 8):
        sum_ref[8 * n : 8 * n + 8] = line

    def pack_step(j, _):
        for c in range(3):
            rp[c, j] = pack_chunks([(rx[c, 4 * k + j + 1], rxt[c, 4 * k + j + 1]) for k in range(4)])
            qp[c, j] = pack_chunks([(qx[c, 4 * k + j], qxt[c, 4 * k + j]) for k in range(4)])
        return 0

    lax.fori_loop(0, 9, pack_step, 0, unroll=3)

    def pack_weights(j, _):
        gpk[j] = pack_chunks([(gf[4 * k + j + 1], gft[4 * k + j + 1]) for k in range(4)])
        return 0

    lax.fori_loop(0, 8, pack_weights, 0)


def pack_chunks(tiles):
    lane = lane_of((WIN, 128))
    out = None
    for k, (main, side) in enumerate(tiles):
        high = roll(side, 32 * k)
        low = roll(jnp.where(lane >= 64, side, main), 32 * k + 28)
        out = high if out is None else jnp.where(lane >= 32 * k, high, out)
        out = jnp.where(lane >= 32 * k + 16, low, out)
    return out


def cross_energy(m, o):
    total = None
    for first, second, pick in (
        (K["a"] - K["b"], K["b"], lambda c: mode(c)),
        (K["p"] - K["r"], K["r"], lambda c: mode(*{0, 1, 2} - {c})),
    ):
        vm, vo = [m[c, pick(c)] for c in range(3)], [o[c, pick(c)] for c in range(3)]
        sm, so = vm[0] + vm[1] + vm[2], vo[0] + vo[1] + vo[2]
        part = (vm[0] * vo[0] + vm[1] * vo[1] + vm[2] * vo[2]) * f32(first) + sm * so * f32(second)
        total = part if total is None else total + part
    shear = None
    for c, e2 in ((0, 1), (0, 2), (1, 2)):
        v = (m[c, mode(e2)] + m[e2, mode(c)]) * (o[c, mode(e2)] + o[e2, mode(c)])
        shear = v if shear is None else shear + v
    triple = None
    for c in range(3):
        v = m[c, (1, 1, 1)] * o[c, (1, 1, 1)]
        triple = v if triple is None else triple + v
    same = cross = None
    for e2 in range(3):
        c, d = [i for i in range(3) if i != e2]
        m1, m2 = m[c, mode(c, e2)], m[d, mode(d, e2)]
        o1, o2 = o[c, mode(c, e2)], o[d, mode(d, e2)]
        sq, cr = m1 * o1 + m2 * o2, m1 * o2 + m2 * o1
        same = sq if same is None else same + sq
        cross = cr if cross is None else cross + cr
    total = total + shear * f32(K["g"]) + triple * f32(K["h"])
    return total + same * f32(K["c"]) + cross * f32(K["d"])


def tail_kernel(rx, qx, gf, rp, qp, gpk, dens_in, out_ref, dens_ref, px, pp, zt, tr, tq, av, ap, bp):
    dens_ref[...] = dens_in[...]
    lane = lane_of((WIN, 128))
    edge = lane == 127

    def half_plane(at, after, t_ref, slot):
        for c in range(3):
            a = at(c)
            n = after(c, a)
            zt[2 * c, 0, 0:24] = a + n
            zt[2 * c + 1, 0, 0:24] = n - a
        for f in range(6):
            for b in range(3):
                lo, hi = zt[f, 0, 8 * b : 8 * b + 8], zt[f, 0, 8 * b + 1 : 8 * b + 9]
                t_ref[slot, 2 * f, 0, 8 * b : 8 * b + 8] = lo + hi
                t_ref[slot, 2 * f + 1, 0, 8 * b : 8 * b + 8] = hi - lo

    def main_plane(i, slot):
        chunk = jnp.minimum(i >> 2, 3)
        j, shift = i - 4 * chunk, 127 - 32 * chunk

        def after(src):
            return lambda c, a: jnp.where(edge, pltpu.roll(src[c, j], shift, 1), roll(a, -1))

        half_plane(lambda c: rx[c, i + 1], after(rp), tr, slot)
        half_plane(lambda c: qx[c, i], after(qp), tq, slot)

    def end_plane(j, slot):
        half_plane(lambda c: rp[c, j], lambda c, a: roll(a, -1), tr, slot)
        half_plane(lambda c: qp[c, j], lambda c, a: roll(a, -1), tq, slot)

    def energies(i, g_ref, out):
        new, old = (i + 1) & 1, i & 1
        for b in range(3):
            rows = slice(8 * b, 8 * b + 8)
            m = modal_of(read_t(tr, old, 0, b), read_t(tr, new, 0, b))
            o = modal_of(read_t(tq, old, 0, b), read_t(tq, new, 0, b))
            g = g_ref[rows]
            out[0, i, rows] = energy_of(m) * g
            out[1, i, rows] = cross_energy(m, o) * (2.0 * g)
            out[2, i, rows] = energy_of(o) * g

    def main_step(i, _):
        main_plane(i + 1, (i + 1) & 1)
        energies(i, gf.at[i + 1], px)
        return 0

    def end_step(j, _):
        end_plane(j + 1, (j + 1) & 1)
        energies(j, gpk.at[j], pp)
        return 0

    main_plane(jnp.int32(0), 0)
    lax.fori_loop(0, 20, main_step, 0, unroll=2)
    end_plane(0, 0)
    lax.fori_loop(0, 8, end_step, 0)

    def parts_of(src, k, x, dst):
        f0 = src[k, x + 2]
        f1 = src[k, x + 1] + src[k, x + 3]
        f2 = src[k, x] + src[k, x + 4]
        for n, part in enumerate(x_parts(f0, f1, f2).values()):
            dst[k, n, 0, 0:24] = part

    def end_cone(j, _):
        for k in range(3):
            parts_of(pp, k, j, ap)
            b = cone_yz(ap.at[k], 0, (4, 20))
            bp[k, j, 0] = b[1]
            bp[k, j, 1] = b[2]
        return 0

    lax.fori_loop(0, 4, end_cone, 0)
    lane16 = lane_of((NYL, 128))
    for chunk in range(4):

        def cone_step(j, _):
            x = 4 * chunk + j
            for k in range(3):
                parts_of(px, k, x, av)
                b0, b1, b2 = cone_yz(av.at[k], 0, (4, 20))
                e1, e2 = bp[k, j, 0], bp[k, j, 1]
                n1 = jnp.where(lane16 == 127, roll(e1, 127 - 32 * chunk), roll(b1, -1))
                p1 = jnp.where(lane16 == 0, roll(e1, -(32 * chunk + 27)), roll(b1, 1))
                n2 = jnp.where(lane16 >= 126, roll(e2, 126 - 32 * chunk), roll(b2, -2))
                p2 = jnp.where(lane16 < 2, roll(e2, -(32 * chunk + 26)), roll(b2, 2))
                out_ref[k, x] = b0 + (n1 + p1) + (n2 + p2)
            return 0

        lax.fori_loop(0, 4, cone_step, 0)


def final_kernel(sum_ref, rx, qx, cones, disp_ref, sens_ref):
    line = jnp.sum(sum_ref[...], axis=0, keepdims=True)
    lane1 = lane_of((1, 128))
    m0, m1, m2, m3 = [jnp.sum(jnp.where(lane1 == n, line, 0.0), axis=1, keepdims=True) for n in range(4)]
    m3 = m3 + spring_rate * m2
    first = m0 / m1
    norm = m0 - 2.0 * first * m1 + first * first * m2
    grown = 1.0 + norm / m0
    second = norm / (grown * grown * m1 - 2.0 * first * grown * m2 + first * first * m3)
    c0 = jnp.broadcast_to(first + second * grown, (NYL, 128))
    c1 = jnp.broadcast_to(-second * first, (NYL, 128))

    def step(x, _):
        for c in range(3):
            disp_ref[c, x] = c0 * rx[c, x + 3, 4:20] + c1 * qx[c, x + 2, 4:20]
        sens_ref[x] = c0 * (c0 * cones[0, x] + c1 * cones[1, x]) + c1 * c1 * cones[2, x]
        return 0

    lax.fori_loop(0, 16, step, 0)


def s(*shape):
    return jax.ShapeDtypeStruct(shape, jnp.float32)


def v(*shape):
    return pltpu.VMEM(shape, jnp.float32)


def call(kernel, outs, scratch, *args, smem=0, hbm=0, flush=(), **kw):
    spec_s, spec_v = pl.BlockSpec(memory_space=pltpu.SMEM), pl.BlockSpec(memory_space=pltpu.VMEM)
    single = not isinstance(outs, (tuple, list))
    outs = [outs] if single else list(outs)
    if not INTERPRET:
        outs = [o if i in flush else pltpu.VMEM(o.shape, o.dtype) for i, o in enumerate(outs)]
        args = [
            a if i < smem else pltpu.with_memory_space_constraint(a, pltpu.HBM if i < smem + hbm else pltpu.VMEM)
            for i, a in enumerate(args)
        ]
    return pl.pallas_call(
        kernel,
        out_shape=outs[0] if single else outs,
        in_specs=[spec_s] * smem
        + [pl.BlockSpec(memory_space=pltpu.HBM)] * hbm
        + [spec_v] * (len(args) - smem - hbm),
        out_specs=spec_v if single else [spec_v] * len(outs),
        scratch_shapes=scratch,
        interpret=INTERPRET,
        compiler_params=pltpu.CompilerParams(vmem_limit_bytes=24 << 20),
        **kw,
    )(*args)


def moved(block, axis, step):
    count = lax.axis_size(axis)
    return lax.ppermute(block, axis, [(i, i - step) for i in range(count) if 0 <= i - step < count])


def body(load, design, solid_map):
    sizes = tuple(lax.axis_size(a) * n for a, n in zip(ALL, (NXL, NYL, NZL)))
    count = lax.axis_size("gx") * lax.axis_size("gy") * lax.axis_size("gz")

    def sized(kernel):
        return lambda *refs: kernel(*refs, sizes=sizes)

    load, design, zc = call(
        pack_z_kernel, (s(3, 16, 16, 128), s(16, 16, 128), s(8, 16, 128)), [pltpu.SemaphoreType.DMA((4,))],
        load, design, hbm=2,
    )
    zhi, zlo = moved(zc, "gz", 1), moved(zc, "gz", -1)
    qk, fl, cl = call(
        sized(place_kernel), (s(6, 2, 24, 128), s(3, 2, 24, 128), s(2, 24, 128)), [], solid_map, zc, smem=1
    )
    ylo_s, yhi_s = call(pack_y_kernel, (s(39, 8, 128), s(39, 8, 128)), [], load, design, zhi, zlo, cl)
    yhi, ylo = moved(ylo_s, "gy", 1), moved(yhi_s, "gy", -1)
    rx_t, dx_t, mo_t, gf_t = s(3, 23, 24, 128), s(26, 2, 32, 128), s(22, 2, 24, 128), s(22, 24, 128)
    dens_t, qx_t = s(16, 16, 128), s(3, 21, 24, 128)
    rx, rxt, dx, xlo_s, xhi_s = call(
        pack_x_kernel, (rx_t, rx_t, dx_t, s(544, 128), s(472, 128)), [v(8, 32, 128)],
        load, design, zhi, zlo, ylo, yhi,
    )
    xhi, xlo = moved(xlo_s, "gx", 1), moved(xhi_s, "gx", -1)
    scratch = [
        v(2, 7, 2, 32, 128), v(2, 6, 2, 32, 128), v(2, 2, 12, 2, 24, 128), v(2, 12, 2, 24, 128),
        v(2, 2, 6, 2, 24, 128), v(2, 2, 6, 2, 32, 128),
    ]
    mo, gf, gft, dens, qx, qxt, acc = call(
        sized(inner_kernel), (mo_t, gf_t, gf_t, dens_t, qx_t, qx_t, s(4, 8, 128)), scratch, rx, rxt, dx, qk, fl, cl
    )
    held = rx_t, rx_t, dx_t, mo_t, gf_t, gf_t, dens_t, qx_t, qx_t
    rx, _, _, _, gf, _, dens, qx, _, rp, qp, gpk, part = call(
        sized(outer_kernel),
        (*held, s(3, 9, 24, 128), s(3, 9, 24, 128), s(8, 24, 128), s(count, 128)), scratch,
        rx, rxt, dx, mo, gf, gft, dens, qx, qxt, acc, xlo, xhi, qk, fl, cl,
        flush=(12,), input_output_aliases={n: n for n in range(len(held))},
    )
    sums = lax.all_to_all(part, ALL, 0, 0, tiled=True)
    cones, dens = call(
        tail_kernel, (s(3, 16, 16, 128), dens_t),
        [
            v(3, 20, 24, 128), v(3, 8, 24, 128), v(6, 2, 32, 128), v(2, 12, 1, 24, 128), v(2, 12, 1, 24, 128),
            v(3, 6, 1, 32, 128), v(3, 6, 1, 32, 128), v(3, 4, 2, 16, 128),
        ],
        rx, qx, gf, rp, qp, gpk, dens, flush=(1,),
    )
    disp, sens = call(
        final_kernel, (s(3, 16, 16, 128), s(16, 16, 128)), [], sums, rx, qx, cones, flush=(0, 1)
    )
    return disp, sens, dens


def solution(mesh):
    nodal, cell = P(None, "gx", "gy", "gz"), P("gx", "gy", "gz")
    return jax.shard_map(
        body, mesh=mesh, in_specs=(nodal, cell, P()), out_specs=(nodal, cell, cell), check_vma=False
    )
```

```python
import math

import jax
import jax.numpy as jnp
import numpy as np
from jax import lax
from jax.experimental import pallas as pl
from jax.experimental.pallas import tpu as pltpu
from jax.sharding import PartitionSpec as P


BRICK = 16
young_floor = 0.001
spring_rate = 0.05
sharpness = 8.0
threshold = 0.5
poisson = 0.3
ALL = ("gx", "gy", "gz")
INTERPRET = False

NXL, NYL, NZL = 16, 16, 128
WIN = 24


def element_matrix():
    lame_first = poisson / ((1.0 + poisson) * (1.0 - 2.0 * poisson))
    shear_mod = 1.0 / (2.0 * (1.0 + poisson))
    elastic = np.zeros((6, 6))
    elastic[:3, :3] = lame_first
    for axis_one in range(3):
        elastic[axis_one, axis_one] += 2.0 * shear_mod
        elastic[axis_one + 3, axis_one + 3] = shear_mod
    gauss_point = 1.0 / math.sqrt(3.0)
    stiffness = np.zeros((24, 24))
    for point_x in (-gauss_point, gauss_point):
        for point_y in (-gauss_point, gauss_point):
            for point_z in (-gauss_point, gauss_point):
                strain = np.zeros((6, 24))
                for corner in range(8):
                    sign_a = 2 * (corner // 4) - 1
                    sign_b = 2 * (corner // 2 % 2) - 1
                    sign_c = 2 * (corner % 2) - 1
                    along_x = 0.25 * sign_a * (1 + sign_b * point_y) * (1 + sign_c * point_z)
                    along_y = 0.25 * (1 + sign_a * point_x) * sign_b * (1 + sign_c * point_z)
                    along_z = 0.25 * (1 + sign_a * point_x) * (1 + sign_b * point_y) * sign_c
                    column = 3 * corner
                    strain[0, column] = along_x
                    strain[1, column + 1] = along_y
                    strain[2, column + 2] = along_z
                    strain[3, column + 1] = along_z
                    strain[3, column + 2] = along_y
                    strain[4, column] = along_z
                    strain[4, column + 2] = along_x
                    strain[5, column] = along_y
                    strain[5, column + 1] = along_x
                stiffness += strain.T @ elastic @ strain * 0.125
    return stiffness


def modal_constants():
    modes = [(px, py, pz) for px in (0, 1) for py in (0, 1) for pz in (0, 1)]
    change = np.zeros((24, 24))
    for c in range(3):
        for m, mode in enumerate(modes):
            for q in range(8):
                corner = (q // 4, q // 2 % 2, q % 2)
                sign = 1.0
                for axis in range(3):
                    if mode[axis] and not corner[axis]:
                        sign = -sign
                change[8 * c + m, 3 * q + c] = sign
    hat = change @ element_matrix() @ change.T / 64.0

    def at(c1, m1, c2, m2):
        return hat[8 * c1 + modes.index(m1), 8 * c2 + modes.index(m2)]

    k = {
        "a": at(0, (1, 0, 0), 0, (1, 0, 0)),
        "b": at(0, (1, 0, 0), 1, (0, 1, 0)),
        "p": at(0, (0, 1, 1), 0, (0, 1, 1)),
        "r": at(0, (0, 1, 1), 1, (1, 0, 1)),
        "g": at(0, (0, 1, 0), 1, (1, 0, 0)),
        "h": at(2, (1, 1, 1), 2, (1, 1, 1)),
        "c": at(1, (1, 1, 0), 1, (1, 1, 0)),
        "d": at(1, (1, 1, 0), 2, (1, 0, 1)),
    }
    made = np.zeros((24, 24))

    def put(c1, m1, c2, m2, v):
        made[8 * c1 + modes.index(m1), 8 * c2 + modes.index(m2)] += v

    for c in range(3):
        unit = tuple(int(i == c) for i in range(3))
        anti = tuple(int(i != c) for i in range(3))
        put(c, (1, 1, 1), c, (1, 1, 1), k["h"])
        for e in range(3):
            unit_e = tuple(int(i == e) for i in range(3))
            anti_e = tuple(int(i != e) for i in range(3))
            put(c, unit, e, unit_e, k["a"] if c == e else k["b"])
            put(c, anti, e, anti_e, k["p"] if c == e else k["r"])
            if c != e:
                put(c, unit_e, c, unit_e, k["g"])
                put(c, unit_e, e, unit, k["g"])
                both = tuple(int(i in (c, e)) for i in range(3))
                o = 3 - c - e
                both_o = tuple(int(i in (o, e)) for i in range(3))
                put(c, both, c, both, k["c"])
                put(c, both, o, both_o, k["d"])
    assert np.abs(made - hat).max() < 1e-12
    return k


K = modal_constants()
W = {n: 3.0 - math.sqrt(n) for n in range(9)}
KS = (0, 1, 2, 4, 5, 8)


def mode(*axes):
    return tuple(int(i in axes) for i in range(3))


def f32(x):
    return float(np.float32(x))


def roll(x, shift):
    shift = shift % 128
    return x if shift == 0 else pltpu.roll(x, shift, 1)


def lane_of(shape):
    return lax.broadcasted_iota(jnp.int32, shape, 1)


def z_next(a0, a1, lane, by=1):
    r0, r1 = roll(a0, -by), roll(a1, -by)
    edge = lane >= 128 - by
    return jnp.where(edge, r1, r0), jnp.where(edge, r0, r1)


def z_prev(a0, a1, lane, by=1):
    r0, r1 = roll(a0, by), roll(a1, by)
    edge = lane < by
    return jnp.where(edge, r1, r0), jnp.where(edge, r0, r1)


def modal_of(lo, hi):
    m = {}
    for (c, py, pz), low in lo.items():
        high = hi[c, py, pz]
        if py or pz:
            m[c, (0, py, pz)] = low + high
        m[c, (1, py, pz)] = high - low
    return m


def forces_of(m, e):
    ea, eb = e * f32(K["a"] - K["b"]), e * f32(K["b"])
    ep, er = e * f32(K["p"] - K["r"]), e * f32(K["r"])
    eg, eh = e * f32(K["g"]), e * f32(K["h"])
    ec, ed = e * f32(K["c"]), e * f32(K["d"])
    f = {}
    for first, second, pick in ((ea, eb, lambda c: mode(c)), (ep, er, lambda c: mode(*{0, 1, 2} - {c}))):
        vals = [m[c, pick(c)] for c in range(3)]
        shared = (vals[0] + vals[1] + vals[2]) * second
        for c in range(3):
            f[c, pick(c)] = vals[c] * first + shared
    for c, e2 in ((0, 1), (0, 2), (1, 2)):
        shared = (m[c, mode(e2)] + m[e2, mode(c)]) * eg
        f[c, mode(e2)] = shared
        f[e2, mode(c)] = shared
    for c in range(3):
        f[c, (1, 1, 1)] = m[c, (1, 1, 1)] * eh
    for e2 in range(3):
        c, o = [i for i in range(3) if i != e2]
        v1, v2 = m[c, mode(c, e2)], m[o, mode(o, e2)]
        f[c, mode(c, e2)] = v1 * ec + v2 * ed
        f[o, mode(o, e2)] = v2 * ec + v1 * ed
    return f


def energy_of(m):
    total = None
    for first, second, pick in (
        (K["a"] - K["b"], K["b"], lambda c: mode(c)),
        (K["p"] - K["r"], K["r"], lambda c: mode(*{0, 1, 2} - {c})),
    ):
        vals = [m[c, pick(c)] for c in range(3)]
        s = vals[0] + vals[1] + vals[2]
        part = (vals[0] * vals[0] + vals[1] * vals[1] + vals[2] * vals[2]) * f32(first) + s * s * f32(second)
        total = part if total is None else total + part
    shear = None
    for c, e2 in ((0, 1), (0, 2), (1, 2)):
        s = m[c, mode(e2)] + m[e2, mode(c)]
        shear = s * s if shear is None else shear + s * s
    total = total + shear * f32(K["g"])
    triple = None
    for c in range(3):
        v = m[c, (1, 1, 1)]
        triple = v * v if triple is None else triple + v * v
    total = total + triple * f32(K["h"])
    squares = cross = None
    for e2 in range(3):
        c, o = [i for i in range(3) if i != e2]
        v1, v2 = m[c, mode(c, e2)], m[o, mode(o, e2)]
        sq, cr = v1 * v1 + v2 * v2, v1 * v2
        squares = sq if squares is None else squares + sq
        cross = cr if cross is None else cross + cr
    return total + squares * f32(K["c"]) + cross * f32(2.0 * K["d"])


def x_parts(f0, f1, f2):
    out = {}
    for k in KS:
        v = f0 * f32(W[k])
        if k + 1 in W:
            v = v + f1 * f32(W[k + 1])
        if k + 4 in W:
            v = v + f2 * f32(W[k + 4])
        out[k] = v
    return out


def pack_z_kernel(load_hbm, design_hbm, load_ref, design_ref, out_ref, sems):
    copies = [pltpu.make_async_copy(load_hbm.at[c], load_ref.at[c], sems.at[c]) for c in range(3)]
    copies.append(pltpu.make_async_copy(design_hbm, design_ref, sems.at[3]))
    for one in copies:
        one.start()
    for one in copies:
        one.wait()
    lane = lane_of((NYL, 128))

    def step(pair, _):
        acc = jnp.zeros((NYL, 128), jnp.float32)
        for par in range(2):
            for fld in range(4):
                off = 64 * par + 16 * fld
                src = load_ref[fld, 2 * pair + par] if fld < 3 else design_ref[2 * pair + par]
                acc = jnp.where(((lane - off + 8) & 127) < 16, roll(src, off), acc)
        out_ref[pair] = acc
        return 0

    lax.fori_loop(0, 8, step, 0)


def halo_merge(high, low):
    lane = lane_of(high.shape)
    return jnp.where((lane & 15) < 8, high, low)


def pack_y_kernel(load_ref, design_ref, zhi_ref, zlo_ref, place_ref, lo_ref, hi_ref):
    del place_ref
    for dst, quad, one in ((lo_ref, 0, 4), (hi_ref, 12, 11)):
        rows = slice(quad, quad + 4)
        for x in range(16):
            dst[x, 0:4] = load_ref[0, x, rows]
            dst[x, 4:8] = load_ref[1, x, rows]
            dst[16 + x, 0:4] = load_ref[2, x, rows]
            dst[16 + x, 4:8] = design_ref[x, rows]
            dst[32 + x // 8, x % 8 : x % 8 + 1] = design_ref[x, one : one + 1]
        for k in range(8):
            dst[35 + k // 2, 4 * (k % 2) : 4 * (k % 2) + 4] = halo_merge(zhi_ref[k, rows], zlo_ref[k, rows])
            dst[34, k : k + 1] = halo_merge(zhi_ref[k, one : one + 1], zlo_ref[k, one : one + 1])


def pack_x_kernel(load_ref, design_ref, zhi_ref, zlo_ref, ylo_ref, yhi_ref, rx, rxt, dx, lo_ref, hi_ref, hx):
    none = jnp.zeros((8, 128), jnp.float32)
    for k in range(8):
        half = slice(4 * (k % 2), 4 * (k % 2) + 4)
        hx[k, 0:8] = none
        hx[k, 24:32] = none
        hx[k, 3:4] = ylo_ref[34, k : k + 1]
        hx[k, 4:8] = ylo_ref[35 + k // 2, half]
        hx[k, 8:24] = halo_merge(zhi_ref[k], zlo_ref[k])
        hx[k, 24:28] = yhi_ref[35 + k // 2, half]
        hx[k, 28:29] = yhi_ref[34, k : k + 1]
    for x in range(16):
        for c in range(3):
            tile, half = (x, slice(4 * c, 4 * c + 4)) if c < 2 else (16 + x, slice(0, 4))
            rx[c, x + 3, 0:4] = ylo_ref[tile, half]
            rx[c, x + 3, 4:20] = load_ref[c, x]
            rx[c, x + 3, 20:24] = yhi_ref[tile, half]
        one = slice(x % 8, x % 8 + 1)
        dx[x + 5, 0, 0:8] = none
        dx[x + 5, 0, 24:32] = none
        dx[x + 5, 0, 3:4] = ylo_ref[32 + x // 8, one]
        dx[x + 5, 0, 4:8] = ylo_ref[16 + x, 4:8]
        dx[x + 5, 0, 8:24] = design_ref[x]
        dx[x + 5, 0, 24:28] = yhi_ref[16 + x, 4:8]
        dx[x + 5, 0, 28:29] = yhi_ref[32 + x // 8, one]
    for i in range(5):
        lo_ref[288 + 32 * i : 320 + 32 * i] = dx[5 + i, 0]
        hi_ref[216 + 32 * i : 248 + 32 * i] = dx[16 + i, 0]
    for i in range(3):
        lo_ref[448 + 32 * i : 480 + 32 * i] = hx[i]
        hi_ref[376 + 32 * i : 408 + 32 * i] = hx[5 + i]
    for c in range(3):
        for i in range(4):
            lo_ref[24 * (4 * c + i) : 24 * (4 * c + i) + 24] = rx[c, 3 + i]
        for i in range(3):
            hi_ref[24 * (3 * c + i) : 24 * (3 * c + i) + 24] = rx[c, 16 + i]
    for k in range(8):
        spread_pair(hx[k], hx[k, 4:28], 2 * k, (2 * k, 2 * k + 1), rxt, dx, True)


def spread_pair(tile, window, x, wanted, rxt, dx, both):
    for par in range(2):
        if x + par in wanted:
            dx[x + par + 5, 1] = roll(tile, -(64 * par + 48))
            if both or -3 <= x + par <= 19:
                for c in range(3):
                    rxt[c, x + par + 3] = roll(window, -(64 * par + 16 * c))


def x_halos(xlo_ref, xhi_ref, rx, rxt, dx):
    for c in range(3):
        for i in range(4):
            rx[c, 19 + i] = xhi_ref[24 * (4 * c + i) : 24 * (4 * c + i) + 24]
        for i in range(3):
            rx[c, i] = xlo_ref[24 * (3 * c + i) : 24 * (3 * c + i) + 24]
    for i in range(5):
        dx[21 + i, 0] = xhi_ref[288 + 32 * i : 320 + 32 * i]
        dx[i, 0] = xlo_ref[216 + 32 * i : 248 + 32 * i]
    for i in range(3):
        at = 448 + 32 * i
        spread_pair(xhi_ref[at : at + 32], xhi_ref[at + 4 : at + 28], 16 + 2 * i, range(16, 21), rxt, dx, False)
        at = 376 + 32 * i
        spread_pair(xlo_ref[at : at + 32], xlo_ref[at + 4 : at + 28], -6 + 2 * i, range(-5, 0), rxt, dx, False)


def place_kernel(map_ref, order_ref, qk, fl, cl, *, sizes):
    del order_ref
    nx, ny, nz = sizes
    i_x, i_y, i_z = (lax.axis_index(a) for a in ALL)
    lane = lane_of((WIN, 128))
    row = lax.broadcasted_iota(jnp.int32, (WIN, 128), 0)
    y_at = i_y * NYL + row - 4
    z_at = [i_z * NZL + lane, i_z * NZL + jnp.where(lane < 64, lane + 128, lane - 128)]

    def inside(at, step, length):
        return jnp.where((at + step >= 0) & (at + step < length), 1.0, 0.0)

    y_in = [inside(y_at, 0, ny)] + [inside(y_at, s, ny) + inside(y_at, -s, ny) for s in (1, 2)]
    for t in range(2):
        z_in = [inside(z_at[t], 0, nz)] + [inside(z_at[t], s, nz) + inside(z_at[t], -s, nz) for s in (1, 2)]
        qk[0, t] = y_in[0] * z_in[0]
        qk[1, t] = y_in[1] * z_in[0] + y_in[0] * z_in[1]
        qk[2, t] = y_in[1] * z_in[1]
        qk[3, t] = y_in[2] * z_in[0] + y_in[0] * z_in[2]
        qk[4, t] = y_in[1] * z_in[2] + y_in[2] * z_in[1]
        qk[5, t] = y_in[2] * z_in[2]
        cl[t] = y_in[0] * z_in[0]
    gbx, gby, gbz = nx // BRICK, ny // BRICK, nz // BRICK
    bricks = NZL // BRICK

    def flag_at(bx, by, bz):
        ok = (bx >= 0) & (bx < gbx) & (by >= 0) & (by < gby) & (bz >= 0) & (bz < gbz)
        value = map_ref[jnp.clip(bx, 0, gbx - 1), jnp.clip(by, 0, gby - 1), jnp.clip(bz, 0, gbz - 1)]
        return jnp.where(ok, value, 0).astype(jnp.float32)

    for xc in range(3):
        lines = []
        for yc in range(3):
            flag = [flag_at(i_x + xc - 1, i_y + yc - 1, i_z * bricks + n - 1) for n in range(bricks + 2)]
            main = jnp.zeros((WIN, 128), jnp.float32)
            for n in range(bricks):
                main = jnp.where((lane >> 4) == n, flag[n + 1], main)
            lines.append((main, jnp.where(lane < 64, flag[bricks + 1], flag[0])))
        for t in range(2):
            fl[xc, t] = jnp.where(row < 4, lines[0][t], jnp.where(row < 20, lines[1][t], lines[2][t]))


def zy_plane(tile, zt, t_ref, slot, lane, tiles=2, base=0, blocks=3):
    for c in range(3):
        a0, a1 = tile(c, 0), tile(c, 1)
        n0, n1 = z_next(a0, a1, lane)
        zt[2 * c, 0, 0:24] = a0 + n0
        zt[2 * c + 1, 0, 0:24] = n0 - a0
        if tiles == 2:
            zt[2 * c, 1, 0:24] = a1 + n1
            zt[2 * c + 1, 1, 0:24] = n1 - a1
    for f in range(6):
        for t in range(tiles):
            for b in range(blocks):
                r = base + 8 * b
                lo, hi = zt[f, t, r : r + 8], zt[f, t, r + 1 : r + 9]
                t_ref[slot, 2 * f, t, 8 * b : 8 * b + 8] = lo + hi
                t_ref[slot, 2 * f + 1, t, 8 * b : 8 * b + 8] = hi - lo


def read_t(t_ref, slot, t, b):
    out = {}
    for c in range(3):
        for pz in range(2):
            for py in range(2):
                out[c, py, pz] = t_ref[slot, 4 * c + 2 * pz + py, t, 8 * b : 8 * b + 8]
    return out


LIFT = math.tanh(sharpness * threshold)
SCALE = LIFT + math.tanh(sharpness * (1.0 - threshold))


def cone_yz(av, t, rows):
    lo, hi = rows

    def at(n, step):
        return av[n, t, lo + step : hi + step]

    def both(n, step):
        return at(n, -step) + at(n, step)

    return [
        at(0, 0) + both(1, 1) + both(3, 2),
        at(1, 0) + both(2, 1) + both(4, 2),
        at(3, 0) + both(4, 1) + both(5, 2),
    ]


def density_plane(e, own, nx, dx, qk, fl, av, mo, gfs, dens_ref):
    lane = lane_of((WIN, 128))
    x_at = lax.axis_index("gx") * NXL + e - 3

    def scalar_inside(at, step):
        return jnp.where((at + step >= 0) & (at + step < nx), 1.0, 0.0)

    for t in range(2):
        f0 = dx[e + 2, t]
        f1 = dx[e + 1, t] + dx[e + 3, t]
        f2 = dx[e, t] + dx[e + 4, t]
        for n, part in enumerate(x_parts(f0, f1, f2).values()):
            av[n, t] = part
    x0 = scalar_inside(x_at, 0)
    x1 = scalar_inside(x_at, 1) + scalar_inside(x_at, -1)
    x2 = scalar_inside(x_at, 2) + scalar_inside(x_at, -2)
    cls = jnp.where(e < 3, 0, jnp.where(e < 19, 1, 2))
    b = [cone_yz(av, t, (4, 28)) for t in range(2)]
    n1, p1 = z_next(b[0][1], b[1][1], lane), z_prev(b[0][1], b[1][1], lane)
    n2, p2 = z_next(b[0][2], b[1][2], lane, 2), z_prev(b[0][2], b[1][2], lane, 2)
    weights = x_parts(x0, x1, x2)
    for t in range(2):
        cone = b[t][0] + (n1[t] + p1[t]) + (n2[t] + p2[t])
        ws = None
        for n, wk in enumerate(weights.values()):
            ws = qk[n, t] * wk if ws is None else ws + qk[n, t] * wk
        inv = 1.0 / jnp.maximum(ws, 1.0)
        th = jnp.tanh(sharpness * (cone * inv - threshold))
        dens = (LIFT + th) * f32(1.0 / SCALE)
        flag = fl[cls, t]
        sq = dens * dens
        mo[e, t] = (young_floor + sq * dens * (1.0 - young_floor)) * flag
        gfs[t][e] = sq * flag * (1.0 - th * th) * inv * f32(-3.0 * (1.0 - young_floor) * sharpness / SCALE)
        if t == 0:
            av[6, 0, 0:24] = dens
    dens_ref[own] = av[6, 0, 4:20]


def operate_planes(firsts, count, nx, rs, mo, cl, qs, zt, tt, gp, yp, yg):
    lane = lane_of((WIN, 128))
    i_x = lax.axis_index("gx")
    for n, first in enumerate(firsts):
        zy_plane(lambda c, t: rs[t][c, first], zt.at[n], tt.at[n], 0, lane)

    def transposes(n, first, i):
        e = first + jnp.maximum(i, 0)
        slot = i & 1
        x_on = jnp.where(i_x * NXL + e - 3 < nx, 1.0, 0.0)
        to = first + jnp.maximum(i - 1, 0)
        for c in range(3):
            p, g = [], []
            for t in range(2):
                zs = yp[n, slot, 2 * c, t] + yg[n, slot, 2 * c, t, 7:31]
                zd = yp[n, slot, 2 * c + 1, t] + yg[n, slot, 2 * c + 1, t, 7:31]
                p.append(zs - zd)
                g.append(zs + zd)
            gb = z_prev(g[0], g[1], lane)
            for t in range(2):
                value = p[t] + gb[t] + rs[t][c, e] * spring_rate
                qs[t][c, to] = value * (cl[t] * x_on)

    def forces(n, first, i):
        new, old = (i + 1) & 1, i & 1
        e = first + i
        zy_plane(lambda c, t: rs[t][c, e + 1], zt.at[n], tt.at[n], new, lane)
        for t in range(2):
            for b in range(3):
                rows = slice(8 * b, 8 * b + 8)
                force = forces_of(
                    modal_of(read_t(tt.at[n], old, t, b), read_t(tt.at[n], new, t, b)), mo[e, t, rows]
                )
                for c in range(3):
                    for pz in range(2):
                        m = []
                        for py in range(2):
                            fd = force[c, (1, py, pz)]
                            fs = force.get((c, (0, py, pz)))
                            at = 4 * c + 2 * pz + py
                            before = gp[n, at, t, rows]
                            if fs is None:
                                gp[n, at, t, rows] = fd
                                m.append(before - fd)
                            else:
                                gp[n, at, t, rows] = fs + fd
                                m.append((fs - fd) + before)
                        yp[n, old, 2 * c + pz, t, rows] = m[0] - m[1]
                        yg[n, old, 2 * c + pz, t, 8 + 8 * b : 16 + 8 * b] = m[0] + m[1]

    def step(i, _):
        for n, first in enumerate(firsts):
            transposes(n, first, i - 1)
            forces(n, first, i)
        return 0

    lax.fori_loop(0, count, step, 0)
    for n, first in enumerate(firsts):
        transposes(n, first, jnp.int32(count - 1))


def sum_planes(firsts, count, acc, rs, qs, mo, zt, tt):
    lane = lane_of((WIN, 128))

    def plane(n, x, slot):
        zy_plane(lambda c, t: qs[t][c, x + 2], zt.at[n], tt.at[n], slot, lane, tiles=1, base=4, blocks=2)

    for n, first in enumerate(firsts):
        plane(n, first, 0)

    def step(i, acc):
        s0, s1, s2, s3 = acc
        new, old = (i + 1) & 1, i & 1
        for n, first in enumerate(firsts):
            x = first + i
            plane(n, x + 1, new)
            for b in range(2):
                rows = slice(4 + 8 * b, 12 + 8 * b)
                for c in range(3):
                    r, q = rs[0][c, x + 3, rows], qs[0][c, x + 2, rows]
                    s0, s1, s2 = s0 + r * r, s1 + r * q, s2 + q * q
                m = modal_of(read_t(tt.at[n], old, 0, b), read_t(tt.at[n], new, 0, b))
                s3 = s3 + energy_of(m) * mo[x + 3, 0, rows]
        return s0, s1, s2, s3

    return lax.fori_loop(0, count, step, acc)


def inner_kernel(
    rx, rxt, dx, qk, fl, cl, mo, gf, gft, dens_ref, qx, qxt, acc_ref, av, zt, tt, gp, yp, yg, *, sizes
):
    nx = sizes[0]

    def density_step(i, _):
        for n in range(2):
            e = 5 + i + 6 * n
            density_plane(e, e - 3, nx, dx, qk, fl, av.at[n], mo, (gf, gft), dens_ref)
        return 0

    lax.fori_loop(0, 6, density_step, 0)
    operate_planes((5,), 12, nx, (rx, rxt), mo, cl, (qx, qxt), zt, tt, gp, yp, yg)
    zero = jnp.zeros((8, 128), jnp.float32)
    for n, part in enumerate(sum_planes((3, 8), 5, (zero,) * 4, (rx, rxt), (qx, qxt), mo, zt, tt)):
        acc_ref[n] = part


def outer_kernel(
    rx_in, rxt_in, dx_in, mo_in, gf_in, gft_in, dens_in, qx_in, qxt_in, acc_ref, xlo_ref, xhi_ref, qk, fl, cl,
    rx, rxt, dx, mo, gf, gft, dens_ref, qx, qxt, rp, qp, gpk, sum_ref, av, zt, tt, gp, yp, yg, *, sizes
):
    del rx_in, rxt_in, dx_in, mo_in, gf_in, gft_in, dens_in, qx_in, qxt_in
    nx = sizes[0]
    rs, qs, gfs = (rx, rxt), (qx, qxt), (gf, gft)
    x_halos(xlo_ref, xhi_ref, rx, rxt, dx)

    def density_step(i, _):
        density_plane(i, jnp.maximum(i - 3, 0), nx, dx, qk, fl, av.at[0], mo, gfs, dens_ref)
        density_plane(21 - i, jnp.minimum(18 - i, 15), nx, dx, qk, fl, av.at[1], mo, gfs, dens_ref)
        return 0

    lax.fori_loop(0, 5, density_step, 0)
    operate_planes((0, 16), 6, nx, rs, mo, cl, qs, zt, tt, gp, yp, yg)
    acc = tuple(acc_ref[n] for n in range(4))
    acc = sum_planes((0, 13), 3, acc, rs, qs, mo, zt, tt)
    line = jnp.zeros((8, 128), jnp.float32)
    lane = lane_of((8, 128))
    for n, part in enumerate(acc):
        total = jnp.sum(jnp.sum(part, axis=0, keepdims=True), axis=1, keepdims=True)
        line = jnp.where(lane == n, total, line)
    for n in range(sum_ref.shape[0] // 8):
        sum_ref[8 * n : 8 * n + 8] = line

    def pack_step(j, _):
        for c in range(3):
            rp[c, j] = pack_chunks([(rx[c, 4 * k + j + 1], rxt[c, 4 * k + j + 1]) for k in range(4)])
            qp[c, j] = pack_chunks([(qx[c, 4 * k + j], qxt[c, 4 * k + j]) for k in range(4)])
        return 0

    lax.fori_loop(0, 9, pack_step, 0, unroll=3)

    def pack_weights(j, _):
        gpk[j] = pack_chunks([(gf[4 * k + j + 1], gft[4 * k + j + 1]) for k in range(4)])
        return 0

    lax.fori_loop(0, 8, pack_weights, 0)


def pack_chunks(tiles):
    lane = lane_of((WIN, 128))
    out = None
    for k, (main, side) in enumerate(tiles):
        high = roll(side, 32 * k)
        low = roll(jnp.where(lane >= 64, side, main), 32 * k + 28)
        out = high if out is None else jnp.where(lane >= 32 * k, high, out)
        out = jnp.where(lane >= 32 * k + 16, low, out)
    return out


def cross_energy(m, o):
    total = None
    for first, second, pick in (
        (K["a"] - K["b"], K["b"], lambda c: mode(c)),
        (K["p"] - K["r"], K["r"], lambda c: mode(*{0, 1, 2} - {c})),
    ):
        vm, vo = [m[c, pick(c)] for c in range(3)], [o[c, pick(c)] for c in range(3)]
        sm, so = vm[0] + vm[1] + vm[2], vo[0] + vo[1] + vo[2]
        part = (vm[0] * vo[0] + vm[1] * vo[1] + vm[2] * vo[2]) * f32(first) + sm * so * f32(second)
        total = part if total is None else total + part
    shear = None
    for c, e2 in ((0, 1), (0, 2), (1, 2)):
        v = (m[c, mode(e2)] + m[e2, mode(c)]) * (o[c, mode(e2)] + o[e2, mode(c)])
        shear = v if shear is None else shear + v
    triple = None
    for c in range(3):
        v = m[c, (1, 1, 1)] * o[c, (1, 1, 1)]
        triple = v if triple is None else triple + v
    same = cross = None
    for e2 in range(3):
        c, d = [i for i in range(3) if i != e2]
        m1, m2 = m[c, mode(c, e2)], m[d, mode(d, e2)]
        o1, o2 = o[c, mode(c, e2)], o[d, mode(d, e2)]
        sq, cr = m1 * o1 + m2 * o2, m1 * o2 + m2 * o1
        same = sq if same is None else same + sq
        cross = cr if cross is None else cross + cr
    total = total + shear * f32(K["g"]) + triple * f32(K["h"])
    return total + same * f32(K["c"]) + cross * f32(K["d"])


def tail_kernel(rx, qx, gf, rp, qp, gpk, dens_in, out_ref, dens_ref, px, pp, zt, tr, tq, av, ap, bp):
    dens_ref[...] = dens_in[...]
    lane = lane_of((WIN, 128))
    edge = lane == 127

    def half_plane(at, after, t_ref, slot):
        for c in range(3):
            a = at(c)
            n = after(c, a)
            zt[2 * c, 0, 0:24] = a + n
            zt[2 * c + 1, 0, 0:24] = n - a
        for f in range(6):
            for b in range(3):
                lo, hi = zt[f, 0, 8 * b : 8 * b + 8], zt[f, 0, 8 * b + 1 : 8 * b + 9]
                t_ref[slot, 2 * f, 0, 8 * b : 8 * b + 8] = lo + hi
                t_ref[slot, 2 * f + 1, 0, 8 * b : 8 * b + 8] = hi - lo

    def main_plane(i, slot):
        chunk = jnp.minimum(i >> 2, 3)
        j, shift = i - 4 * chunk, 127 - 32 * chunk

        def after(src):
            return lambda c, a: jnp.where(edge, pltpu.roll(src[c, j], shift, 1), roll(a, -1))

        half_plane(lambda c: rx[c, i + 1], after(rp), tr, slot)
        half_plane(lambda c: qx[c, i], after(qp), tq, slot)

    def end_plane(j, slot):
        half_plane(lambda c: rp[c, j], lambda c, a: roll(a, -1), tr, slot)
        half_plane(lambda c: qp[c, j], lambda c, a: roll(a, -1), tq, slot)

    def energies(i, g_ref, out):
        new, old = (i + 1) & 1, i & 1
        for b in range(3):
            rows = slice(8 * b, 8 * b + 8)
            m = modal_of(read_t(tr, old, 0, b), read_t(tr, new, 0, b))
            o = modal_of(read_t(tq, old, 0, b), read_t(tq, new, 0, b))
            g = g_ref[rows]
            out[0, i, rows] = energy_of(m) * g
            out[1, i, rows] = cross_energy(m, o) * (2.0 * g)
            out[2, i, rows] = energy_of(o) * g

    def main_step(i, _):
        main_plane(i + 1, (i + 1) & 1)
        energies(i, gf.at[i + 1], px)
        return 0

    def end_step(j, _):
        end_plane(j + 1, (j + 1) & 1)
        energies(j, gpk.at[j], pp)
        return 0

    main_plane(jnp.int32(0), 0)
    lax.fori_loop(0, 20, main_step, 0, unroll=2)
    end_plane(0, 0)
    lax.fori_loop(0, 8, end_step, 0)

    def parts_of(src, k, x, dst):
        f0 = src[k, x + 2]
        f1 = src[k, x + 1] + src[k, x + 3]
        f2 = src[k, x] + src[k, x + 4]
        for n, part in enumerate(x_parts(f0, f1, f2).values()):
            dst[k, n, 0, 0:24] = part

    def end_cone(j, _):
        for k in range(3):
            parts_of(pp, k, j, ap)
            b = cone_yz(ap.at[k], 0, (4, 20))
            bp[k, j, 0] = b[1]
            bp[k, j, 1] = b[2]
        return 0

    lax.fori_loop(0, 4, end_cone, 0)
    lane16 = lane_of((NYL, 128))
    for chunk in range(4):

        def cone_step(j, _):
            x = 4 * chunk + j
            for k in range(3):
                parts_of(px, k, x, av)
                b0, b1, b2 = cone_yz(av.at[k], 0, (4, 20))
                e1, e2 = bp[k, j, 0], bp[k, j, 1]
                n1 = jnp.where(lane16 == 127, roll(e1, 127 - 32 * chunk), roll(b1, -1))
                p1 = jnp.where(lane16 == 0, roll(e1, -(32 * chunk + 27)), roll(b1, 1))
                n2 = jnp.where(lane16 >= 126, roll(e2, 126 - 32 * chunk), roll(b2, -2))
                p2 = jnp.where(lane16 < 2, roll(e2, -(32 * chunk + 26)), roll(b2, 2))
                out_ref[k, x] = b0 + (n1 + p1) + (n2 + p2)
            return 0

        lax.fori_loop(0, 4, cone_step, 0)


def final_kernel(sum_ref, rx, qx, cones, disp_ref, sens_ref):
    line = jnp.sum(sum_ref[...], axis=0, keepdims=True)
    lane1 = lane_of((1, 128))
    m0, m1, m2, m3 = [jnp.sum(jnp.where(lane1 == n, line, 0.0), axis=1, keepdims=True) for n in range(4)]
    m3 = m3 + spring_rate * m2
    first = m0 / m1
    norm = m0 - 2.0 * first * m1 + first * first * m2
    grown = 1.0 + norm / m0
    second = norm / (grown * grown * m1 - 2.0 * first * grown * m2 + first * first * m3)
    c0 = jnp.broadcast_to(first + second * grown, (NYL, 128))
    c1 = jnp.broadcast_to(-second * first, (NYL, 128))

    def step(x, _):
        for c in range(3):
            disp_ref[c, x] = c0 * rx[c, x + 3, 4:20] + c1 * qx[c, x + 2, 4:20]
        sens_ref[x] = c0 * (c0 * cones[0, x] + c1 * cones[1, x]) + c1 * c1 * cones[2, x]
        return 0

    lax.fori_loop(0, 16, step, 0)


def s(*shape):
    return jax.ShapeDtypeStruct(shape, jnp.float32)


def v(*shape):
    return pltpu.VMEM(shape, jnp.float32)


def call(kernel, outs, scratch, *args, smem=0, hbm=0, flush=(), **kw):
    spec_s, spec_v = pl.BlockSpec(memory_space=pltpu.SMEM), pl.BlockSpec(memory_space=pltpu.VMEM)
    single = not isinstance(outs, (tuple, list))
    outs = [outs] if single else list(outs)
    if not INTERPRET:
        outs = [o if i in flush else pltpu.VMEM(o.shape, o.dtype) for i, o in enumerate(outs)]
        args = [
            a if i < smem else pltpu.with_memory_space_constraint(a, pltpu.HBM if i < smem + hbm else pltpu.VMEM)
            for i, a in enumerate(args)
        ]
    return pl.pallas_call(
        kernel,
        out_shape=outs[0] if single else outs,
        in_specs=[spec_s] * smem
        + [pl.BlockSpec(memory_space=pltpu.HBM)] * hbm
        + [spec_v] * (len(args) - smem - hbm),
        out_specs=spec_v if single else [spec_v] * len(outs),
        scratch_shapes=scratch,
        interpret=INTERPRET,
        compiler_params=pltpu.CompilerParams(vmem_limit_bytes=24 << 20),
        **kw,
    )(*args)


def moved(block, axis, step):
    count = lax.axis_size(axis)
    return lax.ppermute(block, axis, [(i, i - step) for i in range(count) if 0 <= i - step < count])


def body(load, design, solid_map):
    sizes = tuple(lax.axis_size(a) * n for a, n in zip(ALL, (NXL, NYL, NZL)))
    count = lax.axis_size("gx") * lax.axis_size("gy") * lax.axis_size("gz")

    def sized(kernel):
        return lambda *refs: kernel(*refs, sizes=sizes)

    load, design, zc = call(
        pack_z_kernel, (s(3, 16, 16, 128), s(16, 16, 128), s(8, 16, 128)), [pltpu.SemaphoreType.DMA((4,))],
        load, design, hbm=2,
    )
    zhi, zlo = moved(zc, "gz", 1), moved(zc, "gz", -1)
    qk, fl, cl = call(
        sized(place_kernel), (s(6, 2, 24, 128), s(3, 2, 24, 128), s(2, 24, 128)), [], solid_map, zc, smem=1
    )
    ylo_s, yhi_s = call(pack_y_kernel, (s(39, 8, 128), s(39, 8, 128)), [], load, design, zhi, zlo, cl)
    yhi, ylo = moved(ylo_s, "gy", 1), moved(yhi_s, "gy", -1)
    rx_t, dx_t, mo_t, gf_t = s(3, 23, 24, 128), s(26, 2, 32, 128), s(22, 2, 24, 128), s(22, 24, 128)
    dens_t, qx_t = s(16, 16, 128), s(3, 21, 24, 128)
    rx, rxt, dx, xlo_s, xhi_s = call(
        pack_x_kernel, (rx_t, rx_t, dx_t, s(544, 128), s(472, 128)), [v(8, 32, 128)],
        load, design, zhi, zlo, ylo, yhi,
    )
    xhi, xlo = moved(xlo_s, "gx", 1), moved(xhi_s, "gx", -1)
    scratch = [
        v(2, 7, 2, 32, 128), v(2, 6, 2, 32, 128), v(2, 2, 12, 2, 24, 128), v(2, 12, 2, 24, 128),
        v(2, 2, 6, 2, 24, 128), v(2, 2, 6, 2, 32, 128),
    ]
    mo, gf, gft, dens, qx, qxt, acc = call(
        sized(inner_kernel), (mo_t, gf_t, gf_t, dens_t, qx_t, qx_t, s(4, 8, 128)), scratch, rx, rxt, dx, qk, fl, cl
    )
    held = rx_t, rx_t, dx_t, mo_t, gf_t, gf_t, dens_t, qx_t, qx_t
    rx, _, _, _, gf, _, dens, qx, _, rp, qp, gpk, part = call(
        sized(outer_kernel),
        (*held, s(3, 9, 24, 128), s(3, 9, 24, 128), s(8, 24, 128), s(count, 128)), scratch,
        rx, rxt, dx, mo, gf, gft, dens, qx, qxt, acc, xlo, xhi, qk, fl, cl,
        flush=(12,), input_output_aliases={n: n for n in range(len(held))},
    )
    sums = lax.all_to_all(part, ALL, 0, 0, tiled=True)
    cones, dens = call(
        tail_kernel, (s(3, 16, 16, 128), dens_t),
        [
            v(3, 20, 24, 128), v(3, 8, 24, 128), v(6, 2, 32, 128), v(2, 12, 1, 24, 128), v(2, 12, 1, 24, 128),
            v(3, 6, 1, 32, 128), v(3, 6, 1, 32, 128), v(3, 4, 2, 16, 128),
        ],
        rx, qx, gf, rp, qp, gpk, dens, flush=(1,),
    )
    disp, sens = call(
        final_kernel, (s(3, 16, 16, 128), s(16, 16, 128)), [], sums, rx, qx, cones, flush=(0, 1)
    )
    return disp, sens, dens


def solution(mesh):
    nodal, cell = P(None, "gx", "gy", "gz"), P("gx", "gy", "gz")
    return jax.shard_map(
        body, mesh=mesh, in_specs=(nodal, cell, P()), out_specs=(nodal, cell, cell), check_vma=False
    )
```

```python
import math

import jax
import jax.numpy as jnp
import numpy as np
from jax import lax
from jax.experimental import pallas as pl
from jax.experimental.pallas import tpu as pltpu
from jax.sharding import PartitionSpec as P


BRICK = 16
young_floor = 0.001
spring_rate = 0.05
sharpness = 8.0
threshold = 0.5
poisson = 0.3
ALL = ("gx", "gy", "gz")
INTERPRET = False

NXL, NYL, NZL = 16, 16, 128
WIN = 24


def element_matrix():
    lame_first = poisson / ((1.0 + poisson) * (1.0 - 2.0 * poisson))
    shear_mod = 1.0 / (2.0 * (1.0 + poisson))
    elastic = np.zeros((6, 6))
    elastic[:3, :3] = lame_first
    for axis_one in range(3):
        elastic[axis_one, axis_one] += 2.0 * shear_mod
        elastic[axis_one + 3, axis_one + 3] = shear_mod
    gauss_point = 1.0 / math.sqrt(3.0)
    stiffness = np.zeros((24, 24))
    for point_x in (-gauss_point, gauss_point):
        for point_y in (-gauss_point, gauss_point):
            for point_z in (-gauss_point, gauss_point):
                strain = np.zeros((6, 24))
                for corner in range(8):
                    sign_a = 2 * (corner // 4) - 1
                    sign_b = 2 * (corner // 2 % 2) - 1
                    sign_c = 2 * (corner % 2) - 1
                    along_x = 0.25 * sign_a * (1 + sign_b * point_y) * (1 + sign_c * point_z)
                    along_y = 0.25 * (1 + sign_a * point_x) * sign_b * (1 + sign_c * point_z)
                    along_z = 0.25 * (1 + sign_a * point_x) * (1 + sign_b * point_y) * sign_c
                    column = 3 * corner
                    strain[0, column] = along_x
                    strain[1, column + 1] = along_y
                    strain[2, column + 2] = along_z
                    strain[3, column + 1] = along_z
                    strain[3, column + 2] = along_y
                    strain[4, column] = along_z
                    strain[4, column + 2] = along_x
                    strain[5, column] = along_y
                    strain[5, column + 1] = along_x
                stiffness += strain.T @ elastic @ strain * 0.125
    return stiffness


def modal_constants():
    modes = [(px, py, pz) for px in (0, 1) for py in (0, 1) for pz in (0, 1)]
    change = np.zeros((24, 24))
    for c in range(3):
        for m, mode in enumerate(modes):
            for q in range(8):
                corner = (q // 4, q // 2 % 2, q % 2)
                sign = 1.0
                for axis in range(3):
                    if mode[axis] and not corner[axis]:
                        sign = -sign
                change[8 * c + m, 3 * q + c] = sign
    hat = change @ element_matrix() @ change.T / 64.0

    def at(c1, m1, c2, m2):
        return hat[8 * c1 + modes.index(m1), 8 * c2 + modes.index(m2)]

    k = {
        "a": at(0, (1, 0, 0), 0, (1, 0, 0)),
        "b": at(0, (1, 0, 0), 1, (0, 1, 0)),
        "p": at(0, (0, 1, 1), 0, (0, 1, 1)),
        "r": at(0, (0, 1, 1), 1, (1, 0, 1)),
        "g": at(0, (0, 1, 0), 1, (1, 0, 0)),
        "h": at(2, (1, 1, 1), 2, (1, 1, 1)),
        "c": at(1, (1, 1, 0), 1, (1, 1, 0)),
        "d": at(1, (1, 1, 0), 2, (1, 0, 1)),
    }
    made = np.zeros((24, 24))

    def put(c1, m1, c2, m2, v):
        made[8 * c1 + modes.index(m1), 8 * c2 + modes.index(m2)] += v

    for c in range(3):
        unit = tuple(int(i == c) for i in range(3))
        anti = tuple(int(i != c) for i in range(3))
        put(c, (1, 1, 1), c, (1, 1, 1), k["h"])
        for e in range(3):
            unit_e = tuple(int(i == e) for i in range(3))
            anti_e = tuple(int(i != e) for i in range(3))
            put(c, unit, e, unit_e, k["a"] if c == e else k["b"])
            put(c, anti, e, anti_e, k["p"] if c == e else k["r"])
            if c != e:
                put(c, unit_e, c, unit_e, k["g"])
                put(c, unit_e, e, unit, k["g"])
                both = tuple(int(i in (c, e)) for i in range(3))
                o = 3 - c - e
                both_o = tuple(int(i in (o, e)) for i in range(3))
                put(c, both, c, both, k["c"])
                put(c, both, o, both_o, k["d"])
    assert np.abs(made - hat).max() < 1e-12
    return k


K = modal_constants()
W = {n: 3.0 - math.sqrt(n) for n in range(9)}
KS = (0, 1, 2, 4, 5, 8)


def mode(*axes):
    return tuple(int(i in axes) for i in range(3))


def f32(x):
    return float(np.float32(x))


def roll(x, shift):
    shift = shift % 128
    return x if shift == 0 else pltpu.roll(x, shift, 1)


def lane_of(shape):
    return lax.broadcasted_iota(jnp.int32, shape, 1)


def z_next(a0, a1, lane, by=1):
    r0, r1 = roll(a0, -by), roll(a1, -by)
    edge = lane >= 128 - by
    return jnp.where(edge, r1, r0), jnp.where(edge, r0, r1)


def z_prev(a0, a1, lane, by=1):
    r0, r1 = roll(a0, by), roll(a1, by)
    edge = lane < by
    return jnp.where(edge, r1, r0), jnp.where(edge, r0, r1)


def modal_of(lo, hi):
    m = {}
    for (c, py, pz), low in lo.items():
        high = hi[c, py, pz]
        if py or pz:
            m[c, (0, py, pz)] = low + high
        m[c, (1, py, pz)] = high - low
    return m


def forces_of(m, e):
    ea, eb = e * f32(K["a"] - K["b"]), e * f32(K["b"])
    ep, er = e * f32(K["p"] - K["r"]), e * f32(K["r"])
    eg, eh = e * f32(K["g"]), e * f32(K["h"])
    ec, ed = e * f32(K["c"]), e * f32(K["d"])
    f = {}
    for first, second, pick in ((ea, eb, lambda c: mode(c)), (ep, er, lambda c: mode(*{0, 1, 2} - {c}))):
        vals = [m[c, pick(c)] for c in range(3)]
        shared = (vals[0] + vals[1] + vals[2]) * second
        for c in range(3):
            f[c, pick(c)] = vals[c] * first + shared
    for c, e2 in ((0, 1), (0, 2), (1, 2)):
        shared = (m[c, mode(e2)] + m[e2, mode(c)]) * eg
        f[c, mode(e2)] = shared
        f[e2, mode(c)] = shared
    for c in range(3):
        f[c, (1, 1, 1)] = m[c, (1, 1, 1)] * eh
    for e2 in range(3):
        c, o = [i for i in range(3) if i != e2]
        v1, v2 = m[c, mode(c, e2)], m[o, mode(o, e2)]
        f[c, mode(c, e2)] = v1 * ec + v2 * ed
        f[o, mode(o, e2)] = v2 * ec + v1 * ed
    return f


def energy_of(m):
    total = None
    for first, second, pick in (
        (K["a"] - K["b"], K["b"], lambda c: mode(c)),
        (K["p"] - K["r"], K["r"], lambda c: mode(*{0, 1, 2} - {c})),
    ):
        vals = [m[c, pick(c)] for c in range(3)]
        s = vals[0] + vals[1] + vals[2]
        part = (vals[0] * vals[0] + vals[1] * vals[1] + vals[2] * vals[2]) * f32(first) + s * s * f32(second)
        total = part if total is None else total + part
    shear = None
    for c, e2 in ((0, 1), (0, 2), (1, 2)):
        s = m[c, mode(e2)] + m[e2, mode(c)]
        shear = s * s if shear is None else shear + s * s
    total = total + shear * f32(K["g"])
    triple = None
    for c in range(3):
        v = m[c, (1, 1, 1)]
        triple = v * v if triple is None else triple + v * v
    total = total + triple * f32(K["h"])
    squares = cross = None
    for e2 in range(3):
        c, o = [i for i in range(3) if i != e2]
        v1, v2 = m[c, mode(c, e2)], m[o, mode(o, e2)]
        sq, cr = v1 * v1 + v2 * v2, v1 * v2
        squares = sq if squares is None else squares + sq
        cross = cr if cross is None else cross + cr
    return total + squares * f32(K["c"]) + cross * f32(2.0 * K["d"])


def x_parts(f0, f1, f2):
    out = {}
    for k in KS:
        v = f0 * f32(W[k])
        if k + 1 in W:
            v = v + f1 * f32(W[k + 1])
        if k + 4 in W:
            v = v + f2 * f32(W[k + 4])
        out[k] = v
    return out


def pack_z_kernel(load_hbm, design_hbm, load_ref, design_ref, out_ref, sems):
    copies = [pltpu.make_async_copy(load_hbm.at[c], load_ref.at[c], sems.at[c]) for c in range(3)]
    copies.append(pltpu.make_async_copy(design_hbm, design_ref, sems.at[3]))
    for one in copies:
        one.start()
    for one in copies:
        one.wait()
    lane = lane_of((NYL, 128))

    def step(pair, _):
        acc = jnp.zeros((NYL, 128), jnp.float32)
        for par in range(2):
            for fld in range(4):
                off = 64 * par + 16 * fld
                src = load_ref[fld, 2 * pair + par] if fld < 3 else design_ref[2 * pair + par]
                acc = jnp.where(((lane - off + 8) & 127) < 16, roll(src, off), acc)
        out_ref[pair] = acc
        return 0

    lax.fori_loop(0, 8, step, 0, unroll=2)


def halo_merge(high, low):
    lane = lane_of(high.shape)
    return jnp.where((lane & 15) < 8, high, low)


def pack_y_kernel(load_ref, design_ref, zhi_ref, zlo_ref, place_ref, lo_ref, hi_ref):
    del place_ref
    for dst, quad, one in ((lo_ref, 0, 4), (hi_ref, 12, 11)):
        rows = slice(quad, quad + 4)
        for x in range(16):
            dst[x, 0:4] = load_ref[0, x, rows]
            dst[x, 4:8] = load_ref[1, x, rows]
            dst[16 + x, 0:4] = load_ref[2, x, rows]
            dst[16 + x, 4:8] = design_ref[x, rows]
            dst[32 + x // 8, x % 8 : x % 8 + 1] = design_ref[x, one : one + 1]
        for k in range(8):
            dst[35 + k // 2, 4 * (k % 2) : 4 * (k % 2) + 4] = halo_merge(zhi_ref[k, rows], zlo_ref[k, rows])
            dst[34, k : k + 1] = halo_merge(zhi_ref[k, one : one + 1], zlo_ref[k, one : one + 1])


def pack_x_kernel(load_ref, design_ref, zhi_ref, zlo_ref, ylo_ref, yhi_ref, rx, rxt, dx, lo_ref, hi_ref, hx):
    none = jnp.zeros((8, 128), jnp.float32)
    for k in range(8):
        half = slice(4 * (k % 2), 4 * (k % 2) + 4)
        hx[k, 0:8] = none
        hx[k, 24:32] = none
        hx[k, 3:4] = ylo_ref[34, k : k + 1]
        hx[k, 4:8] = ylo_ref[35 + k // 2, half]
        hx[k, 8:24] = halo_merge(zhi_ref[k], zlo_ref[k])
        hx[k, 24:28] = yhi_ref[35 + k // 2, half]
        hx[k, 28:29] = yhi_ref[34, k : k + 1]
    for x in range(16):
        for c in range(3):
            tile, half = (x, slice(4 * c, 4 * c + 4)) if c < 2 else (16 + x, slice(0, 4))
            rx[c, x + 3, 0:4] = ylo_ref[tile, half]
            rx[c, x + 3, 4:20] = load_ref[c, x]
            rx[c, x + 3, 20:24] = yhi_ref[tile, half]
        one = slice(x % 8, x % 8 + 1)
        dx[x + 5, 0, 0:8] = none
        dx[x + 5, 0, 24:32] = none
        dx[x + 5, 0, 3:4] = ylo_ref[32 + x // 8, one]
        dx[x + 5, 0, 4:8] = ylo_ref[16 + x, 4:8]
        dx[x + 5, 0, 8:24] = design_ref[x]
        dx[x + 5, 0, 24:28] = yhi_ref[16 + x, 4:8]
        dx[x + 5, 0, 28:29] = yhi_ref[32 + x // 8, one]
    for i in range(5):
        lo_ref[288 + 32 * i : 320 + 32 * i] = dx[5 + i, 0]
        hi_ref[216 + 32 * i : 248 + 32 * i] = dx[16 + i, 0]
    for i in range(3):
        lo_ref[448 + 32 * i : 480 + 32 * i] = hx[i]
        hi_ref[376 + 32 * i : 408 + 32 * i] = hx[5 + i]
    for c in range(3):
        for i in range(4):
            lo_ref[24 * (4 * c + i) : 24 * (4 * c + i) + 24] = rx[c, 3 + i]
        for i in range(3):
            hi_ref[24 * (3 * c + i) : 24 * (3 * c + i) + 24] = rx[c, 16 + i]
    for k in range(8):
        spread_pair(hx[k], hx[k, 4:28], 2 * k, (2 * k, 2 * k + 1), rxt, dx, True)


def spread_pair(tile, window, x, wanted, rxt, dx, both):
    for par in range(2):
        if x + par in wanted:
            dx[x + par + 5, 1] = roll(tile, -(64 * par + 48))
            if both or -3 <= x + par <= 19:
                for c in range(3):
                    rxt[c, x + par + 3] = roll(window, -(64 * par + 16 * c))


def x_halos(xlo_ref, xhi_ref, rx, rxt, dx):
    for c in range(3):
        for i in range(4):
            rx[c, 19 + i] = xhi_ref[24 * (4 * c + i) : 24 * (4 * c + i) + 24]
        for i in range(3):
            rx[c, i] = xlo_ref[24 * (3 * c + i) : 24 * (3 * c + i) + 24]
    for i in range(5):
        dx[21 + i, 0] = xhi_ref[288 + 32 * i : 320 + 32 * i]
        dx[i, 0] = xlo_ref[216 + 32 * i : 248 + 32 * i]
    for i in range(3):
        at = 448 + 32 * i
        spread_pair(xhi_ref[at : at + 32], xhi_ref[at + 4 : at + 28], 16 + 2 * i, range(16, 21), rxt, dx, False)
        at = 376 + 32 * i
        spread_pair(xlo_ref[at : at + 32], xlo_ref[at + 4 : at + 28], -6 + 2 * i, range(-5, 0), rxt, dx, False)


def place_kernel(map_ref, order_ref, qk, fl, cl, *, sizes):
    del order_ref
    nx, ny, nz = sizes
    i_x, i_y, i_z = (lax.axis_index(a) for a in ALL)
    lane = lane_of((WIN, 128))
    row = lax.broadcasted_iota(jnp.int32, (WIN, 128), 0)
    y_at = i_y * NYL + row - 4
    z_at = [i_z * NZL + lane, i_z * NZL + jnp.where(lane < 64, lane + 128, lane - 128)]

    def inside(at, step, length):
        return jnp.where((at + step >= 0) & (at + step < length), 1.0, 0.0)

    y_in = [inside(y_at, 0, ny)] + [inside(y_at, s, ny) + inside(y_at, -s, ny) for s in (1, 2)]
    for t in range(2):
        z_in = [inside(z_at[t], 0, nz)] + [inside(z_at[t], s, nz) + inside(z_at[t], -s, nz) for s in (1, 2)]
        qk[0, t] = y_in[0] * z_in[0]
        qk[1, t] = y_in[1] * z_in[0] + y_in[0] * z_in[1]
        qk[2, t] = y_in[1] * z_in[1]
        qk[3, t] = y_in[2] * z_in[0] + y_in[0] * z_in[2]
        qk[4, t] = y_in[1] * z_in[2] + y_in[2] * z_in[1]
        qk[5, t] = y_in[2] * z_in[2]
        cl[t] = y_in[0] * z_in[0]
    gbx, gby, gbz = nx // BRICK, ny // BRICK, nz // BRICK
    bricks = NZL // BRICK

    def flag_at(bx, by, bz):
        ok = (bx >= 0) & (bx < gbx) & (by >= 0) & (by < gby) & (bz >= 0) & (bz < gbz)
        value = map_ref[jnp.clip(bx, 0, gbx - 1), jnp.clip(by, 0, gby - 1), jnp.clip(bz, 0, gbz - 1)]
        return jnp.where(ok, value, 0).astype(jnp.float32)

    for xc in range(3):
        lines = []
        for yc in range(3):
            flag = [flag_at(i_x + xc - 1, i_y + yc - 1, i_z * bricks + n - 1) for n in range(bricks + 2)]
            main = jnp.zeros((WIN, 128), jnp.float32)
            for n in range(bricks):
                main = jnp.where((lane >> 4) == n, flag[n + 1], main)
            lines.append((main, jnp.where(lane < 64, flag[bricks + 1], flag[0])))
        for t in range(2):
            fl[xc, t] = jnp.where(row < 4, lines[0][t], jnp.where(row < 20, lines[1][t], lines[2][t]))


def zy_plane(tile, zt, t_ref, slot, lane, tiles=2, base=0, blocks=3):
    for c in range(3):
        a0, a1 = tile(c, 0), tile(c, 1)
        n0, n1 = z_next(a0, a1, lane)
        zt[2 * c, 0, 0:24] = a0 + n0
        zt[2 * c + 1, 0, 0:24] = n0 - a0
        if tiles == 2:
            zt[2 * c, 1, 0:24] = a1 + n1
            zt[2 * c + 1, 1, 0:24] = n1 - a1
    for f in range(6):
        for t in range(tiles):
            for b in range(blocks):
                r = base + 8 * b
                lo, hi = zt[f, t, r : r + 8], zt[f, t, r + 1 : r + 9]
                t_ref[slot, 2 * f, t, 8 * b : 8 * b + 8] = lo + hi
                t_ref[slot, 2 * f + 1, t, 8 * b : 8 * b + 8] = hi - lo


def read_t(t_ref, slot, t, b):
    out = {}
    for c in range(3):
        for pz in range(2):
            for py in range(2):
                out[c, py, pz] = t_ref[slot, 4 * c + 2 * pz + py, t, 8 * b : 8 * b + 8]
    return out


LIFT = math.tanh(sharpness * threshold)
SCALE = LIFT + math.tanh(sharpness * (1.0 - threshold))


def cone_yz(av, t, rows):
    lo, hi = rows

    def at(n, step):
        return av[n, t, lo + step : hi + step]

    def both(n, step):
        return at(n, -step) + at(n, step)

    return [
        at(0, 0) + both(1, 1) + both(3, 2),
        at(1, 0) + both(2, 1) + both(4, 2),
        at(3, 0) + both(4, 1) + both(5, 2),
    ]


def density_plane(e, own, nx, dx, qk, fl, av, mo, gfs, dens_ref):
    lane = lane_of((WIN, 128))
    x_at = lax.axis_index("gx") * NXL + e - 3

    def scalar_inside(at, step):
        return jnp.where((at + step >= 0) & (at + step < nx), 1.0, 0.0)

    for t in range(2):
        f0 = dx[e + 2, t]
        f1 = dx[e + 1, t] + dx[e + 3, t]
        f2 = dx[e, t] + dx[e + 4, t]
        for n, part in enumerate(x_parts(f0, f1, f2).values()):
            av[n, t] = part
    x0 = scalar_inside(x_at, 0)
    x1 = scalar_inside(x_at, 1) + scalar_inside(x_at, -1)
    x2 = scalar_inside(x_at, 2) + scalar_inside(x_at, -2)
    cls = jnp.where(e < 3, 0, jnp.where(e < 19, 1, 2))
    b = [cone_yz(av, t, (4, 28)) for t in range(2)]
    n1, p1 = z_next(b[0][1], b[1][1], lane), z_prev(b[0][1], b[1][1], lane)
    n2, p2 = z_next(b[0][2], b[1][2], lane, 2), z_prev(b[0][2], b[1][2], lane, 2)
    weights = x_parts(x0, x1, x2)
    for t in range(2):
        cone = b[t][0] + (n1[t] + p1[t]) + (n2[t] + p2[t])
        ws = None
        for n, wk in enumerate(weights.values()):
            ws = qk[n, t] * wk if ws is None else ws + qk[n, t] * wk
        inv = 1.0 / jnp.maximum(ws, 1.0)
        th = jnp.tanh(sharpness * (cone * inv - threshold))
        dens = (LIFT + th) * f32(1.0 / SCALE)
        flag = fl[cls, t]
        sq = dens * dens
        mo[e, t] = (young_floor + sq * dens * (1.0 - young_floor)) * flag
        gfs[t][e] = sq * flag * (1.0 - th * th) * inv * f32(-3.0 * (1.0 - young_floor) * sharpness / SCALE)
        if t == 0:
            av[6, 0, 0:24] = dens
    dens_ref[own] = av[6, 0, 4:20]


def operate_planes(firsts, count, nx, rs, mo, cl, qs, zt, tt, gp, yp, yg):
    lane = lane_of((WIN, 128))
    i_x = lax.axis_index("gx")
    for n, first in enumerate(firsts):
        zy_plane(lambda c, t: rs[t][c, first], zt.at[n], tt.at[n], 0, lane)

    def transposes(n, first, i):
        e = first + jnp.maximum(i, 0)
        slot = i & 1
        x_on = jnp.where(i_x * NXL + e - 3 < nx, 1.0, 0.0)
        to = first + jnp.maximum(i - 1, 0)
        for c in range(3):
            p, g = [], []
            for t in range(2):
                zs = yp[n, slot, 2 * c, t] + yg[n, slot, 2 * c, t, 7:31]
                zd = yp[n, slot, 2 * c + 1, t] + yg[n, slot, 2 * c + 1, t, 7:31]
                p.append(zs - zd)
                g.append(zs + zd)
            gb = z_prev(g[0], g[1], lane)
            for t in range(2):
                value = p[t] + gb[t] + rs[t][c, e] * spring_rate
                qs[t][c, to] = value * (cl[t] * x_on)

    def forces(n, first, i):
        new, old = (i + 1) & 1, i & 1
        e = first + i
        zy_plane(lambda c, t: rs[t][c, e + 1], zt.at[n], tt.at[n], new, lane)
        for t in range(2):
            for b in range(3):
                rows = slice(8 * b, 8 * b + 8)
                force = forces_of(
                    modal_of(read_t(tt.at[n], old, t, b), read_t(tt.at[n], new, t, b)), mo[e, t, rows]
                )
                for c in range(3):
                    for pz in range(2):
                        m = []
                        for py in range(2):
                            fd = force[c, (1, py, pz)]
                            fs = force.get((c, (0, py, pz)))
                            at = 4 * c + 2 * pz + py
                            before = gp[n, at, t, rows]
                            if fs is None:
                                gp[n, at, t, rows] = fd
                                m.append(before - fd)
                            else:
                                gp[n, at, t, rows] = fs + fd
                                m.append((fs - fd) + before)
                        yp[n, old, 2 * c + pz, t, rows] = m[0] - m[1]
                        yg[n, old, 2 * c + pz, t, 8 + 8 * b : 16 + 8 * b] = m[0] + m[1]

    def step(i, _):
        for n, first in enumerate(firsts):
            transposes(n, first, i - 1)
            forces(n, first, i)
        return 0

    lax.fori_loop(0, count, step, 0)
    for n, first in enumerate(firsts):
        transposes(n, first, jnp.int32(count - 1))


def sum_planes(firsts, count, acc, rs, qs, mo, zt, tt):
    lane = lane_of((WIN, 128))

    def plane(n, x, slot):
        zy_plane(lambda c, t: qs[t][c, x + 2], zt.at[n], tt.at[n], slot, lane, tiles=1, base=4, blocks=2)

    for n, first in enumerate(firsts):
        plane(n, first, 0)

    def step(i, acc):
        s0, s1, s2, s3 = acc
        new, old = (i + 1) & 1, i & 1
        for n, first in enumerate(firsts):
            x = first + i
            plane(n, x + 1, new)
            for b in range(2):
                rows = slice(4 + 8 * b, 12 + 8 * b)
                for c in range(3):
                    r, q = rs[0][c, x + 3, rows], qs[0][c, x + 2, rows]
                    s0, s1, s2 = s0 + r * r, s1 + r * q, s2 + q * q
                m = modal_of(read_t(tt.at[n], old, 0, b), read_t(tt.at[n], new, 0, b))
                s3 = s3 + energy_of(m) * mo[x + 3, 0, rows]
        return s0, s1, s2, s3

    return lax.fori_loop(0, count, step, acc)


def inner_kernel(
    rx, rxt, dx, qk, fl, cl, mo, gf, gft, dens_ref, qx, qxt, acc_ref, av, zt, tt, gp, yp, yg, *, sizes
):
    nx = sizes[0]

    def density_step(i, _):
        for n in range(2):
            e = 5 + i + 6 * n
            density_plane(e, e - 3, nx, dx, qk, fl, av.at[n], mo, (gf, gft), dens_ref)
        return 0

    lax.fori_loop(0, 6, density_step, 0)
    operate_planes((5,), 12, nx, (rx, rxt), mo, cl, (qx, qxt), zt, tt, gp, yp, yg)
    zero = jnp.zeros((8, 128), jnp.float32)
    for n, part in enumerate(sum_planes((3, 8), 5, (zero,) * 4, (rx, rxt), (qx, qxt), mo, zt, tt)):
        acc_ref[n] = part


def outer_kernel(
    rx_in, rxt_in, dx_in, mo_in, gf_in, gft_in, dens_in, qx_in, qxt_in, acc_ref, xlo_ref, xhi_ref, qk, fl, cl,
    rx, rxt, dx, mo, gf, gft, dens_ref, qx, qxt, rp, qp, gpk, sum_ref, av, zt, tt, gp, yp, yg, *, sizes
):
    del rx_in, rxt_in, dx_in, mo_in, gf_in, gft_in, dens_in, qx_in, qxt_in
    nx = sizes[0]
    rs, qs, gfs = (rx, rxt), (qx, qxt), (gf, gft)
    x_halos(xlo_ref, xhi_ref, rx, rxt, dx)

    def density_step(i, _):
        density_plane(i, jnp.maximum(i - 3, 0), nx, dx, qk, fl, av.at[0], mo, gfs, dens_ref)
        density_plane(21 - i, jnp.minimum(18 - i, 15), nx, dx, qk, fl, av.at[1], mo, gfs, dens_ref)
        return 0

    lax.fori_loop(0, 5, density_step, 0)
    operate_planes((0, 16), 6, nx, rs, mo, cl, qs, zt, tt, gp, yp, yg)
    acc = tuple(acc_ref[n] for n in range(4))
    acc = sum_planes((0, 13), 3, acc, rs, qs, mo, zt, tt)
    line = jnp.zeros((8, 128), jnp.float32)
    lane = lane_of((8, 128))
    for n, part in enumerate(acc):
        total = jnp.sum(jnp.sum(part, axis=0, keepdims=True), axis=1, keepdims=True)
        line = jnp.where(lane == n, total, line)
    for n in range(sum_ref.shape[0] // 8):
        sum_ref[8 * n : 8 * n + 8] = line

    def pack_step(j, _):
        for c in range(3):
            rp[c, j] = pack_chunks([(rx[c, 4 * k + j + 1], rxt[c, 4 * k + j + 1]) for k in range(4)])
            qp[c, j] = pack_chunks([(qx[c, 4 * k + j], qxt[c, 4 * k + j]) for k in range(4)])
        return 0

    lax.fori_loop(0, 9, pack_step, 0, unroll=3)

    def pack_weights(j, _):
        gpk[j] = pack_chunks([(gf[4 * k + j + 1], gft[4 * k + j + 1]) for k in range(4)])
        return 0

    lax.fori_loop(0, 8, pack_weights, 0)


def pack_chunks(tiles):
    lane = lane_of((WIN, 128))
    out = None
    for k, (main, side) in enumerate(tiles):
        high = roll(side, 32 * k)
        low = roll(jnp.where(lane >= 64, side, main), 32 * k + 28)
        out = high if out is None else jnp.where(lane >= 32 * k, high, out)
        out = jnp.where(lane >= 32 * k + 16, low, out)
    return out


def cross_energy(m, o):
    total = None
    for first, second, pick in (
        (K["a"] - K["b"], K["b"], lambda c: mode(c)),
        (K["p"] - K["r"], K["r"], lambda c: mode(*{0, 1, 2} - {c})),
    ):
        vm, vo = [m[c, pick(c)] for c in range(3)], [o[c, pick(c)] for c in range(3)]
        sm, so = vm[0] + vm[1] + vm[2], vo[0] + vo[1] + vo[2]
        part = (vm[0] * vo[0] + vm[1] * vo[1] + vm[2] * vo[2]) * f32(first) + sm * so * f32(second)
        total = part if total is None else total + part
    shear = None
    for c, e2 in ((0, 1), (0, 2), (1, 2)):
        v = (m[c, mode(e2)] + m[e2, mode(c)]) * (o[c, mode(e2)] + o[e2, mode(c)])
        shear = v if shear is None else shear + v
    triple = None
    for c in range(3):
        v = m[c, (1, 1, 1)] * o[c, (1, 1, 1)]
        triple = v if triple is None else triple + v
    same = cross = None
    for e2 in range(3):
        c, d = [i for i in range(3) if i != e2]
        m1, m2 = m[c, mode(c, e2)], m[d, mode(d, e2)]
        o1, o2 = o[c, mode(c, e2)], o[d, mode(d, e2)]
        sq, cr = m1 * o1 + m2 * o2, m1 * o2 + m2 * o1
        same = sq if same is None else same + sq
        cross = cr if cross is None else cross + cr
    total = total + shear * f32(K["g"]) + triple * f32(K["h"])
    return total + same * f32(K["c"]) + cross * f32(K["d"])


def tail_kernel(rx, qx, gf, rp, qp, gpk, dens_in, out_ref, dens_ref, px, pp, zt, tr, tq, av, ap, bp):
    dens_ref[...] = dens_in[...]
    lane = lane_of((WIN, 128))
    edge = lane == 127

    def half_plane(at, after, t_ref, slot):
        for c in range(3):
            a = at(c)
            n = after(c, a)
            zt[2 * c, 0, 0:24] = a + n
            zt[2 * c + 1, 0, 0:24] = n - a
        for f in range(6):
            for b in range(3):
                lo, hi = zt[f, 0, 8 * b : 8 * b + 8], zt[f, 0, 8 * b + 1 : 8 * b + 9]
                t_ref[slot, 2 * f, 0, 8 * b : 8 * b + 8] = lo + hi
                t_ref[slot, 2 * f + 1, 0, 8 * b : 8 * b + 8] = hi - lo

    def main_plane(i, slot):
        chunk = jnp.minimum(i >> 2, 3)
        j, shift = i - 4 * chunk, 127 - 32 * chunk

        def after(src):
            return lambda c, a: jnp.where(edge, pltpu.roll(src[c, j], shift, 1), roll(a, -1))

        half_plane(lambda c: rx[c, i + 1], after(rp), tr, slot)
        half_plane(lambda c: qx[c, i], after(qp), tq, slot)

    def end_plane(j, slot):
        half_plane(lambda c: rp[c, j], lambda c, a: roll(a, -1), tr, slot)
        half_plane(lambda c: qp[c, j], lambda c, a: roll(a, -1), tq, slot)

    def energies(i, g_ref, out):
        new, old = (i + 1) & 1, i & 1
        for b in range(3):
            rows = slice(8 * b, 8 * b + 8)
            m = modal_of(read_t(tr, old, 0, b), read_t(tr, new, 0, b))
            o = modal_of(read_t(tq, old, 0, b), read_t(tq, new, 0, b))
            g = g_ref[rows]
            out[0, i, rows] = energy_of(m) * g
            out[1, i, rows] = cross_energy(m, o) * (2.0 * g)
            out[2, i, rows] = energy_of(o) * g

    def main_step(i, _):
        main_plane(i + 1, (i + 1) & 1)
        energies(i, gf.at[i + 1], px)
        return 0

    def end_step(j, _):
        end_plane(j + 1, (j + 1) & 1)
        energies(j, gpk.at[j], pp)
        return 0

    main_plane(jnp.int32(0), 0)
    lax.fori_loop(0, 20, main_step, 0, unroll=2)
    end_plane(0, 0)
    lax.fori_loop(0, 8, end_step, 0, unroll=2)

    def parts_of(src, k, x, dst):
        f0 = src[k, x + 2]
        f1 = src[k, x + 1] + src[k, x + 3]
        f2 = src[k, x] + src[k, x + 4]
        for n, part in enumerate(x_parts(f0, f1, f2).values()):
            dst[k, n, 0, 0:24] = part

    def end_cone(j, _):
        for k in range(3):
            parts_of(pp, k, j, ap)
            b = cone_yz(ap.at[k], 0, (4, 20))
            bp[k, j, 0] = b[1]
            bp[k, j, 1] = b[2]
        return 0

    lax.fori_loop(0, 4, end_cone, 0, unroll=2)
    lane16 = lane_of((NYL, 128))
    for chunk in range(4):

        def cone_step(j, _):
            x = 4 * chunk + j
            for k in range(3):
                parts_of(px, k, x, av)
                b0, b1, b2 = cone_yz(av.at[k], 0, (4, 20))
                e1, e2 = bp[k, j, 0], bp[k, j, 1]
                n1 = jnp.where(lane16 == 127, roll(e1, 127 - 32 * chunk), roll(b1, -1))
                p1 = jnp.where(lane16 == 0, roll(e1, -(32 * chunk + 27)), roll(b1, 1))
                n2 = jnp.where(lane16 >= 126, roll(e2, 126 - 32 * chunk), roll(b2, -2))
                p2 = jnp.where(lane16 < 2, roll(e2, -(32 * chunk + 26)), roll(b2, 2))
                out_ref[k, x] = b0 + (n1 + p1) + (n2 + p2)
            return 0

        lax.fori_loop(0, 4, cone_step, 0, unroll=2)


def final_kernel(sum_ref, rx, qx, cones, disp_ref, sens_ref):
    line = jnp.sum(sum_ref[...], axis=0, keepdims=True)
    lane1 = lane_of((1, 128))
    m0, m1, m2, m3 = [jnp.sum(jnp.where(lane1 == n, line, 0.0), axis=1, keepdims=True) for n in range(4)]
    m3 = m3 + spring_rate * m2
    first = m0 / m1
    norm = m0 - 2.0 * first * m1 + first * first * m2
    grown = 1.0 + norm / m0
    second = norm / (grown * grown * m1 - 2.0 * first * grown * m2 + first * first * m3)
    c0 = jnp.broadcast_to(first + second * grown, (NYL, 128))
    c1 = jnp.broadcast_to(-second * first, (NYL, 128))

    def step(x, _):
        for c in range(3):
            disp_ref[c, x] = c0 * rx[c, x + 3, 4:20] + c1 * qx[c, x + 2, 4:20]
        sens_ref[x] = c0 * (c0 * cones[0, x] + c1 * cones[1, x]) + c1 * c1 * cones[2, x]
        return 0

    lax.fori_loop(0, 16, step, 0)


def s(*shape):
    return jax.ShapeDtypeStruct(shape, jnp.float32)


def v(*shape):
    return pltpu.VMEM(shape, jnp.float32)


def call(kernel, outs, scratch, *args, smem=0, hbm=0, flush=(), **kw):
    spec_s, spec_v = pl.BlockSpec(memory_space=pltpu.SMEM), pl.BlockSpec(memory_space=pltpu.VMEM)
    single = not isinstance(outs, (tuple, list))
    outs = [outs] if single else list(outs)
    if not INTERPRET:
        outs = [o if i in flush else pltpu.VMEM(o.shape, o.dtype) for i, o in enumerate(outs)]
        args = [
            a if i < smem else pltpu.with_memory_space_constraint(a, pltpu.HBM if i < smem + hbm else pltpu.VMEM)
            for i, a in enumerate(args)
        ]
    return pl.pallas_call(
        kernel,
        out_shape=outs[0] if single else outs,
        in_specs=[spec_s] * smem
        + [pl.BlockSpec(memory_space=pltpu.HBM)] * hbm
        + [spec_v] * (len(args) - smem - hbm),
        out_specs=spec_v if single else [spec_v] * len(outs),
        scratch_shapes=scratch,
        interpret=INTERPRET,
        compiler_params=pltpu.CompilerParams(vmem_limit_bytes=24 << 20),
        **kw,
    )(*args)


def moved(block, axis, step):
    count = lax.axis_size(axis)
    return lax.ppermute(block, axis, [(i, i - step) for i in range(count) if 0 <= i - step < count])


def body(load, design, solid_map):
    sizes = tuple(lax.axis_size(a) * n for a, n in zip(ALL, (NXL, NYL, NZL)))
    count = lax.axis_size("gx") * lax.axis_size("gy") * lax.axis_size("gz")

    def sized(kernel):
        return lambda *refs: kernel(*refs, sizes=sizes)

    load, design, zc = call(
        pack_z_kernel, (s(3, 16, 16, 128), s(16, 16, 128), s(8, 16, 128)), [pltpu.SemaphoreType.DMA((4,))],
        load, design, hbm=2,
    )
    zhi, zlo = moved(zc, "gz", 1), moved(zc, "gz", -1)
    qk, fl, cl = call(
        sized(place_kernel), (s(6, 2, 24, 128), s(3, 2, 24, 128), s(2, 24, 128)), [], solid_map, zc, smem=1
    )
    ylo_s, yhi_s = call(pack_y_kernel, (s(39, 8, 128), s(39, 8, 128)), [], load, design, zhi, zlo, cl)
    yhi, ylo = moved(ylo_s, "gy", 1), moved(yhi_s, "gy", -1)
    rx_t, dx_t, mo_t, gf_t = s(3, 23, 24, 128), s(26, 2, 32, 128), s(22, 2, 24, 128), s(22, 24, 128)
    dens_t, qx_t = s(16, 16, 128), s(3, 21, 24, 128)
    rx, rxt, dx, xlo_s, xhi_s = call(
        pack_x_kernel, (rx_t, rx_t, dx_t, s(544, 128), s(472, 128)), [v(8, 32, 128)],
        load, design, zhi, zlo, ylo, yhi,
    )
    xhi, xlo = moved(xlo_s, "gx", 1), moved(xhi_s, "gx", -1)
    scratch = [
        v(2, 7, 2, 32, 128), v(2, 6, 2, 32, 128), v(2, 2, 12, 2, 24, 128), v(2, 12, 2, 24, 128),
        v(2, 2, 6, 2, 24, 128), v(2, 2, 6, 2, 32, 128),
    ]
    mo, gf, gft, dens, qx, qxt, acc = call(
        sized(inner_kernel), (mo_t, gf_t, gf_t, dens_t, qx_t, qx_t, s(4, 8, 128)), scratch, rx, rxt, dx, qk, fl, cl
    )
    held = rx_t, rx_t, dx_t, mo_t, gf_t, gf_t, dens_t, qx_t, qx_t
    rx, _, _, _, gf, _, dens, qx, _, rp, qp, gpk, part = call(
        sized(outer_kernel),
        (*held, s(3, 9, 24, 128), s(3, 9, 24, 128), s(8, 24, 128), s(count, 128)), scratch,
        rx, rxt, dx, mo, gf, gft, dens, qx, qxt, acc, xlo, xhi, qk, fl, cl,
        flush=(12,), input_output_aliases={n: n for n in range(len(held))},
    )
    sums = lax.all_to_all(part, ALL, 0, 0, tiled=True)
    cones, dens = call(
        tail_kernel, (s(3, 16, 16, 128), dens_t),
        [
            v(3, 20, 24, 128), v(3, 8, 24, 128), v(6, 2, 32, 128), v(2, 12, 1, 24, 128), v(2, 12, 1, 24, 128),
            v(3, 6, 1, 32, 128), v(3, 6, 1, 32, 128), v(3, 4, 2, 16, 128),
        ],
        rx, qx, gf, rp, qp, gpk, dens, flush=(1,),
    )
    disp, sens = call(
        final_kernel, (s(3, 16, 16, 128), s(16, 16, 128)), [], sums, rx, qx, cones, flush=(0, 1)
    )
    return disp, sens, dens


def solution(mesh):
    nodal, cell = P(None, "gx", "gy", "gz"), P("gx", "gy", "gz")
    return jax.shard_map(
        body, mesh=mesh, in_specs=(nodal, cell, P()), out_specs=(nodal, cell, cell), check_vma=False
    )
```
